32 devices in a mesh: batch: 16 (over z, x, core), branch: 2 (over y).
Axes of the slice: x: 2, y: 2, z: 4, core: 2. Of those that a mesh axis runs over, the one named last changes fastest.
Arguments:
- tokens: bfloat16 [25088, 768], P(('batch', 'branch')), may hold values from -6 to 6
- cotangent: bfloat16 [25088, 768], P(('batch', 'branch')), may hold values from -6 to 6
- image_tokens: int32 [16, 8], P('batch'), may hold values from 0 to 784, as said below
- w_qkv: float32 [3, 768, 768], P(None, ('batch', 'branch')), may hold values from -0.21875 to 0.21875
- w_out: float32 [768, 768], P(None, ('batch', 'branch')), may hold values from -0.875 to 0.875
- w_up: float32 [768, 3072], P(('batch', 'branch')), may hold values from -0.21875 to 0.21875
- bias_up: float32 [3072], P(('batch', 'branch')), may hold values from -3 to 3
- w_down: float32 [3072, 768], P(None, ('batch', 'branch')), may hold values from -0.109375 to 0.109375
- bias_down: float32 [768], P(('batch', 'branch')), may hold values from -3 to 3
- norm_gain: float32 [768], P(('batch', 'branch')), may hold values from 0.25 to 1.75
- query_gain: float32 [64], replicated, may hold values from 0.25 to 1.75
- key_gain: float32 [64], replicated, may hold values from 0.25 to 1.75
Outputs:
- block_out: bfloat16 [25088, 768], P(('batch', 'branch'))
- grad_tokens: bfloat16 [25088, 768], P(('batch', 'branch'))
- grad_w_qkv: float32 [3, 768, 768], P(None, ('batch', 'branch'))
- grad_w_out: float32 [768, 768], P(None, ('batch', 'branch'))
- grad_w_up: float32 [768, 3072], P(('batch', 'branch'))
- grad_bias_up: float32 [3072], P(('batch', 'branch'))
- grad_w_down: float32 [3072, 768], P(None, ('batch', 'branch'))
- grad_bias_down: float32 [768], P(('batch', 'branch'))
- grad_norm_gain: float32 [768], P(('batch', 'branch'))
- grad_query_gain: float32 [64], replicated
- grad_key_gain: float32 [64], replicated
The draws below stay inside these ranges and needn't reach their ends.
Inputs may be any that keep to these rules, and one draw needn't show every extreme that they name: `image_tokens`: row j lists, in order, the token counts of the 8 image slots laid end to end in rows j * 1568 to (j + 1) * 1568 - 1 of tokens; each count is 0, 196 or 784, a row holds at most one count of 784, and each row sums to 1568.
All inputs are finite; a program needn't handle non-finite values.
Results may differ from the reference program's by a relative error of at most 0.02.
Values may be sent and summed in bfloat16 or wider, within the bound.
A program may use at most 320 MiB of HBM per device.

```python
import jax
import jax.numpy as jnp
from jax import lax

D = 768
H = 12
HD = 64
FF = 3072
PATCHES = 196
IMG_DEV = 4
GROUP = 1568
LONGEST = 784
PAIRS = 16
TOKENS = 25088


def draw_image_tokens(key, part):
    slots = 2 * IMG_DEV
    drawn = jnp.full((slots,), PATCHES, jnp.int32)
    mixed = jnp.concatenate([jnp.full((1,), LONGEST, jnp.int32), jnp.full((slots - 4,), PATCHES, jnp.int32), jnp.zeros((3,), jnp.int32)])
    picked = jax.random.randint(jax.random.fold_in(key, 11), (PAIRS,), 0, 2)
    picked = picked.at[0].set(1)
    layout = jnp.where(picked[:, None] == 1, mixed[None, :], drawn[None, :])
    order_keys = jax.random.split(jax.random.fold_in(key, 23), PAIRS)
    orders = jax.vmap(lambda okey: jax.random.permutation(okey, slots))(order_keys)
    return jnp.take_along_axis(layout, orders.astype(jnp.int32), axis=1)


def strengthened(result, key, source, target, parts, factor):
    def block_of(dim):
        return (jnp.arange(result.shape[dim]) // (result.shape[dim] // parts)).reshape((-1,) + (1,) * (result.ndim - 1 - dim))

    first = jax.random.permutation(key, parts)[block_of(target)]
    other_side = (block_of(target) + parts // 2) % parts
    return jnp.where((block_of(source) == first) | (block_of(source) == other_side), factor * result, result)


def steps_of(stream_key, extent, cuts, smallest, top_value):
    factor_of = 1.0
    for axis_at, blocks in cuts:
        heights = jax.random.uniform(jax.random.fold_in(jax.random.fold_in(stream_key, 6), axis_at), (blocks,), jnp.float32, smallest / len(cuts), top_value / len(cuts))
        factor_of = factor_of * jnp.repeat(jnp.exp(heights), extent[axis_at] // blocks).reshape((-1,) + (1,) * (len(extent) - 1 - axis_at))
    return factor_of


def noise(key, dims, deviation, reach, cuts=(), kind=jnp.bfloat16):
    loudness = steps_of(key, dims, cuts, -0.22, 0.18) if cuts else 1.0
    values = jax.random.normal(key, dims, jnp.float32) * deviation * loudness
    return jnp.minimum(jnp.maximum(values, -reach), reach).astype(kind)


def gaussian_with(key, dims, deviation, most, shards, heavy, kind=jnp.bfloat16):
    drawn = deviation * jax.random.normal(key, dims, jnp.float32)
    if shards:
        drawn = drawn * steps_of(key, dims, shards, -0.22, 0.18)
    return jnp.clip(strengthened(drawn, jax.random.fold_in(key, 3), *heavy), -most, most).astype(kind)


def setup_inputs(seed: int = 0) -> dict:
    key_of = jax.random.split(jax.random.key(seed), 13)
    return {
        "tokens": noise(key_of[0], (TOKENS, D), 1.0, 6.0, ((0, 32),)),
        "cotangent": gaussian_with(key_of[1], (TOKENS, D), 1.0, 6.0, ((0, 32),), (0, 1, 32, 2.75)),
        "image_tokens": draw_image_tokens(jax.random.fold_in(key_of[12], 71), 0),
        "w_qkv": noise(key_of[3], (3, D, D), D ** -0.5, 0.21875, ((1, 32),), jnp.float32),
        "w_out": noise(key_of[4], (D, D), (D // 16) ** -0.5, 0.875, ((1, 32),), jnp.float32),
        "w_up": noise(key_of[5], (D, FF), D ** -0.5, 0.21875, ((0, 32),), jnp.float32),
        "bias_up": noise(key_of[6], (FF,), 0.5, 3.0, ((0, 32),), jnp.float32),
        "w_down": noise(key_of[7], (FF, D), FF ** -0.5, 0.109375, ((1, 32),), jnp.float32),
        "bias_down": noise(key_of[8], (D,), 0.5, 3.0, ((0, 32),), jnp.float32),
        "norm_gain": jnp.clip(1.0 + 0.15 * jax.random.normal(key_of[9], (D,), jnp.float32), 0.25, 1.75),
        "query_gain": jnp.clip(1.0 + 0.15 * jax.random.normal(key_of[10], (HD,), jnp.float32), 0.25, 1.75),
        "key_gain": jnp.clip(1.0 + 0.15 * jax.random.normal(key_of[11], (HD,), jnp.float32), 0.25, 1.75),
    }


NORM_EPS = 1e-06

@jax.custom_vjp
def low(v):
    return lax.optimization_barrier(v.astype(jnp.bfloat16)).astype(jnp.float32)

@jax.custom_vjp
def low_back(v):
    return v

def low_keep(v):
    return (low(v), None)

def low_pass(kept, grad):
    return (grad,)

def back_keep(v):
    return (v, None)

def back_low(kept, grad):
    return (low(grad),)
low.defvjp(low_keep, low_pass)
low_back.defvjp(back_keep, back_low)

def norm_rows(values, gain):
    centred = values - lax.optimization_barrier(jnp.mean(values, axis=-1, keepdims=True))
    spread = lax.optimization_barrier(jnp.mean(centred * centred, axis=-1, keepdims=True))
    return centred * lax.rsqrt(spread + NORM_EPS) * gain

def gelu_tanh(values):
    return jax.nn.gelu(values, approximate=True)

def segment_ids(counts, row_count):
    bounds = jnp.cumsum(counts, dtype=jnp.int32)
    places = lax.broadcasted_iota(jnp.int32, (row_count, counts.shape[0]), 0)
    return lax.optimization_barrier(jnp.sum((places >= bounds[None, :]).astype(jnp.int32), axis=1, dtype=jnp.int32))

def group_forward(params, token_values, segment):
    rounded = [low(master) for master in params]
    w_qkv, w_out, w_up, bias_up, w_down, bias_down, norm_gain, query_gain, key_gain = rounded
    row_count = token_values.shape[0]
    normed = low(norm_rows(token_values, norm_gain))
    projected = jnp.einsum('pd,sde->spe', normed, w_qkv, precision=lax.Precision.HIGHEST)
    query_raw = low_back(projected[0])
    key_raw = low_back(projected[1])
    values = low(low_back(projected[2])).reshape(row_count, H, HD)
    queries = low(norm_rows(query_raw.reshape(row_count, H, HD), query_gain))
    keys_all = low(norm_rows(key_raw.reshape(row_count, H, HD), key_gain))
    block_rows = LONGEST
    block_count = row_count // block_rows

    def one_block(inputs):
        query_b, segment_b = inputs
        scores = low_back(jnp.einsum('qhd,khd->hqk', query_b, keys_all, precision=lax.Precision.HIGHEST) * 0.125)
        scores = jnp.where(segment_b[None, :, None] == segment[None, None, :], scores, -1e+30)
        weights = low(jax.nn.softmax(scores, axis=-1))
        return jnp.einsum('hqk,khd->qhd', weights, values, precision=lax.Precision.HIGHEST)
    mixed = lax.map(jax.checkpoint(one_block), (queries.reshape(block_count, block_rows, H, HD), segment.reshape(block_count, block_rows)))
    heads_out = low(low_back(mixed.reshape(row_count, D)))
    attended = jnp.dot(heads_out, w_out, precision=lax.Precision.HIGHEST)
    hidden = low_back(jnp.dot(normed, w_up, precision=lax.Precision.HIGHEST) + bias_up)
    activated = low(gelu_tanh(hidden))
    return token_values + attended + jnp.dot(activated, w_down, precision=lax.Precision.HIGHEST) + bias_down

def reference(tokens, cotangent, image_tokens, w_qkv, w_out, w_up, bias_up, w_down, bias_down, norm_gain, query_gain, key_gain):
    params = (w_qkv, w_out, w_up, bias_up, w_down, bias_down, norm_gain, query_gain, key_gain)
    token_values = tokens.astype(jnp.float32).reshape(PAIRS, GROUP, D)
    segments = jax.vmap(lambda counts: segment_ids(counts, GROUP))(image_tokens)
    checked = jax.checkpoint(group_forward)

    def forward(params, token_values):
        return lax.map(lambda inputs: checked(params, inputs[0], inputs[1]), (token_values, segments))
    outputs, pullback = jax.vjp(forward, params, token_values)
    grad_params, grad_values = pullback(cotangent.astype(jnp.float32).reshape(PAIRS, GROUP, D))
    return (outputs.reshape(TOKENS, D).astype(jnp.bfloat16), grad_values.reshape(TOKENS, D).astype(jnp.bfloat16), grad_params[0], grad_params[1], grad_params[2], grad_params[3], grad_params[4], grad_params[5], grad_params[6], grad_params[7], grad_params[8])
```

```python
import functools
import jax
import jax.numpy as jnp
from jax import lax
from jax.experimental import pallas as pl
from jax.experimental.pallas import tpu as pltpu
from jax.sharding import PartitionSpec as P

HD = 64
LANES = 128
NORM_EPS = 1e-06
LONGEST = 784
PATCHES = 196
SLOT = 200
VMEM_CAP = 66_000_000
BF = jnp.bfloat16
F32 = jnp.float32


def dot(a, b, dims=((1,), (0,))):
    return lax.dot_general(a, b, (dims, ((), ())), preferred_element_type=F32)


NT = ((1,), (1,))
TN = ((0,), (0,))


def norm_stats(values):
    centred = values - jnp.mean(values, axis=-1, keepdims=True)
    spread = jnp.mean(centred * centred, axis=-1, keepdims=True)
    scale = lax.rsqrt(spread + NORM_EPS)
    return centred * scale, scale


def split_dot(values, ones_low):
    high = values.astype(BF)
    low = (values - high.astype(F32)).astype(BF)
    return dot(high, ones_low) + dot(low, ones_low)


def head_ones(width):
    row = lax.broadcasted_iota(jnp.int32, (width, width), 0) // HD
    col = lax.broadcasted_iota(jnp.int32, (width, width), 1) // HD
    return jnp.where(row == col, 1.0 / HD, 0.0).astype(BF)


def head_stats(raw, ones_low):
    centred = raw - split_dot(raw, ones_low)
    scale = lax.rsqrt(split_dot(centred * centred, ones_low) + NORM_EPS)
    return centred * scale, scale


def ffn_kernel(x_ref, dy_ref, g_ref, b1_ref, w1_ref, w2_ref, dw1_ref, dw2_ref, gb1_ref, out_ref, dn_ref, normed_ref, nt_ref, dyt_ref, act_ref, dh_ref, *, chunk):
    step = pl.program_id(0)
    rows = x_ref.shape[0]

    @pl.when(step == 0)
    def _():
        for first in range(0, rows, chunk):
            part = slice(first, first + chunk)
            vhat, _ = norm_stats(x_ref[part, :].astype(F32))
            normed_ref[part, :] = (vhat * g_ref[...]).astype(BF)
        nt_ref[...] = normed_ref[...].T
        dyt_ref[...] = dy_ref[...].T

    w1, w2 = w1_ref[...], w2_ref[...]
    total_b = jnp.zeros((1, w1.shape[1]), F32)
    for first in range(0, rows, chunk):
        part = slice(first, first + chunk)
        hidden = dot(normed_ref[part, :], w1) + b1_ref[...]
        d_act = dot(dy_ref[part, :], w2)
        square = hidden * hidden
        inner = 0.7978845608028654 * hidden * (1.0 + 0.044715 * square)
        tanh = jnp.tanh(inner)
        half = 0.5 * (1.0 + tanh)
        act = (hidden * half).astype(BF)
        slope = half + 0.5 * hidden * (1.0 - tanh * tanh) * (0.7978845608028654 * (1.0 + 0.134145 * square))
        d_hid = (slope * d_act).astype(BF)
        act_ref[part, :] = act
        dh_ref[part, :] = d_hid
        total_b += jnp.sum(d_hid.astype(F32), axis=0, keepdims=True)
        out_part = dot(act, w2, NT)
        dn_part = dot(d_hid, w1, NT)

        @pl.when(step == 0)
        def _():
            out_ref[part, :] = out_part
            dn_ref[part, :] = dn_part

        @pl.when(step > 0)
        def _():
            out_ref[part, :] += out_part
            dn_ref[part, :] += dn_part

    gb1_ref[...] = total_b
    dw1_ref[...] = dot(nt_ref[...], dh_ref[...]).astype(BF)
    dw2_ref[...] = dot(dyt_ref[...], act_ref[...]).astype(BF)


def whole(shape):
    return pl.BlockSpec(shape, lambda j: (0,) * len(shape))


def ffn(x, dy, gain, b1, w1, w2t, block=256, chunk=392):
    rows, width = x.shape
    hidden = w1.shape[1]
    steps = hidden // block
    col = pl.BlockSpec((width, block), lambda j: (0, j))
    row1 = pl.BlockSpec((1, block), lambda j: (0, j))
    return pl.pallas_call(
        functools.partial(ffn_kernel, chunk=chunk),
        grid=(steps,),
        in_specs=[whole((rows, width)), whole((rows, width)), whole((1, width)), row1, col, col],
        out_specs=[col, col, row1, whole((rows, width)), whole((rows, width)), whole((rows, width))],
        out_shape=[
            jax.ShapeDtypeStruct((width, hidden), BF),
            jax.ShapeDtypeStruct((width, hidden), BF),
            jax.ShapeDtypeStruct((1, hidden), F32),
            jax.ShapeDtypeStruct((rows, width), F32),
            jax.ShapeDtypeStruct((rows, width), F32),
            jax.ShapeDtypeStruct((rows, width), BF),
        ],
        scratch_shapes=[
            pltpu.VMEM((width, rows), BF),
            pltpu.VMEM((width, rows), BF),
            pltpu.VMEM((rows, block), BF),
            pltpu.VMEM((rows, block), BF),
        ],
        compiler_params=pltpu.CompilerParams(vmem_limit_bytes=VMEM_CAP),
        cost_estimate=pl.CostEstimate(flops=12 * rows * width * hidden, bytes_accessed=30_000_000, transcendentals=rows * hidden),
        name="feed_forward",
    )(x, dy, gain, b1, w1, w2t)


def project_kernel(normed_ref, dy_ref, w_ref, qg_ref, kg_ref, q_ref, k_ref, v_ref, do_ref, qraw_ref, kraw_ref, *, cols):
    ones_low = head_ones(cols)
    normed = normed_ref[...]
    for raw_ref, low_ref, gain_ref, place in ((qraw_ref, q_ref, qg_ref, 0), (kraw_ref, k_ref, kg_ref, 1)):
        raw = dot(normed, w_ref[:, place * cols : (place + 1) * cols])
        raw_ref[...] = raw
        hat, _ = head_stats(raw, ones_low)
        spread(low_ref, (hat * gain_ref[...]).astype(BF).astype(F32))
    spread(v_ref, dot(normed, w_ref[:, 2 * cols : 3 * cols]).astype(BF).astype(F32))
    spread(do_ref, dot(dy_ref[...], w_ref[:, 3 * cols : 4 * cols]).astype(BF).astype(F32))


def project(normed, dy, w, qg, kg, chunk=2 * PATCHES):
    rows, width = normed.shape
    cols = qg.shape[1]
    blk = pl.BlockSpec((chunk, width), lambda j: (j, 0))
    out = pl.BlockSpec((chunk, cols), lambda j: (j, 0))
    return pl.pallas_call(
        functools.partial(project_kernel, cols=cols),
        grid=(rows // chunk,),
        in_specs=[blk, blk, whole(w.shape), whole((1, cols)), whole((1, cols))],
        out_specs=[pl.BlockSpec((2 * SLOT, cols), lambda j: (j, 0))] * 4 + [out] * 2,
        out_shape=[jax.ShapeDtypeStruct((rows // PATCHES * SLOT, cols), F32)] * 4 + [jax.ShapeDtypeStruct((rows, cols), F32)] * 2,
        compiler_params=pltpu.CompilerParams(vmem_limit_bytes=VMEM_CAP),
        cost_estimate=pl.CostEstimate(flops=8 * rows * width * cols, bytes_accessed=20_000_000, transcendentals=0),
        name="head_projections",
    )(normed, dy, w, qg, kg)


def load_image(ref, block, blocks, lanes):
    parts = [ref[pl.ds(pl.multiple_of((block + at) * SLOT, 8), PATCHES), lanes] for at in range(blocks)]
    return (parts[0] if blocks == 1 else jnp.concatenate(parts, axis=0)).astype(BF)


def store_image(ref, block, blocks, lanes, values):
    for at in range(blocks):
        ref[pl.ds(pl.multiple_of((block + at) * SLOT, 8), PATCHES), lanes] = values[at * PATCHES : (at + 1) * PATCHES]


def attend_image(block, blocks, pieces, pair, refs):
    q_ref, k_ref, v_ref, do_ref, o_ref, dq_ref, dk_ref, dv_ref = refs
    lanes = pl.ds(pl.multiple_of(pair * 2 * HD, 2 * HD), 2 * HD)
    pair_q, pair_k, pair_v, pair_do = (load_image(ref, block, blocks, lanes) for ref in (q_ref, k_ref, v_ref, do_ref))
    results = [[], [], [], []]
    for head in range(2):
        part = slice(head * HD, (head + 1) * HD)
        k, v = pair_k[:, part], pair_v[:, part]
        mixed, grads_q, grad_k, grad_v = [], [], None, None
        for first, size in pieces:
            q, d_o = pair_q[first : first + size, part], pair_do[first : first + size, part]
            scores = dot(k, q, NT) * 0.125
            top = jnp.max(scores, axis=0, keepdims=True)
            shifted = jnp.exp(scores - top)
            total = jnp.sum(shifted, axis=0, keepdims=True)
            weights = shifted * (1.0 / total)
            low = weights.astype(BF)
            d_weights = dot(v, d_o, NT)
            inner = jnp.sum(weights * d_weights, axis=0, keepdims=True)
            d_scores = (weights * (d_weights - inner)).astype(BF)
            mixed.append(dot(low, v, TN))
            grads_q.append(dot(d_scores, k, TN) * 0.125)
            gv, gk = dot(low, d_o), dot(d_scores, q)
            grad_v = gv if grad_v is None else grad_v + gv
            grad_k = gk if grad_k is None else grad_k + gk
        join = lambda parts: parts[0] if len(parts) == 1 else jnp.concatenate(parts, axis=0)
        for kept, value in zip(results, (join(mixed), join(grads_q), grad_k * 0.125, grad_v)):
            kept.append(value)
    for ref, kept in zip((o_ref, dq_ref, dk_ref, dv_ref), results):
        store_image(ref, block, blocks, lanes, jnp.concatenate(kept, axis=1))


def attention_kernel(start_ref, count_ref, *refs, pairs, pieces):
    slots = start_ref.shape[0]

    @pl.loop(0, slots)
    def _(slot):
        block, count = start_ref[slot] // PATCHES, count_ref[slot]

        @pl.when(count == LONGEST)
        def _():
            @pl.loop(0, pairs)
            def _(pair):
                attend_image(block, LONGEST // PATCHES, pieces, pair, refs)

        @pl.when(count == PATCHES)
        def _():
            for pair in range(pairs):
                attend_image(block, 1, ((0, PATCHES),), pair, refs)


def attention(counts, q, k, v, d_o, pieces=((0, 256), (256, 256), (512, 272))):
    rows, cols = q.shape
    starts = jnp.cumsum(counts) - counts
    vm = pl.BlockSpec(memory_space=pltpu.VMEM)
    sm = pl.BlockSpec(memory_space=pltpu.SMEM)
    return pl.pallas_call(
        functools.partial(attention_kernel, pairs=cols // (2 * HD), pieces=pieces),
        in_specs=[sm, sm] + [vm] * 4,
        out_specs=[vm] * 4,
        out_shape=[jax.ShapeDtypeStruct((rows, cols), F32)] * 4,
        compiler_params=pltpu.CompilerParams(vmem_limit_bytes=VMEM_CAP),
        cost_estimate=pl.CostEstimate(flops=20_000_000_000, bytes_accessed=20_000_000, transcendentals=rows * 784 * 6),
        name="attention",
    )(starts, counts, q, k, v, d_o)


def spread(ref, values):
    ref[:PATCHES, :] = values[:PATCHES]
    ref[SLOT : SLOT + PATCHES, :] = values[PATCHES:]


def compact(ref):
    return jnp.concatenate([ref[:PATCHES, :], ref[SLOT : SLOT + PATCHES, :]], axis=0)


def finish_kernel(x_ref, normed_ref, dy_ref, w_ref, g_ref, qg_ref, kg_ref, o_ref, dq_ref, dk_ref, dv_ref, qraw_ref, kraw_ref, out_in_ref, dn_in_ref,
                  out_ref, dn_ref, dw_ref, gq_ref, gk_ref, gg_ref, acc_ref, *, cols):
    step = pl.program_id(0)
    ones_low = head_ones(cols)
    grads = []
    sums = []
    for raw_ref, grad_ref, gain_ref in ((qraw_ref, dq_ref, qg_ref), (kraw_ref, dk_ref, kg_ref)):
        hat, scale = head_stats(raw_ref[...], ones_low)
        grad = compact(grad_ref)
        sums.append(jnp.sum(grad * hat, axis=0, keepdims=True))
        scaled = grad * gain_ref[...]
        d_raw = (scaled - split_dot(scaled, ones_low) - hat * split_dot(scaled * hat, ones_low)) * scale
        grads.append(d_raw.astype(BF))
    grads.append(compact(dv_ref).astype(BF))
    d_proj = jnp.concatenate(grads, axis=1)
    mixed = compact(o_ref).astype(BF)
    d_normed = dn_in_ref[...] + dot(d_proj, w_ref[:, : 3 * cols], NT)
    dn_ref[...] = d_normed.astype(dn_ref.dtype)
    out_ref[...] = (out_in_ref[...] + dot(mixed, w_ref[:, 3 * cols : 4 * cols], NT)).astype(out_ref.dtype)
    vhat, _ = norm_stats(x_ref[...].astype(F32))
    sums.append(jnp.sum(d_normed * vhat, axis=0, keepdims=True))
    dw = (dot(normed_ref[...], d_proj, TN), dot(dy_ref[...], mixed, TN))

    @pl.when(step == 0)
    def _():
        acc_ref[:, : 3 * cols] = dw[0]
        acc_ref[:, 3 * cols :] = dw[1]
        for ref, value in zip((gq_ref, gk_ref, gg_ref), sums):
            ref[...] = value

    @pl.when(step > 0)
    def _():
        acc_ref[:, : 3 * cols] += dw[0]
        acc_ref[:, 3 * cols :] += dw[1]
        for ref, value in zip((gq_ref, gk_ref, gg_ref), sums):
            ref[...] += value

    @pl.when(step == pl.num_programs(0) - 1)
    def _():
        dw_ref[...] = acc_ref[...].astype(BF)


def finish(x, normed, dy, w, gain, qg, kg, o, dq, dk, dv, qraw, kraw, out_in, dn_in, chunk=2 * PATCHES):
    rows, width = normed.shape
    cols = qg.shape[1]
    blk = pl.BlockSpec((chunk, width), lambda j: (j, 0))
    small = pl.BlockSpec((chunk, cols), lambda j: (j, 0))
    return pl.pallas_call(
        functools.partial(finish_kernel, cols=cols),
        grid=(rows // chunk,),
        in_specs=[blk, blk, blk, whole(w.shape), whole((1, width)), whole((1, cols)), whole((1, cols))] + [pl.BlockSpec((2 * SLOT, cols), lambda j: (j, 0))] * 4 + [small] * 2 + [blk, blk],
        out_specs=[blk, blk, whole((width, 4 * cols)), whole((1, cols)), whole((1, cols)), whole((1, width))],
        out_shape=[
            jax.ShapeDtypeStruct((rows, width), BF),
            jax.ShapeDtypeStruct((rows, width), BF),
            jax.ShapeDtypeStruct((width, 4 * cols), BF),
            jax.ShapeDtypeStruct((1, cols), F32),
            jax.ShapeDtypeStruct((1, cols), F32),
            jax.ShapeDtypeStruct((1, width), F32),
        ],
        scratch_shapes=[pltpu.VMEM((width, 4 * cols), F32)],
        compiler_params=pltpu.CompilerParams(vmem_limit_bytes=VMEM_CAP),
        cost_estimate=pl.CostEstimate(flops=16 * rows * width * cols, bytes_accessed=40_000_000, transcendentals=0),
        name="head_gradients",
    )(x, normed, dy, w, gain, qg, kg, o, dq, dk, dv, qraw, kraw, out_in, dn_in)
MESH = pl.DeviceIdType.MESH


def place():
    return lax.axis_index("batch"), lax.axis_index("branch")


def grid_of(batch):
    chips = batch // 2
    across = 1
    while across * across * 4 <= chips:
        across *= 2
    return chips // across, across


def greet(peers):
    barrier = pltpu.get_barrier_semaphore()
    for peer in peers:
        pl.semaphore_signal(barrier, inc=1, device_id=peer, device_id_type=MESH)
    pl.semaphore_wait(barrier, len(peers))


def neighbours(deep, wide):
    batch, branch = place()
    core, x, z = batch % 2, (batch // 2) % wide, batch // (2 * wide)
    at = lambda zz, xx, cc: (zz * wide + xx) * 2 + cc
    partner = (batch, 1 - branch)
    along_z = [(at((z + s) % deep, x, core), branch) for s in range(1, deep)]
    along_x = [(at(z, (x + s) % wide, core), branch) for s in range(1, wide)]
    sibling = (at(z, x, 1 - core), branch)
    return (z, x, core, branch), partner, along_z, along_x, sibling


def remote(src, dst, send, recv, peer):
    return pltpu.make_async_remote_copy(src_ref=src, dst_ref=dst, send_sem=send, recv_sem=recv, device_id=peer, device_id_type=MESH)


def gather_kernel(*refs, deep, wide, parts):
    tokens, cotan = refs[:2]
    packs = refs[2 : 2 + parts]
    rows_x, rows_dy = refs[2 + parts : 4 + parts]
    gathered = refs[4 + parts : 4 + 2 * parts]
    send, recv, local = refs[4 + 2 * parts :]
    (z, x, core, y), partner, along_z, along_x, sibling = neighbours(deep, wide)
    greet([partner, sibling] + along_z + along_x)
    own = []
    for at, (src, dst) in enumerate([(packs[i].at[y], gathered[i].at[z, x, core, y]) for i in range(parts)] + [(tokens, rows_x.at[y]), (cotan, rows_dy.at[y])]):
        copy = pltpu.make_async_copy(src, dst, local.at[at])
        copy.start()
        own.append(copy)
    first = []
    for i in range(parts):
        first.append(remote(packs[i].at[1 - y], gathered[i].at[z, x, core, y], send.at[i, 0], recv.at[i, 0], partner))
    first.append(remote(tokens, rows_x.at[y], send.at[parts, 0], recv.at[parts, 0], partner))
    first.append(remote(cotan, rows_dy.at[y], send.at[parts, 1], recv.at[parts, 1], partner))
    for copy in first:
        copy.start()
    second, third, fourth = [], [], []
    for i in range(parts):
        own[i].wait()
        first[i].wait_recv()
        block = gathered[i].at[z, x, core]
        second.append([remote(block, block, send.at[i, 1 + s], recv.at[i, 1 + s], peer) for s, peer in enumerate(along_z)])
        for copy in second[i]:
            copy.start()

    def over_x(i):
        for copy in second[i]:
            copy.wait_recv()
        block = gathered[i].at[:, x, core]
        third.append([remote(block, block, send.at[i, deep + s], recv.at[i, deep + s], peer) for s, peer in enumerate(along_x)])
        for copy in third[i]:
            copy.start()

    def over_core(i):
        for copy in third[i]:
            copy.wait_recv()
        block = gathered[i].at[:, :, core]
        fourth.append(remote(block, block, send.at[i, deep + wide - 1], recv.at[i, deep + wide - 1], sibling))
        fourth[i].start()

    for i in range(parts):
        over_x(i)
        if i:
            over_core(i - 1)
    over_core(parts - 1)
    for copy in first[parts:]:
        copy.wait_recv()
    for copy in fourth:
        copy.wait_recv()
    for copy in own[parts:]:
        copy.wait()
    for copy in first + [c for group in second + third for c in group] + fourth:
        copy.wait_send()


def gather_all(tokens, cotan, packs, batch):
    deep, wide = grid_of(batch)
    parts = len(packs)
    vm = pl.BlockSpec(memory_space=pltpu.VMEM)
    hbm = pl.BlockSpec(memory_space=pl.ANY)
    rows, width = tokens.shape
    results = pl.pallas_call(
        functools.partial(gather_kernel, deep=deep, wide=wide, parts=parts),
        in_specs=[vm] * (2 + parts),
        out_specs=[hbm] * (2 + parts),
        out_shape=[jax.ShapeDtypeStruct((2, rows, width), BF)] * 2 + [jax.ShapeDtypeStruct((deep, wide, 2) + pack.shape, BF) for pack in packs],
        scratch_shapes=[
            pltpu.SemaphoreType.DMA((parts + 1, deep + wide)),
            pltpu.SemaphoreType.DMA((parts + 1, deep + wide)),
            pltpu.SemaphoreType.DMA((parts + 2,)),
        ],
        compiler_params=pltpu.CompilerParams(collective_id=0, has_side_effects=True, vmem_limit_bytes=VMEM_CAP),
        name="gather",
    )(tokens, cotan, *packs)
    merged = [g.reshape(2 * batch * p.shape[1], p.shape[2]) for g, p in zip(results[2:], packs)]
    return results[0].reshape(2 * rows, width), results[1].reshape(2 * rows, width), merged


def scatter_kernel(*refs, deep, wide, parts, cuts):
    grads = refs[:parts]
    sums = refs[parts : 2 * parts]
    scratch = refs[2 * parts :]
    got_core, to_x, got_x, to_z, got_z, to_y, got_y = (scratch[i * parts : (i + 1) * parts] for i in range(7))
    send, recv = scratch[7 * parts :]
    (z, x, core, y), partner, along_z, along_x, sibling = neighbours(deep, wide)
    greet([partner, sibling] + along_z + along_x)
    first, second, third, fourth = [], [], [], []
    for i, (part, cols) in enumerate(cuts):
        first.append(remote(grads[part].at[:, :, 1 - core, :, :, cols], got_core[part].at[:, :, :, :, cols], send.at[i, 0], recv.at[i, 0], sibling))
        first[i].start()

    def over_x(i):
        part, cols = cuts[i]
        first[i].wait_recv()

        @pl.loop(0, deep)
        def _(zz):
            for xx in range(wide):
                total = grads[part][zz, xx, core, :, :, cols].astype(F32) + got_core[part][zz, xx, :, :, cols].astype(F32)
                to_x[part][xx, zz, :, :, cols] = total.astype(BF)

        group = []
        for s, peer in enumerate(along_x):
            xx = (x + s + 1) % wide
            group.append(remote(to_x[part].at[xx, :, :, :, cols], got_x[part].at[x, :, :, :, cols], send.at[i, 1 + s], recv.at[i, 1 + s], peer))
            group[s].start()
        second.append(group)

    def over_z(i):
        part, cols = cuts[i]
        got_x[part][x, :, :, :, cols] = to_x[part][x, :, :, :, cols]
        for copy in second[i]:
            copy.wait_recv()

        @pl.loop(0, deep)
        def _(zz):
            total = got_x[part][0, zz, :, :, cols].astype(F32)
            for xx in range(1, wide):
                total += got_x[part][xx, zz, :, :, cols].astype(F32)
            to_z[part][zz, :, :, cols] = total.astype(BF)

        group = []
        for s, peer in enumerate(along_z):
            zz = (z + s + 1) % deep
            group.append(remote(to_z[part].at[zz, :, :, cols], got_z[part].at[z, :, :, cols], send.at[i, wide + s], recv.at[i, wide + s], peer))
            group[s].start()
        third.append(group)

    def over_y(i):
        part, cols = cuts[i]
        got_z[part][z, :, :, cols] = to_z[part][z, :, :, cols]
        for copy in third[i]:
            copy.wait_recv()
        total = got_z[part][0, :, :, cols].astype(F32)
        for zz in range(1, deep):
            total += got_z[part][zz, :, :, cols].astype(F32)
        to_y[part][:, :, cols] = total.astype(BF)
        fourth.append(remote(to_y[part].at[1 - y, :, cols], got_y[part].at[:, cols], send.at[i, wide + deep - 1], recv.at[i, wide + deep - 1], partner))
        fourth[i].start()
        sums[part][y, :, cols] = to_y[part][y, :, cols].astype(F32)

    def last(i):
        part, cols = cuts[i]
        fourth[i].wait_recv()
        sums[part][1 - y, :, cols] = got_y[part][:, cols].astype(F32)

    stages = (over_x, over_z, over_y, last)
    for turn in range(len(cuts) + len(stages) - 1):
        for late, stage in enumerate(stages):
            if 0 <= turn - late < len(cuts):
                stage(turn - late)
    for copy in first + [c for group in second + third for c in group] + fourth:
        copy.wait_send()


def scatter_all(grads, batch, piece=768):
    deep, wide = grid_of(batch)
    parts = len(grads)
    rows = grads[0].shape[0] // (2 * batch)
    widths = [g.shape[1] for g in grads]
    cuts = []
    for part, width in enumerate(widths):
        step = min(piece, width)
        cuts += [(part, slice(at, at + step)) for at in range(0, width, step)]
    vm = pl.BlockSpec(memory_space=pltpu.VMEM)
    buf = lambda lead: [pltpu.VMEM(lead + (rows, w), BF) for w in widths]
    shaped = [g.reshape(deep, wide, 2, 2, rows, g.shape[1]) for g in grads]
    return pl.pallas_call(
        functools.partial(scatter_kernel, deep=deep, wide=wide, parts=parts, cuts=cuts),
        in_specs=[vm] * parts,
        out_specs=[vm] * parts,
        out_shape=[jax.ShapeDtypeStruct((2, rows, w), F32) for w in widths],
        scratch_shapes=buf((deep, wide, 2)) + buf((wide, deep, 2)) + buf((wide, deep, 2)) + buf((deep, 2)) + buf((deep, 2)) + buf((2,)) + buf(())
        + [pltpu.SemaphoreType.DMA((len(cuts), deep + wide))] * 2,
        compiler_params=pltpu.CompilerParams(collective_id=1, has_side_effects=True, vmem_limit_bytes=VMEM_CAP),
        name="scatter",
    )(*shaped)


def local(tokens, cotangent, image_tokens, w_qkv, w_out, w_up, bias_up, w_down, bias_down, norm_gain, query_gain, key_gain):
    batch = lax.axis_size("batch")
    own_rows, width = tokens.shape
    shard = w_up.shape[0]
    hidden = w_up.shape[1]
    side = lax.axis_index("branch")
    half_of = lambda m: jnp.stack([m[:, : m.shape[1] // 2], m[:, m.shape[1] // 2 :]])
    low = lambda m: m.astype(BF)
    heads = jnp.concatenate([half_of(low(w_qkv[0])), half_of(low(w_qkv[1])), half_of(low(w_qkv[2])), half_of(low(w_out.T))], axis=2)
    extra = jnp.concatenate([low(norm_gain)[:, None], low(bias_down)[:, None], low(bias_up).reshape(shard, -1)], axis=1)
    extra = jnp.pad(extra, ((0, 0), (0, LANES - extra.shape[1])))
    packs = [jnp.stack([extra, extra]), half_of(low(w_up)), half_of(low(w_down.T)), heads]
    xs, dys, (extras, up_w, down_w, head_w) = gather_all(tokens, cotangent, packs, batch)

    extras = extras.astype(F32)
    gain = extras[:, 0][None, :]
    down_b = extras[:, 1][None, :]
    per = bias_up.shape[0] // shard
    up_b = extras[:, 2 : 2 + per].reshape(1, hidden)
    own_b = lax.dynamic_slice_in_dim(up_b, side * (hidden // 2), hidden // 2, axis=1)
    cols = w_qkv.shape[2] // 2
    query_g = jnp.tile(low(query_gain).astype(F32), cols // HD)[None, :]
    key_g = jnp.tile(low(key_gain).astype(F32), cols // HD)[None, :]

    d_up, d_down, d_up_b, out, d_normed, normed = ffn(xs, dys, gain, own_b, up_w, down_w)
    q, k, v, d_o, q_raw, k_raw = project(normed, dys, head_w, query_g, key_g)
    o, dq, dk, dv = attention(image_tokens[0], q, k, v, d_o)
    out, d_normed, d_heads, grad_qg, grad_kg, grad_g = finish(xs, normed, dys, head_w, gain, query_g, key_g, o, dq, dk, dv, q_raw, k_raw, out, d_normed)

    swap = [(0, 1), (1, 0)]
    halves = lambda m: (lax.dynamic_slice_in_dim(m, side * own_rows, own_rows, axis=0), lax.dynamic_slice_in_dim(m, (1 - side) * own_rows, own_rows, axis=0))
    out_own, out_other = halves(out)
    dn_own, dn_other = halves(d_normed)
    out_got = lax.ppermute(out_other, "branch", swap)
    dn_got = lax.ppermute(dn_other, "branch", swap)

    gains = jnp.concatenate([grad_qg.reshape(-1, HD).sum(0), grad_kg.reshape(-1, HD).sum(0)])
    gain_cols = -(-gains.shape[0] // shard)
    gains = jnp.pad(gains, (0, gain_cols * shard - gains.shape[0])).reshape(1, shard, gain_cols)
    gains = jnp.broadcast_to(gains, (2 * batch, shard, gain_cols)).reshape(width, gain_cols)
    full_b = lax.dynamic_update_slice_in_dim(jnp.zeros((1, hidden), F32), d_up_b, side * (hidden // 2), axis=1).reshape(width, per)
    grad_down_b = jnp.sum(cotangent.astype(F32), axis=0)
    small = jnp.concatenate([grad_g.reshape(width, 1), grad_down_b[:, None], full_b, gains], axis=1)
    small = low(jnp.pad(small, ((0, 0), (0, LANES - small.shape[1]))))
    s_up, s_down, s_heads, s_small = scatter_all([d_up, d_down, d_heads, small], batch)

    block_out = (tokens.astype(F32) + out_own.astype(F32) + out_got.astype(F32) + down_b).astype(BF)
    dn = dn_own.astype(F32) + dn_got.astype(F32)
    vhat, scale = norm_stats(tokens.astype(F32))
    scaled = dn * gain
    d_tokens = (scaled - jnp.mean(scaled, axis=-1, keepdims=True) - vhat * jnp.mean(scaled * vhat, axis=-1, keepdims=True)) * scale
    grad_tokens = (cotangent.astype(F32) + d_tokens).astype(BF)
    joined = lambda m: jnp.concatenate([m[0], m[1]], axis=1)
    small = s_small[0] + s_small[1]
    grad_heads = [joined(s_heads[:, :, i * cols : (i + 1) * cols]) for i in range(4)]
    sum_gains = small[:, 2 + per : 2 + per + gain_cols].reshape(-1)
    return (
        block_out,
        grad_tokens,
        jnp.stack(grad_heads[:3]),
        grad_heads[3].T,
        joined(s_up),
        small[:, 2 : 2 + per].reshape(-1),
        joined(s_down).T,
        small[:, 1],
        small[:, 0],
        sum_gains[:HD],
        sum_gains[HD : 2 * HD],
    )


def solution(mesh):
    both = ("batch", "branch")
    in_specs = (P(both, None), P(both, None), P("batch", None), P(None, both, None), P(None, both), P(both, None), P(both), P(None, both), P(both), P(both), P(), P())
    out_specs = (P(both, None), P(both, None), P(None, both, None), P(None, both), P(both, None), P(both), P(None, both), P(both), P(both), P(), P())
    return jax.shard_map(local, mesh=mesh, in_specs=in_specs, out_specs=out_specs, check_vma=False)
```

```python
import functools
import jax
import jax.numpy as jnp
from jax import lax
from jax.experimental import pallas as pl
from jax.experimental.pallas import tpu as pltpu
from jax.sharding import PartitionSpec as P

HD = 64
LANES = 128
NORM_EPS = 1e-06
LONGEST = 784
PATCHES = 196
SLOT = 208
VMEM_CAP = 66_000_000
BF = jnp.bfloat16
F32 = jnp.float32


def dot(a, b, dims=((1,), (0,))):
    return lax.dot_general(a, b, (dims, ((), ())), preferred_element_type=F32)


NT = ((1,), (1,))
TN = ((0,), (0,))


def norm_stats(values):
    centred = values - jnp.mean(values, axis=-1, keepdims=True)
    spread = jnp.mean(centred * centred, axis=-1, keepdims=True)
    scale = lax.rsqrt(spread + NORM_EPS)
    return centred * scale, scale


def split_dot(values, ones_low):
    high = values.astype(BF)
    low = (values - high.astype(F32)).astype(BF)
    return dot(high, ones_low) + dot(low, ones_low)


def head_ones(width):
    row = lax.broadcasted_iota(jnp.int32, (width, width), 0) // HD
    col = lax.broadcasted_iota(jnp.int32, (width, width), 1) // HD
    return jnp.where(row == col, 1.0 / HD, 0.0).astype(BF)


def head_stats(raw, ones_low):
    centred = raw - split_dot(raw, ones_low)
    scale = lax.rsqrt(split_dot(centred * centred, ones_low) + NORM_EPS)
    return centred * scale, scale


MESH = pl.DeviceIdType.MESH


def place():
    return lax.axis_index("batch"), lax.axis_index("branch")


def grid_of(batch):
    chips = batch // 2
    across = 1
    while across * across * 4 <= chips:
        across *= 2
    return chips // across, across


def greet(peers):
    barrier = pltpu.get_barrier_semaphore()
    for peer in peers:
        pl.semaphore_signal(barrier, inc=1, device_id=peer, device_id_type=MESH)
    pl.semaphore_wait(barrier, len(peers))


def neighbours(deep, wide):
    batch, branch = place()
    core, x, z = batch % 2, (batch // 2) % wide, batch // (2 * wide)
    at = lambda zz, xx, cc: (zz * wide + xx) * 2 + cc
    partner = (batch, 1 - branch)
    along_z = [(at((z + s) % deep, x, core), branch) for s in range(1, deep)]
    along_x = [(at(z, (x + s) % wide, core), branch) for s in range(1, wide)]
    sibling = (at(z, x, 1 - core), branch)
    return (z, x, core, branch), partner, along_z, along_x, sibling


def remote(src, dst, send, recv, peer):
    return pltpu.make_async_remote_copy(src_ref=src, dst_ref=dst, send_sem=send, recv_sem=recv, device_id=peer, device_id_type=MESH)


TINY = (8, LANES)


def lay_out(values):
    rows = [jnp.pad(v.astype(BF).astype(F32), (0, LANES - v.shape[0]))[None, :] for v in values]
    return jnp.concatenate(rows + [jnp.zeros((TINY[0] - len(rows), LANES), F32)], axis=0)


def gelu_parts(hidden, d_act):
    square = hidden * hidden
    tanh = jnp.tanh(hidden * (0.7978845608028654 + 0.035677408136300125 * square))
    half = 0.5 + 0.5 * tanh
    act = hidden * half
    slope = half + (act * (1.0 - tanh)) * (0.7978845608028654 + 0.1070322244089 * square)
    return act.astype(BF), (slope * d_act).astype(BF)


def first_kernel(*refs, deep, wide, cuts, block):
    tokens, cotan, tiny, qg_ref, kg_ref = refs[:5]
    packs = refs[5:8]
    o_x, o_dy, o_normed, o_q, o_k, o_v, o_do, o_qraw, o_kraw, o_heads, o_out, o_dn, o_up, o_down = refs[8:22]
    gb_ref, gain_ref, db_ref = refs[22:25]
    scratch = refs[25:]
    lands, wires = scratch[:3], scratch[3:6]
    tiny_all, x_par, dy_par, normed, act, d_hid, s_q, s_k, s_v, s_do, s_qraw, s_kraw, s_out, s_dn, s_up, s_down = scratch[6:22]
    flats = scratch[22:25]
    send, recv, tsend, trecv, osem = scratch[25:]
    (z, x, core, y), partner, along_z, along_x, sibling = neighbours(deep, wide)
    batch = 2 * deep * wide
    own_rows, width = tokens.shape
    shard = packs[0].shape[1]
    hidden = packs[0].shape[2]
    cols = hidden // 4
    direct = (2 * shard) % 16 == 0

    greet([partner, sibling] + along_z + along_x)
    outs = []

    def put(src, dst):
        copy = pltpu.make_async_copy(src, dst, osem.at[len(outs)])
        copy.start()
        outs.append(copy)

    tiny_all[z, x, core, y] = tiny[...]
    spread_tiny = [remote(tiny, tiny_all.at[z, x, core, y], tsend.at[0], trecv.at[0], partner)]
    spread_tiny[0].start()
    over_y = []
    for i, (part, at) in enumerate(cuts):
        over_y.append(remote(packs[part].at[1 - y, :, at], lands[part].at[:, at], send.at[i, 0], recv.at[i, 0], partner))
        over_y[i].start()
    rows_copy = [remote(tokens, x_par, tsend.at[deep + wide], trecv.at[deep + wide], partner), remote(cotan, dy_par, tsend.at[deep + wide + 1], trecv.at[deep + wide + 1], partner)]
    for copy in rows_copy:
        copy.start()

    def tiny_stage(block, peers, first):
        group = [remote(block, block, tsend.at[first + s], trecv.at[first + s], peer) for s, peer in enumerate(peers)]
        for copy in group:
            copy.start()
        for copy in group:
            copy.wait_recv()
        spread_tiny.extend(group)

    over_z, over_x, over_core = [], [], []

    def start_z(i):
        part, at = cuts[i]
        over_y[i].wait_recv()
        mine, other = packs[part][y, :, at].astype(F32), lands[part][:, at].astype(F32)
        pair = jnp.concatenate([jnp.where(y == 0, mine, other), jnp.where(y == 0, other, mine)], axis=0)
        wires[part][z, x, core, :, at] = pair.astype(BF)
        block = wires[part].at[z, x, core, :, at]
        over_z.append([remote(block, block, send.at[i, 1 + s], recv.at[i, 1 + s], peer) for s, peer in enumerate(along_z)])
        for copy in over_z[i]:
            copy.start()

    def start_x(i):
        part, at = cuts[i]
        for copy in over_z[i]:
            copy.wait_recv()
        block = wires[part].at[:, x, core, :, at]
        over_x.append([remote(block, block, send.at[i, deep + s], recv.at[i, deep + s], peer) for s, peer in enumerate(along_x)])
        for copy in over_x[i]:
            copy.start()

    def start_core(i):
        part, at = cuts[i]
        for copy in over_x[i]:
            copy.wait_recv()
        block = wires[part].at[:, :, core, :, at]
        over_core.append(remote(block, block, send.at[i, deep + wide - 1], recv.at[i, deep + wide - 1], sibling))
        over_core[i].start()

    def arrive(i):
        part, at = cuts[i]
        over_core[i].wait_recv()
        if not direct:
            for b in range(batch):
                flats[part][2 * shard * b : 2 * shard * (b + 1), at] = wires[part][b // (2 * wide), (b // 2) % wide, b % 2, :, at]

    def weight(part, at):
        if direct:
            return wires[part][:, :, :, :, at].reshape(2 * shard * batch, at.stop - at.start if isinstance(at, slice) else at.size)
        return flats[part][:, at]

    for i in range(len(cuts)):
        start_z(i)
        if i == 0:
            spread_tiny[0].wait_recv()
            tiny_stage(tiny_all.at[z, x, core], along_z, 1)
        if i == 1:
            tiny_stage(tiny_all.at[:, x, core], along_x, deep)
        if i == 2:
            tiny_stage(tiny_all.at[:, :, core], [sibling], deep + wide - 1)
    blocks = [tiny_all.at[b // (2 * wide), (b // 2) % wide, b % 2] for b in range(batch)]
    gain_ref[...] = jnp.concatenate([blocks[b][s, 0:1, :shard] for b in range(batch) for s in range(2)], axis=1)
    db_ref[...] = jnp.concatenate([blocks[b][s, 1:2, :shard] for b in range(batch) for s in range(2)], axis=1)
    per = 2 * hidden // (2 * batch)
    low_b = jnp.concatenate([blocks[b][s, 2:3, :per] for b in range(batch // 2) for s in range(2)], axis=1)
    high_b = jnp.concatenate([blocks[b][s, 2:3, :per] for b in range(batch // 2, batch) for s in range(2)], axis=1)
    gb_ref[...] = jnp.where(y == 0, low_b, high_b)
    bias = gb_ref[...]

    sides = ((tokens, cotan, slice(0, own_rows)), (x_par, dy_par, slice(own_rows, 2 * own_rows)))

    def normalise(side):
        vhat, _ = norm_stats(sides[side][0][...].astype(F32))
        normed[sides[side][2], :] = (vhat * gain_ref[...]).astype(BF)

    def expand(side, at):
        rows = sides[side][2]
        up, down = weight(0, at), weight(1, at)
        act[rows, at], d_hid[rows, at] = gelu_parts(dot(normed[rows, :], up) + bias[:, at], dot(sides[side][1][...], down))

    def contract(side):
        rows = sides[side][2]
        for low, kept, part in ((act, s_out, 1), (d_hid, s_dn, 0)):
            kept[rows, :] = dot(low[rows, :], weight(part, slice(0, hidden)), NT).astype(BF)

    def heads(side):
        rows = sides[side][2]
        base = (y if side == 0 else 1 - y) * (own_rows // PATCHES)
        ones_low = head_ones(cols)

        def place_rows(ref, values):
            for at in range(own_rows // PATCHES):
                ref[pl.ds(pl.multiple_of((base + at) * SLOT, 16), PATCHES), :] = values[at * PATCHES : (at + 1) * PATCHES].astype(BF)

        for at, (raw_ref, low_ref, gain) in enumerate(((s_qraw, s_q, qg_ref), (s_kraw, s_k, kg_ref))):
            raw = dot(normed[rows, :], weight(2, slice(at * cols, (at + 1) * cols)))
            raw_ref[rows, :] = raw.astype(BF)
            hat, _ = head_stats(raw, ones_low)
            place_rows(low_ref, hat * gain[...])
        place_rows(s_v, dot(normed[rows, :], weight(2, slice(2 * cols, 3 * cols))))
        place_rows(s_do, dot(sides[side][1][...], weight(2, slice(3 * cols, 4 * cols))))

    half = slice(0, block), slice(block, 2 * block)
    start_x(0)
    normalise(0)
    start_x(1)
    start_core(0)
    start_x(2)
    start_core(1)
    arrive(0)
    arrive(1)
    expand(0, half[0])
    start_x(3)
    start_core(2)
    rows_copy[0].wait_recv()
    normalise(1)
    put(x_par, o_x)
    put(normed, o_normed)
    start_x(4)
    start_core(3)
    arrive(2)
    arrive(3)
    expand(0, half[1])
    start_x(5)
    start_core(4)
    contract(0)
    start_core(5)
    arrive(4)
    arrive(5)
    heads(0)
    rows_copy[1].wait_recv()
    put(dy_par, o_dy)
    heads(1)
    for src, dst in ((s_q, o_q), (s_k, o_k), (s_v, o_v), (s_do, o_do), (s_qraw, o_qraw), (s_kraw, o_kraw)):
        put(src, dst)
    if direct:
        put(wires[2], o_heads)
    else:
        put(flats[2], o_heads)
    for at in half:
        expand(1, at)
    contract(1)
    put(s_out, o_out)
    put(s_dn, o_dn)
    for at in half:
        gb_ref[:, at] = dot(jnp.ones((8, 2 * own_rows), BF), d_hid[:, at])[:1]
        own, other = (side[2] for side in sides)
        s_up[:, at] = dot(normed[...], d_hid[:, at], TN).astype(BF)
        s_down[:, at] = (dot(cotan[...], act[own, at], TN) + dot(dy_par[...], act[other, at], TN)).astype(BF)
    put(s_up, o_up)
    put(s_down, o_down)
    for copy in outs:
        copy.wait()
    for copy in spread_tiny + over_y + rows_copy + [c for group in over_z + over_x for c in group] + over_core:
        copy.wait_send()


def first_half(tokens, cotan, tiny, packs, qg, kg, batch):
    deep, wide = grid_of(batch)
    own_rows, width = tokens.shape
    _, shard, hidden = packs[0].shape
    cols = hidden // 4
    block = hidden // 2
    rows = 2 * own_rows
    spread_rows = rows // PATCHES * SLOT
    cuts = [(0, slice(0, block)), (1, slice(0, block)), (0, slice(block, hidden)), (1, slice(block, hidden)), (2, slice(0, block)), (2, slice(block, hidden))]
    vm = pl.BlockSpec(memory_space=pltpu.VMEM)
    hbm = pl.BlockSpec(memory_space=pl.ANY)
    direct = (2 * shard) % 16 == 0
    full = (width, hidden)
    head_shape = (deep, wide, 2, 2 * shard, hidden) if direct else full
    low = lambda *shape: jax.ShapeDtypeStruct(shape, BF)
    outs = [low(own_rows, width), low(own_rows, width), low(rows, width)] + [low(spread_rows, cols)] * 4 + [low(rows, cols)] * 2 + [low(*head_shape), low(rows, width), low(rows, width), low(*full), low(*full)]
    tiny_outs = [jax.ShapeDtypeStruct((1, hidden), F32), jax.ShapeDtypeStruct((1, width), F32), jax.ShapeDtypeStruct((1, width), F32)]
    buf = lambda *shape: pltpu.VMEM(shape, BF)
    scratch = [buf(shard, hidden)] * 3 + [buf(deep, wide, 2, 2 * shard, hidden)] * 3
    scratch += [pltpu.VMEM((deep, wide, 2, 2) + TINY, F32), buf(own_rows, width), buf(own_rows, width), buf(rows, width), buf(rows, hidden), buf(rows, hidden)]
    scratch += [buf(spread_rows, cols)] * 4 + [buf(rows, cols)] * 2 + [buf(rows, width)] * 2 + [buf(*full)] * 2
    scratch += [buf(16, LANES) if direct else buf(*full)] * 3
    scratch += [pltpu.SemaphoreType.DMA((len(cuts), deep + wide))] * 2 + [pltpu.SemaphoreType.DMA((deep + wide + 2,))] * 2 + [pltpu.SemaphoreType.DMA((len(outs),))]
    return pl.pallas_call(
        functools.partial(first_kernel, deep=deep, wide=wide, cuts=cuts, block=block),
        in_specs=[vm] * 8,
        out_specs=[hbm] * len(outs) + [vm] * 3,
        out_shape=outs + tiny_outs,
        scratch_shapes=scratch,
        compiler_params=pltpu.CompilerParams(collective_id=0, has_side_effects=True, vmem_limit_bytes=VMEM_CAP),
        name="gather_and_feed_forward",
    )(tokens, cotan, tiny, qg, kg, *packs)


def load_rows(ref, block, blocks):
    parts = [ref[pl.ds(pl.multiple_of((block + at) * SLOT, 16), PATCHES), :] for at in range(blocks)]
    return parts[0] if blocks == 1 else jnp.concatenate([p.astype(F32) for p in parts], axis=0).astype(BF)

def attend_pair(pair_q, pair_k, pair_v, pair_do, pieces):
    count = pair_q.shape[0]
    lane = lax.broadcasted_iota(jnp.int32, (count, 2 * HD), 1)
    pair_q = pair_q * jnp.asarray(0.125, BF)
    zero = jnp.zeros_like(pair_q)
    v_t, k_t = pair_v.T, pair_k.T
    mixed, grads_q, grad_k, grad_v = [], [], None, None
    for head in range(2):
        mine = (lane < HD) if head == 0 else (lane >= HD)
        q_m, do_m = jnp.where(mine, pair_q, zero), jnp.where(mine, pair_do, zero)
        part = slice(head * HD, (head + 1) * HD)
        outs, gqs = [], []
        for first, size in pieces:
            q, d_o = q_m[first : first + size], do_m[first : first + size]
            shifted = jnp.exp(dot(pair_k, q, NT))
            total = jnp.sum(shifted, axis=0, keepdims=True)
            weights = shifted * (1.0 / total)
            low = weights.astype(BF)
            d_weights = dot(pair_v, d_o, NT)
            inner = jnp.sum(weights * d_weights, axis=0, keepdims=True)
            d_scores = (weights * (d_weights - inner)).astype(BF)
            outs.append(dot(v_t[part], low))
            gqs.append(dot(k_t[part], d_scores))
            gv, gk = dot(low, d_o), dot(d_scores, q)
            grad_v = gv if grad_v is None else grad_v + gv
            grad_k = gk if grad_k is None else grad_k + gk
        join = lambda parts: parts[0] if len(parts) == 1 else jnp.concatenate(parts, axis=1)
        mixed.append(join(outs))
        grads_q.append(join(gqs))
    turn = lambda parts: jnp.concatenate(parts, axis=0).T
    return turn(mixed), turn(grads_q) * 0.125, grad_k, grad_v

def attention_kernel(count_ref, *refs, pieces, together):
    ins, outs, (small_ref,) = refs[:4], refs[4:8], refs[8:]
    place, smalls, bigs, big_at = 0, 0, 0, 0
    for slot in range(count_ref.shape[0]):
        count = count_ref[slot]
        is_small = (count == PATCHES).astype(jnp.int32)
        is_big = (count == LONGEST).astype(jnp.int32)
        small_ref[smalls] = place
        big_at = jnp.where(is_big == 1, place, big_at)
        smalls, bigs = smalls + is_small, bigs + is_big
        place = place + is_small + (LONGEST // PATCHES) * is_big

    def images(firsts, blocks, pieces):
        loaded = [[load_rows(ref, block, blocks) for ref in ins] for block in firsts]
        results = [attend_pair(*values, pieces) for values in loaded]
        for block, result in zip(firsts, results):
            for ref, values in zip(outs, result):
                for at in range(blocks):
                    ref[pl.ds(pl.multiple_of((block + at) * SLOT, 16), PATCHES), :] = values[at * PATCHES : (at + 1) * PATCHES].astype(ref.dtype)

    @pl.when(bigs > 0)
    def _():
        images([big_at], LONGEST // PATCHES, pieces)

    @pl.loop(0, smalls // together)
    def _(turn):
        images([small_ref[turn * together + at] for at in range(together)], 1, ((0, PATCHES),))

def attention(counts, q, k, v, d_o, pieces=((0, 784),), together=4):
    rows, cols = q.shape
    sm = pl.BlockSpec(memory_space=pltpu.SMEM)
    blk = pl.BlockSpec((rows, 2 * HD), lambda j: (0, j))
    return pl.pallas_call(
        functools.partial(attention_kernel, pieces=pieces, together=together),
        grid=(cols // (2 * HD),),
        in_specs=[sm] + [blk] * 4,
        out_specs=[blk] * 4,
        out_shape=[jax.ShapeDtypeStruct((rows, cols), t) for t in (BF, BF, BF, BF)],
        scratch_shapes=[pltpu.SMEM((counts.shape[0] + 1,), jnp.int32)],
        compiler_params=pltpu.CompilerParams(vmem_limit_bytes=VMEM_CAP),
        cost_estimate=pl.CostEstimate(flops=20_000_000_000, bytes_accessed=20_000_000, transcendentals=rows * LONGEST * cols // HD),
        name="attention",
    )(counts, q, k, v, d_o)


def last_kernel(*refs, deep, wide, cuts):
    tokens, cotan, gain_ref, db_ref, gb_ref, qg_ref, kg_ref = refs[:7]
    i_x, i_dy, i_normed, i_o, i_dq, i_dk, i_dv, i_qraw, i_kraw, i_heads, i_out, i_dn = refs[7:19]
    i_grads = refs[19:21]
    block_ref, grad_ref, qkv_ref, wo_ref, up_ref, down_ref, small_ref = refs[21:28]
    scratch = refs[28:]
    x_par, dy_par, normed, s_o, s_dq, s_dk, s_dv, qraw, kraw, head_w, out, dn = scratch[:12]
    mine = scratch[12:15]
    got_core, got_x, to_z, got_z, to_y, got_y = (scratch[15 + 3 * i : 18 + 3 * i] for i in range(6))
    d_proj, mixed, out_got, dn_got = scratch[33:37]
    t_all, t_core, t_x, t_xgot, t_z, t_zgot, t_y, t_ygot = scratch[37:45]
    send, recv, tsend, trecv, lsem, gsem = scratch[45:]
    (z, x, core, y), partner, along_z, along_x, sibling = neighbours(deep, wide)
    batch = 2 * deep * wide
    own_rows, width = tokens.shape
    rows = 2 * own_rows
    cols = qraw.shape[1]
    shard = to_y[0].shape[1]
    places = [(b // (2 * wide), (b // 2) % wide, b % 2, s) for b in range(batch) for s in range(2)]
    own, other = slice(0, own_rows), slice(own_rows, rows)
    greet([partner, sibling] + along_z + along_x)

    first, second, third, fourth = [], [], [], []

    def over_core(i):
        part, at = cuts[i]
        if part < 2:
            src = i_grads[part].at[:, :, 1 - core, :, :, at]
        else:
            src = mine[part].at[:, :, 1 - core, :, :, at]
        first.append(remote(src, got_core[part].at[:, :, :, :, at], send.at[i, 0], recv.at[i, 0], sibling))
        first[i].start()

    for i in range(4):
        over_core(i)
    held = []
    for i in range(4):
        part, at = cuts[i]
        copy = pltpu.make_async_copy(i_grads[part].at[:, :, core, :, :, at], mine[part].at[:, :, :, :, at], gsem.at[i])
        copy.start()
        held.append(copy)
    loads = {}
    for at, (name, src, dst) in enumerate((("o", i_o, s_o), ("heads", i_heads, head_w), ("out", i_out, out), ("dq", i_dq, s_dq), ("qraw", i_qraw, qraw), ("dk", i_dk, s_dk), ("kraw", i_kraw, kraw), ("dv", i_dv, s_dv), ("dn", i_dn, dn), ("normed", i_normed, normed), ("dy", i_dy, dy_par), ("x", i_x, x_par))):
        loads[name] = pltpu.make_async_copy(src, dst, lsem.at[at])
        loads[name].start()

    def own_term(part, zz, xx, at):
        return mine[part][zz, xx, core, :, :, at] if part == 2 else mine[part][zz, xx, :, :, at]

    def over_x(i):
        part, at = cuts[i]
        first[i].wait_recv()
        if i < 4:
            held[i].wait()

        @pl.loop(0, deep)
        def _(zz):
            for xx in range(wide):
                got_core[part][zz, xx, :, :, at] = (own_term(part, zz, xx, at).astype(F32) + got_core[part][zz, xx, :, :, at].astype(F32)).astype(BF)

        group = []
        for s, peer in enumerate(along_x):
            xx = (x + s + 1) % wide
            group.append(remote(got_core[part].at[:, xx, :, :, at], got_x[part].at[x, :, :, :, at], send.at[i, 1 + s], recv.at[i, 1 + s], peer))
            group[s].start()
        second.append(group)

    def over_z(i):
        part, at = cuts[i]

        @pl.loop(0, deep)
        def _(zz):
            got_x[part][x, zz, :, :, at] = got_core[part][zz, x, :, :, at]

        for copy in second[i]:
            copy.wait_recv()

        @pl.loop(0, deep)
        def _(zz):
            total = got_x[part][0, zz, :, :, at].astype(F32)
            for xx in range(1, wide):
                total += got_x[part][xx, zz, :, :, at].astype(F32)
            to_z[part][zz, :, :, at] = total.astype(BF)

        group = []
        for s, peer in enumerate(along_z):
            zz = (z + s + 1) % deep
            group.append(remote(to_z[part].at[zz, :, :, at], got_z[part].at[z, :, :, at], send.at[i, wide + s], recv.at[i, wide + s], peer))
            group[s].start()
        third.append(group)

    def over_y(i):
        part, at = cuts[i]
        got_z[part][z, :, :, at] = to_z[part][z, :, :, at]
        for copy in third[i]:
            copy.wait_recv()
        total = got_z[part][0, :, :, at].astype(F32)
        for zz in range(1, deep):
            total += got_z[part][zz, :, :, at].astype(F32)
        to_y[part][:, :, at] = total.astype(BF)
        fourth.append(remote(to_y[part].at[1 - y, :, at], got_y[part].at[:, at], send.at[i, wide + deep - 1], recv.at[i, wide + deep - 1], partner))
        fourth[i].start()

    def deliver(part, half, at, values):
        hidden = 4 * cols
        if part == 0:
            up_ref[:, pl.ds(pl.multiple_of(half * hidden + at.start, LANES), at.stop - at.start)] = values
        elif part == 1:
            down_ref[pl.ds(pl.multiple_of(half * hidden + at.start, 8), at.stop - at.start), :] = values.T
        else:
            for piece in range(at.start // cols, at.stop // cols):
                some = values[:, piece * cols - at.start : (piece + 1) * cols - at.start]
                if piece < 3:
                    qkv_ref[piece, :, pl.ds(pl.multiple_of(half * cols, LANES), cols)] = some
                else:
                    wo_ref[pl.ds(pl.multiple_of(half * cols, 8), cols), :] = some.T

    def last(i):
        part, at = cuts[i]
        deliver(part, y, at, to_y[part][y, :, at].astype(F32))
        fourth[i].wait_recv()
        deliver(part, 1 - y, at, got_y[part][:, at].astype(F32))

    def compact_rows(ref, side):
        base = (y if side == 0 else 1 - y) * (own_rows // PATCHES)
        parts = [ref[pl.ds(pl.multiple_of((base + at) * SLOT, 16), PATCHES), :].astype(F32) for at in range(own_rows // PATCHES)]
        return jnp.concatenate(parts, axis=0)

    def head_weight(at):
        value = head_w[..., at]
        return value.reshape(width, value.shape[-1])

    for name in ("o", "heads", "out"):
        loads[name].wait()
    for side, part in ((1, other), (0, own)):
        mixed[part, :] = compact_rows(s_o, side).astype(BF)
    out_weight = head_weight(slice(3 * cols, 4 * cols))

    def add_out(part):
        out[part, :] = (out[part, :].astype(F32) + dot(mixed[part, :], out_weight, NT)).astype(BF)

    add_out(other)
    rows_copy = [remote(out.at[pl.ds(own_rows, own_rows)], out_got, tsend.at[deep + wide], trecv.at[deep + wide], partner)]
    rows_copy[0].start()
    for i in range(4):
        over_x(i)

    ones_low = head_ones(cols)
    gains = []
    for names, grad_in, raw_ref, gain, at in ((("dq", "qraw"), s_dq, qraw, qg_ref, 0), (("dk", "kraw"), s_dk, kraw, kg_ref, 1)):
        for name in names:
            loads[name].wait()
        total = jnp.zeros((1, cols), F32)
        for side, part in ((1, other), (0, own)):
            hat, scale = head_stats(raw_ref[part, :].astype(F32), ones_low)
            grad = compact_rows(grad_in, side)
            total += jnp.sum(grad * hat, axis=0, keepdims=True)
            scaled = grad * gain[...]
            d_raw = (scaled - split_dot(scaled, ones_low) - hat * split_dot(scaled * hat, ones_low)) * scale
            d_proj[part, at * cols : (at + 1) * cols] = d_raw.astype(BF)
        folded = total[:, :HD]
        for head in range(1, cols // HD):
            folded += total[:, head * HD : (head + 1) * HD]
        gains.append(folded)
    loads["dv"].wait()
    for side, part in ((1, other), (0, own)):
        d_proj[part, 2 * cols : 3 * cols] = compact_rows(s_dv, side).astype(BF)

    loads["dn"].wait()

    def add_dn(part):
        dn[part, :] = (dn[part, :].astype(F32) + dot(d_proj[part, :], head_weight(slice(0, 3 * cols)), NT)).astype(BF)

    add_dn(other)
    rows_copy.append(remote(dn.at[pl.ds(own_rows, own_rows)], dn_got, tsend.at[deep + wide + 1], trecv.at[deep + wide + 1], partner))
    rows_copy[1].start()
    over_z(0)
    loads["normed"].wait()
    loads["dy"].wait()

    def keep(at, values):
        for b, (zz, xx, cc, s) in enumerate(places):
            mine[2][zz, xx, cc, s, :, at] = values[b * shard : (b + 1) * shard].astype(BF)

    for piece in range(2):
        at = slice(piece * cols, (piece + 1) * cols)
        keep(at, dot(normed[...], d_proj[:, at], TN))
    over_core(4)
    over_z(1)
    keep(slice(2 * cols, 3 * cols), dot(normed[...], d_proj[:, 2 * cols : 3 * cols], TN))
    keep(slice(3 * cols, 4 * cols), dot(cotan[...], mixed[own, :], TN) + dot(dy_par[...], mixed[other, :], TN))
    over_core(5)
    over_y(0)
    over_z(2)
    over_x(4)
    add_out(own)
    add_dn(own)
    loads["x"].wait()
    grad_g = jnp.zeros((1, width), F32)
    for side, part in ((tokens, own), (x_par, other)):
        vhat, _ = norm_stats(side[...].astype(F32))
        grad_g += jnp.sum(dn[part, :].astype(F32) * vhat, axis=0, keepdims=True)
    grad_db = jnp.sum(cotan[...].astype(F32), axis=0, keepdims=True)
    per = gb_ref.shape[1] // batch
    both = jnp.concatenate(gains, axis=1)
    bias = gb_ref[...]
    for b, (zz, xx, cc, s) in enumerate(places):
        inside = jnp.where(y == b // batch, 1.0, 0.0)
        t_all[zz, xx, cc, s, 0:1, :shard] = grad_g[:, b * shard : (b + 1) * shard]
        t_all[zz, xx, cc, s, 1:2, :shard] = grad_db[:, b * shard : (b + 1) * shard]
        t_all[zz, xx, cc, s, 2:3, :per] = bias[:, (b % batch) * per : (b % batch + 1) * per] * inside
        t_all[zz, xx, cc, s, 3:4, : 2 * HD] = both
    tiny = [remote(t_all.at[:, :, 1 - core], t_core, tsend.at[0], trecv.at[0], sibling)]
    tiny[0].start()
    over_x(5)
    over_y(1)
    over_z(3)
    tiny[0].wait_recv()
    t_x[...] = t_all[:, :, core] + t_core[...]
    group = []
    for s, peer in enumerate(along_x):
        group.append(remote(t_x.at[:, (x + s + 1) % wide], t_xgot.at[x], tsend.at[1 + s], trecv.at[1 + s], peer))
        group[s].start()
    tiny += group
    t_xgot[x] = t_x[:, x]
    over_y(2)
    rows_copy[0].wait_recv()
    block_ref[...] = (tokens[...].astype(F32) + out[own, :].astype(F32) + out_got[...].astype(F32) + db_ref[...]).astype(BF)
    for copy in group:
        copy.wait_recv()
    total = t_xgot[0]
    for xx in range(1, wide):
        total += t_xgot[xx]
    t_z[...] = total
    group = []
    for s, peer in enumerate(along_z):
        group.append(remote(t_z.at[(z + s + 1) % deep], t_zgot.at[z], tsend.at[wide + s], trecv.at[wide + s], peer))
        group[s].start()
    tiny += group
    t_zgot[z] = t_z[z]
    over_z(4)
    over_y(3)
    for copy in group:
        copy.wait_recv()
    total = t_zgot[0]
    for zz in range(1, deep):
        total += t_zgot[zz]
    t_y[...] = total
    tiny.append(remote(t_y.at[1 - y], t_ygot, tsend.at[wide + deep - 1], trecv.at[wide + deep - 1], partner))
    tiny[-1].start()
    over_z(5)
    for i in range(4):
        last(i)
    over_y(4)
    over_y(5)
    tiny[-1].wait_recv()
    small_ref[...] = t_y[y] + t_ygot[...]
    last(4)
    last(5)
    vhat, scale = norm_stats(tokens[...].astype(F32))
    rows_copy[1].wait_recv()
    scaled = (dn[own, :].astype(F32) + dn_got[...].astype(F32)) * gain_ref[...]
    d_tokens = (scaled - jnp.mean(scaled, axis=-1, keepdims=True) - vhat * jnp.mean(scaled * vhat, axis=-1, keepdims=True)) * scale
    grad_ref[...] = (cotan[...].astype(F32) + d_tokens).astype(BF)
    for copy in first + [c for g in second + third for c in g] + fourth + tiny + rows_copy:
        copy.wait_send()


def last_half(tokens, cotan, gain, down_b, gb, qg, kg, kept, grads, batch):
    deep, wide = grid_of(batch)
    own_rows, width = tokens.shape
    rows = 2 * own_rows
    hidden = grads[0].shape[1]
    cols = hidden // 4
    block = hidden // 2
    shard = width // (2 * batch)
    x_par, dy_par, normed, o, dq, dk, dv, qraw, kraw, head_w, out, dn = kept
    direct = head_w.ndim > 2
    cuts = [(part, slice(at, at + block)) for part in range(3) for at in (0, block)]
    vm = pl.BlockSpec(memory_space=pltpu.VMEM)
    hbm = pl.BlockSpec(memory_space=pl.ANY)
    shaped = [g.reshape(deep, wide, 2, 2, shard, hidden) for g in grads]
    buf = lambda *shape: pltpu.VMEM(shape, BF)
    tile = lambda *lead: pltpu.VMEM(lead + TINY, F32)
    half = (deep, wide, 2, shard, hidden)
    scratch = [buf(*k.shape) for k in kept]
    scratch += [buf(*half), buf(*half), buf(deep, wide, 2, 2, shard, hidden)]
    scratch += [buf(*half)] * 3 + [buf(wide, deep, 2, shard, hidden)] * 3 + [buf(deep, 2, shard, hidden)] * 6 + [buf(2, shard, hidden)] * 3 + [buf(shard, hidden)] * 3
    scratch += [buf(rows, 3 * cols), buf(rows, cols), buf(own_rows, width), buf(own_rows, width)]
    scratch += [tile(deep, wide, 2, 2), tile(deep, wide, 2), tile(deep, wide, 2), tile(wide, deep, 2), tile(deep, 2), tile(deep, 2), tile(2), tile()]
    scratch += [pltpu.SemaphoreType.DMA((len(cuts), deep + wide))] * 2 + [pltpu.SemaphoreType.DMA((deep + wide + 2,))] * 2 + [pltpu.SemaphoreType.DMA((len(kept),)), pltpu.SemaphoreType.DMA((4,))]
    full = lambda *shape: jax.ShapeDtypeStruct(shape, F32)
    return pl.pallas_call(
        functools.partial(last_kernel, deep=deep, wide=wide, cuts=cuts),
        in_specs=[vm] * 7 + [hbm] * 14,
        out_specs=[vm] * 7,
        out_shape=[jax.ShapeDtypeStruct((own_rows, width), BF)] * 2 + [full(3, shard, 2 * cols), full(2 * cols, shard), full(shard, 2 * hidden), full(2 * hidden, shard), full(*TINY)],
        scratch_shapes=scratch,
        compiler_params=pltpu.CompilerParams(collective_id=1, has_side_effects=True, vmem_limit_bytes=VMEM_CAP),
        name="head_gradients_and_scatter",
    )(tokens, cotan, gain, down_b, gb, qg, kg, *kept, *shaped)


def local(tokens, cotangent, image_tokens, w_qkv, w_out, w_up, bias_up, w_down, bias_down, norm_gain, query_gain, key_gain):
    batch = lax.axis_size("batch")
    shard = w_up.shape[0]
    half_of = lambda m: jnp.stack([m[:, : m.shape[1] // 2], m[:, m.shape[1] // 2 :]])
    low = lambda m: m.astype(BF)
    head_pack = jnp.concatenate([half_of(low(w_qkv[0])), half_of(low(w_qkv[1])), half_of(low(w_qkv[2])), half_of(low(w_out.T))], axis=2)
    packs = [half_of(low(w_up)), half_of(low(w_down.T)), head_pack]
    cols = w_qkv.shape[2] // 2
    query_g = jnp.tile(low(query_gain).astype(F32), cols // HD)[None, :]
    key_g = jnp.tile(low(key_gain).astype(F32), cols // HD)[None, :]
    tiny = lay_out([norm_gain, bias_down, bias_up])
    x_par, dy_par, normed, q, k, v, d_o, qraw, kraw, head_w, out, dn, d_up, d_down, gb, gain, down_b = first_half(tokens, cotangent, tiny, packs, query_g, key_g, batch)
    o, dq, dk, dv = attention(image_tokens[0], q, k, v, d_o)
    kept = [x_par, dy_par, normed, o, dq, dk, dv, qraw, kraw, head_w, out, dn]
    block_out, grad_tokens, g_qkv, g_out, g_up, g_down, small = last_half(tokens, cotangent, gain, down_b, gb, query_g, key_g, kept, [d_up, d_down], batch)
    per = bias_up.shape[0]
    return (block_out, grad_tokens, g_qkv, g_out, g_up, small[2, :per], g_down, small[1, :shard], small[0, :shard], small[3, :HD], small[3, HD : 2 * HD])


def solution(mesh):
    both = ("batch", "branch")
    in_specs = (P(both, None), P(both, None), P("batch", None), P(None, both, None), P(None, both), P(both, None), P(both), P(None, both), P(both), P(both), P(), P())
    out_specs = (P(both, None), P(both, None), P(None, both, None), P(None, both), P(both, None), P(both), P(None, both), P(both), P(both), P(), P())
    return jax.shard_map(local, mesh=mesh, in_specs=in_specs, out_specs=out_specs, check_vma=False)
```

```python
import functools
import jax
import jax.numpy as jnp
from jax import lax
from jax.experimental import pallas as pl
from jax.experimental.pallas import tpu as pltpu
from jax.sharding import PartitionSpec as P

HD = 64
LANES = 128
NORM_EPS = 1e-06
LONGEST = 784
PATCHES = 196
SLOT = 208
VMEM_CAP = 66_000_000
BF = jnp.bfloat16
F32 = jnp.float32


def dot(a, b, dims=((1,), (0,))):
    return lax.dot_general(a, b, (dims, ((), ())), preferred_element_type=F32)


NT = ((1,), (1,))
TN = ((0,), (0,))


def norm_stats(values):
    centred = values - jnp.mean(values, axis=-1, keepdims=True)
    spread = jnp.mean(centred * centred, axis=-1, keepdims=True)
    scale = lax.rsqrt(spread + NORM_EPS)
    return centred * scale, scale


def head_means(values, ones_low):
    means = []
    for at in range(0, values.shape[1], LANES):
        some = values[:, at : at + LANES]
        high = some.astype(BF)
        low = (some - high.astype(F32)).astype(BF)
        means.append(dot(jnp.concatenate([high, low], axis=1), ones_low))
    return jnp.concatenate(means, axis=1)


def head_ones():
    row = lax.broadcasted_iota(jnp.int32, (2 * LANES, LANES), 0) % LANES // HD
    col = lax.broadcasted_iota(jnp.int32, (2 * LANES, LANES), 1) // HD
    return jnp.where(row == col, 1.0 / HD, 0.0).astype(BF)


def head_stats(raw, ones_low):
    centred = raw - head_means(raw, ones_low)
    scale = lax.rsqrt(head_means(centred * centred, ones_low) + NORM_EPS)
    return centred * scale, scale


MESH = pl.DeviceIdType.MESH


def place():
    return lax.axis_index("batch"), lax.axis_index("branch")


def grid_of(batch):
    chips = batch // 2
    across = 1
    while across * across * 4 <= chips:
        across *= 2
    return chips // across, across


def greet(peers):
    barrier = pltpu.get_barrier_semaphore()
    for peer in peers:
        pl.semaphore_signal(barrier, inc=1, device_id=peer, device_id_type=MESH)
    pl.semaphore_wait(barrier, len(peers))


def neighbours(deep, wide):
    batch, branch = place()
    core, x, z = batch % 2, (batch // 2) % wide, batch // (2 * wide)
    at = lambda zz, xx, cc: (zz * wide + xx) * 2 + cc
    partner = (batch, 1 - branch)
    along_z = [(at((z + s) % deep, x, core), branch) for s in range(1, deep)]
    along_x = [(at(z, (x + s) % wide, core), branch) for s in range(1, wide)]
    sibling = (at(z, x, 1 - core), branch)
    return (z, x, core, branch), partner, along_z, along_x, sibling


def remote(src, dst, send, recv, peer):
    return pltpu.make_async_remote_copy(src_ref=src, dst_ref=dst, send_sem=send, recv_sem=recv, device_id=peer, device_id_type=MESH)


TINY = (8, LANES)


def gelu_parts(hidden):
    square = hidden * hidden
    tanh = jnp.tanh(hidden * (0.7978845608028654 + 0.035677408136300125 * square))
    half = 0.5 + 0.5 * tanh
    act = hidden * half
    slope = half + (act * (1.0 - tanh)) * (0.7978845608028654 + 0.1070322244089 * square)
    return act.astype(BF), slope


def repeated(values, count):
    return jnp.concatenate([values] * count, axis=1)


def first_kernel(*refs, deep, wide, cuts, block):
    tokens, cotan, qkv_ref, wo_ref, up_ref, down_ref, nb_ref, db_ref, ub_ref, qg_ref, kg_ref = refs[:11]
    o_x, o_dy, o_normed, o_q, o_k, o_v, o_do, o_qraw, o_kraw, o_heads, o_own, o_other, o_dn = refs[11:24]
    o_sums = (refs[24 : 24 + wide], refs[24 + wide : 24 + 2 * wide])
    gb_ref, gain_ref, bias_ref, tiny = refs[24 + 2 * wide : 28 + 2 * wide]
    scratch = refs[28 + 2 * wide :]
    packs, lands, wires = scratch[:3], scratch[3:6], scratch[6:9]
    rounded, tiny_all, x_par, dy_par, normed, act, d_hid, s_q, s_k, s_v, s_do, s_qraw, s_kraw, s_out, s_dn = scratch[9:24]
    grads, got_core, flats = scratch[24:26], scratch[26:28], scratch[28:31]
    send, recv, tsend, trecv, csend, crecv, osem = scratch[31:]
    (z, x, core, y), partner, along_z, along_x, sibling = neighbours(deep, wide)
    batch = 2 * deep * wide
    own_rows, width = tokens.shape
    shard, hidden = packs[0].shape[1:]
    cols = hidden // 4
    pair = 2 * shard
    direct = pair % 16 == 0
    places = [(b // (2 * wide), (b // 2) % wide, b % 2, s) for b in range(batch) for s in range(2)]

    for half in range(2):
        some = slice(half * cols, (half + 1) * cols)
        packs[0][half] = up_ref[:, half * hidden : (half + 1) * hidden].astype(BF)
        packs[1][half] = down_ref[:, half * hidden : (half + 1) * hidden].astype(BF)
        for at in range(3):
            packs[2][half, :, at * cols : (at + 1) * cols] = qkv_ref[at, :, some].astype(BF)
        packs[2][half, :, 3 * cols :] = wo_ref[...].astype(BF)
    rounded[...] = jnp.zeros(TINY, BF)
    for row, ref in enumerate((nb_ref, db_ref, ub_ref, qg_ref, kg_ref)):
        rounded[row : row + 1, : ref.shape[1]] = ref[...].astype(BF)
    tiny[...] = rounded[...].astype(F32)
    tiny_all[z, x, core, y] = tiny[...]
    greet([partner, sibling] + along_z + along_x)
    outs = []

    def put(src, dst):
        copy = pltpu.make_async_copy(src, dst, osem.at[len(outs)])
        copy.start()
        outs.append(copy)

    spread_tiny = [remote(tiny, tiny_all.at[z, x, core, y], tsend.at[0], trecv.at[0], partner)]
    spread_tiny[0].start()
    over_y = []
    for i, (part, at) in enumerate(cuts):
        over_y.append(remote(packs[part].at[1 - y, :, at], lands[part].at[:, at], send.at[i, 0], recv.at[i, 0], partner))
        over_y[i].start()
    rows_copy = [remote(tokens, x_par, tsend.at[deep + wide], trecv.at[deep + wide], partner), remote(cotan, dy_par, tsend.at[deep + wide + 1], trecv.at[deep + wide + 1], partner)]
    for copy in rows_copy:
        copy.start()

    def tiny_stage(block, peers, first):
        group = [remote(block, block, tsend.at[first + s], trecv.at[first + s], peer) for s, peer in enumerate(peers)]
        for copy in group:
            copy.start()
        for copy in group:
            copy.wait_recv()
        spread_tiny.extend(group)

    over_z, over_x, over_core = [], [], []

    def start_z(i):
        part, at = cuts[i]
        over_y[i].wait_recv()
        mine, other = packs[part][y, :, at].astype(F32), lands[part][:, at].astype(F32)
        pair = jnp.concatenate([jnp.where(y == 0, mine, other), jnp.where(y == 0, other, mine)], axis=0)
        wires[part][z, x, core, :, at] = pair.astype(BF)
        block = wires[part].at[z, x, core, :, at]
        over_z.append([remote(block, block, send.at[i, 1 + s], recv.at[i, 1 + s], peer) for s, peer in enumerate(along_z)])
        for copy in over_z[i]:
            copy.start()

    def start_x(i):
        part, at = cuts[i]
        for copy in over_z[i]:
            copy.wait_recv()
        block = wires[part].at[:, x, core, :, at]
        over_x.append([remote(block, block, send.at[i, deep + s], recv.at[i, deep + s], peer) for s, peer in enumerate(along_x)])
        for copy in over_x[i]:
            copy.start()

    def start_core(i):
        part, at = cuts[i]
        for copy in over_x[i]:
            copy.wait_recv()
        block = wires[part].at[:, :, core, :, at]
        over_core.append(remote(block, block, send.at[i, deep + wide - 1], recv.at[i, deep + wide - 1], sibling))
        over_core[i].start()

    def arrive(i):
        part, at = cuts[i]
        over_core[i].wait_recv()
        if not direct:
            for b in range(batch):
                flats[part][2 * shard * b : 2 * shard * (b + 1), at] = wires[part][b // (2 * wide), (b // 2) % wide, b % 2, :, at]

    def weight(part, at):
        if direct:
            value = wires[part][:, :, :, :, at]
            return value.reshape(width, value.shape[-1])
        return flats[part][:, at]

    for i in range(len(cuts)):
        start_z(i)
        if i == 0:
            spread_tiny[0].wait_recv()
            tiny_stage(tiny_all.at[z, x, core], along_z, 1)
        if i == 1:
            tiny_stage(tiny_all.at[:, x, core], along_x, deep)
        if i == 2:
            tiny_stage(tiny_all.at[:, :, core], [sibling], deep + wide - 1)
    per = ub_ref.shape[1]
    gain_ref[...] = jnp.concatenate([tiny_all[p][0:1, :shard] for p in places], axis=1)
    bias_ref[...] = jnp.concatenate([tiny_all[p][1:2, :shard] for p in places], axis=1)
    low_b = jnp.concatenate([tiny_all[p][2:3, :per] for p in places[:batch]], axis=1)
    high_b = jnp.concatenate([tiny_all[p][2:3, :per] for p in places[batch:]], axis=1)
    gb_ref[...] = jnp.where(y == 0, low_b, high_b)

    sides = ((tokens, cotan, slice(0, own_rows)), (x_par, dy_par, slice(own_rows, 2 * own_rows)))

    def normalise(side):
        vhat, _ = norm_stats(sides[side][0][...].astype(F32))
        normed[sides[side][2], :] = (vhat * gain_ref[...]).astype(BF)

    def expand(side, at, back):
        rows = sides[side][2]
        act[rows, at], slope = gelu_parts(dot(normed[rows, :], weight(0, at)) + gb_ref[:, at])
        if back:
            slope *= dot(sides[side][1][...], weight(1, at))
        d_hid[rows, at] = slope.astype(BF)

    def apply_back(side, at):
        rows = sides[side][2]
        d_hid[rows, at] = (d_hid[rows, at].astype(F32) * dot(sides[side][1][...], weight(1, at))).astype(BF)

    def contract(side, low, kept, part):
        rows = sides[side][2]
        kept[rows, :] = dot(low[rows, :], weight(part, slice(0, hidden)), NT).astype(BF)

    def place_rows(side, ref, values):
        base = (y if side == 0 else 1 - y) * (own_rows // PATCHES)
        for at in range(own_rows // PATCHES):
            ref[pl.ds(pl.multiple_of((base + at) * SLOT, 16), PATCHES), :] = values[at * PATCHES : (at + 1) * PATCHES].astype(BF)

    def queries_keys(side):
        rows = sides[side][2]
        ones_low = head_ones()
        for at, (raw_ref, low_ref, gain) in enumerate(((s_qraw, s_q, 3), (s_kraw, s_k, 4))):
            raw = dot(normed[rows, :], weight(2, slice(at * cols, (at + 1) * cols)))
            raw_ref[rows, :] = raw.astype(BF)
            hat, _ = head_stats(raw, ones_low)
            place_rows(side, low_ref, hat * repeated(tiny[gain : gain + 1, :HD], cols // HD))

    def values_of(side):
        place_rows(side, s_v, dot(normed[sides[side][2], :], weight(2, slice(2 * cols, 3 * cols))))

    def back_of(side):
        place_rows(side, s_do, dot(sides[side][1][...], weight(2, pl.ds(pl.multiple_of((3 + y) * cols, LANES), cols))))

    over_sib = []

    def grad_own(part, at):
        rows = sides[0][2]
        value = dot(normed[rows, :], d_hid[rows, at], TN) if part == 0 else dot(cotan[...], act[rows, at], TN)
        for b in range(batch):
            grads[part][b // (2 * wide), (b // 2) % wide, b % 2, :, at] = value[b * pair : (b + 1) * pair].astype(BF)

    def grad_rest(part, at):
        rows = sides[1][2]
        value = dot(normed[rows, :], d_hid[rows, at], TN) if part == 0 else dot(dy_par[...], act[rows, at], TN)
        for b in range(batch):
            block_at = (b // (2 * wide), (b // 2) % wide, b % 2, slice(None), at)
            grads[part][block_at] = (grads[part][block_at].astype(F32) + value[b * pair : (b + 1) * pair]).astype(BF)
        i = len(over_sib)
        over_sib.append(remote(grads[part].at[:, :, 1 - core, :, at], got_core[part].at[:, :, :, at], csend.at[i], crecv.at[i], sibling))
        over_sib[i].start()

    def add_core(i, part, at):
        over_sib[i].wait_recv()

        @pl.loop(0, deep)
        def _(zz):
            for xx in range(wide):
                total = grads[part][zz, xx, core, :, at].astype(F32) + got_core[part][zz, xx, :, at].astype(F32)
                got_core[part][zz, xx, :, at] = total.astype(BF)

    first, second = slice(0, block), slice(block, 2 * block)
    start_x(0)
    normalise(0)
    start_x(1)
    start_core(0)
    start_x(2)
    start_core(1)
    arrive(0)
    arrive(1)
    expand(0, first, True)
    start_x(3)
    start_core(2)
    rows_copy[0].wait_recv()
    normalise(1)
    put(x_par, o_x)
    put(normed, o_normed)
    expand(1, first, False)
    start_x(4)
    grad_own(0, first)
    start_core(3)
    grad_own(1, first)
    arrive(2)
    arrive(3)
    expand(0, second, True)
    start_core(4)
    expand(1, second, False)
    start_x(5)
    contract(0, act, s_out, 1)
    contract(0, d_hid, s_dn, 0)
    grad_own(0, second)
    grad_own(1, second)
    arrive(4)
    queries_keys(0)
    start_core(5)
    queries_keys(1)
    for src, dst in ((s_q, o_q), (s_k, o_k), (s_qraw, o_qraw), (s_kraw, o_kraw)):
        put(src, dst)
    contract(1, act, s_out, 1)
    put(s_out.at[pl.ds(0, own_rows)], o_own)
    put(s_out.at[pl.ds(own_rows, own_rows)], o_other)
    arrive(5)
    put(wires[2] if direct else flats[2], o_heads)
    values_of(0)
    values_of(1)
    put(s_v, o_v)
    back_of(0)
    rows_copy[1].wait_recv()
    put(dy_par, o_dy)
    back_of(1)
    put(s_do, o_do)
    apply_back(1, first)
    apply_back(1, second)
    contract(1, d_hid, s_dn, 0)
    put(s_dn, o_dn)
    grad_rest(0, first)
    grad_rest(0, second)
    add_core(0, 0, first)
    grad_rest(1, first)
    add_core(1, 0, second)
    for s in range(wide):
        put(got_core[0].at[:, (x + s) % wide], o_sums[0][s])
    grad_rest(1, second)
    add_core(2, 1, first)
    gb_ref[...] = dot(jnp.ones((8, 2 * own_rows), BF), d_hid[...])[:1]
    add_core(3, 1, second)
    for s in range(wide):
        put(got_core[1].at[:, (x + s) % wide], o_sums[1][s])
    for copy in outs:
        copy.wait()
    for copy in spread_tiny + over_y + rows_copy + [c for group in over_z + over_x for c in group] + over_core + over_sib:
        copy.wait_send()


def first_half(tokens, cotan, weights, vectors, batch):
    deep, wide = grid_of(batch)
    own_rows, width = tokens.shape
    shard, hidden = weights[2].shape[0], weights[2].shape[1] // 2
    cols = hidden // 4
    block = hidden // 2
    rows = 2 * own_rows
    spread_rows = rows // PATCHES * SLOT
    widths = (hidden, hidden, 5 * cols)
    first, second = slice(0, block), slice(block, hidden)
    cuts = [(0, first), (1, first), (0, second), (1, second), (2, slice(0, 2 * cols)), (2, slice(2 * cols, 5 * cols))]
    vm = pl.BlockSpec(memory_space=pltpu.VMEM)
    hbm = pl.BlockSpec(memory_space=pl.ANY)
    direct = (2 * shard) % 16 == 0
    wire_shapes = [(deep, wide, 2, 2 * shard, w) for w in widths]
    flat_shapes = [(width, w) for w in widths]
    low = lambda *shape: jax.ShapeDtypeStruct(shape, BF)
    outs = [low(own_rows, width)] * 2 + [low(rows, width)] + [low(spread_rows, cols)] * 4 + [low(rows, cols)] * 2
    outs += [low(*(wire_shapes if direct else flat_shapes)[2])] + [low(own_rows, width)] * 2 + [low(rows, width)] + [low(deep, 2 * shard, hidden)] * (2 * wide)
    tiny_outs = [jax.ShapeDtypeStruct((1, hidden), F32), jax.ShapeDtypeStruct((1, width), F32), jax.ShapeDtypeStruct((1, width), F32), jax.ShapeDtypeStruct(TINY, F32)]
    buf = lambda *shape: pltpu.VMEM(shape, BF)
    scratch = [buf(2, shard, w) for w in widths] + [buf(shard, w) for w in widths] + [buf(*s) for s in wire_shapes]
    scratch += [buf(*TINY), pltpu.VMEM((deep, wide, 2, 2) + TINY, F32), buf(own_rows, width), buf(own_rows, width), buf(rows, width), buf(rows, hidden), buf(rows, hidden)]
    scratch += [buf(spread_rows, cols)] * 4 + [buf(rows, cols)] * 2 + [buf(rows, width)] * 2
    scratch += [buf(deep, wide, 2, 2 * shard, hidden)] * 2 + [buf(deep, wide, 2 * shard, hidden)] * 2
    scratch += [buf(16, LANES) if direct else buf(*s) for s in flat_shapes]
    scratch += [pltpu.SemaphoreType.DMA((len(cuts), deep + wide))] * 2 + [pltpu.SemaphoreType.DMA((deep + wide + 2,))] * 2 + [pltpu.SemaphoreType.DMA((4,))] * 2 + [pltpu.SemaphoreType.DMA((len(outs),))]
    return pl.pallas_call(
        functools.partial(first_kernel, deep=deep, wide=wide, cuts=cuts, block=block),
        in_specs=[vm] * 11,
        out_specs=[hbm] * len(outs) + [vm] * 4,
        out_shape=outs + tiny_outs,
        scratch_shapes=scratch,
        compiler_params=pltpu.CompilerParams(collective_id=0, has_side_effects=True, vmem_limit_bytes=VMEM_CAP),
        name="gather_and_feed_forward",
    )(tokens, cotan, *weights, *vectors)


def load_rows(ref, block, blocks):
    parts = [ref[pl.ds(pl.multiple_of((block + at) * SLOT, 16), PATCHES), :] for at in range(blocks)]
    return parts[0] if blocks == 1 else jnp.concatenate([p.astype(F32) for p in parts], axis=0).astype(BF)

def attend_pair(pair_q, pair_k, pair_v, pair_do, pieces):
    count = pair_q.shape[0]
    lane = lax.broadcasted_iota(jnp.int32, (count, 2 * HD), 1)
    pair_q = pair_q * jnp.asarray(0.125, BF)
    zero = jnp.zeros_like(pair_q)
    v_t, k_t = pair_v.T, pair_k.T
    mixed, grads_q, grad_k, grad_v = [], [], None, None
    for head in range(2):
        mine = (lane < HD) if head == 0 else (lane >= HD)
        q_m, do_m = jnp.where(mine, pair_q, zero), jnp.where(mine, pair_do, zero)
        part = slice(head * HD, (head + 1) * HD)
        outs, gqs = [], []
        for first, size in pieces:
            q, d_o = q_m[first : first + size], do_m[first : first + size]
            shifted = jnp.exp(dot(pair_k, q, NT))
            total = jnp.sum(shifted, axis=0, keepdims=True)
            weights = shifted * (1.0 / total)
            low = weights.astype(BF)
            d_weights = dot(pair_v, d_o, NT)
            inner = jnp.sum(weights * d_weights, axis=0, keepdims=True)
            d_scores = (weights * (d_weights - inner)).astype(BF)
            outs.append(dot(v_t[part], low))
            gqs.append(dot(k_t[part], d_scores))
            gv, gk = dot(low, d_o), dot(d_scores, q)
            grad_v = gv if grad_v is None else grad_v + gv
            grad_k = gk if grad_k is None else grad_k + gk
        join = lambda parts: parts[0] if len(parts) == 1 else jnp.concatenate(parts, axis=1)
        mixed.append(join(outs))
        grads_q.append(join(gqs))
    turn = lambda parts: jnp.concatenate(parts, axis=0).T
    return turn(mixed), turn(grads_q) * 0.125, grad_k, grad_v

def attention_kernel(count_ref, *refs, pieces, together):
    ins, outs, (small_ref,) = refs[:4], refs[4:8], refs[8:]
    place, smalls, bigs, big_at = 0, 0, 0, 0
    for slot in range(count_ref.shape[0]):
        count = count_ref[slot]
        is_small = (count == PATCHES).astype(jnp.int32)
        is_big = (count == LONGEST).astype(jnp.int32)
        small_ref[smalls] = place
        big_at = jnp.where(is_big == 1, place, big_at)
        smalls, bigs = smalls + is_small, bigs + is_big
        place = place + is_small + (LONGEST // PATCHES) * is_big

    def images(firsts, blocks, pieces):
        loaded = [[load_rows(ref, block, blocks) for ref in ins] for block in firsts]
        results = [attend_pair(*values, pieces) for values in loaded]
        for block, result in zip(firsts, results):
            for ref, values in zip(outs, result):
                for at in range(blocks):
                    ref[pl.ds(pl.multiple_of((block + at) * SLOT, 16), PATCHES), :] = values[at * PATCHES : (at + 1) * PATCHES].astype(ref.dtype)

    @pl.when(bigs > 0)
    def _():
        images([big_at], LONGEST // PATCHES, pieces)

    @pl.loop(0, smalls // together)
    def _(turn):
        images([small_ref[turn * together + at] for at in range(together)], 1, ((0, PATCHES),))

def attention(counts, q, k, v, d_o, pieces=((0, 784),), together=4):
    rows, cols = q.shape
    sm = pl.BlockSpec(memory_space=pltpu.SMEM)
    blk = pl.BlockSpec((rows, 2 * HD), lambda j: (0, j))
    return pl.pallas_call(
        functools.partial(attention_kernel, pieces=pieces, together=together),
        grid=(cols // (2 * HD),),
        in_specs=[sm] + [blk] * 4,
        out_specs=[blk] * 4,
        out_shape=[jax.ShapeDtypeStruct((rows, cols), t) for t in (BF, BF, BF, BF)],
        scratch_shapes=[pltpu.SMEM((counts.shape[0] + 1,), jnp.int32)],
        compiler_params=pltpu.CompilerParams(vmem_limit_bytes=VMEM_CAP),
        cost_estimate=pl.CostEstimate(flops=20_000_000_000, bytes_accessed=20_000_000, transcendentals=rows * LONGEST * cols // HD),
        name="attention",
    )(counts, q, k, v, d_o)


def last_kernel(*refs, deep, wide, cuts):
    tokens, cotan, bias_ref, gb_ref, gains_ref = refs[:5]
    i_x, i_dy, i_normed, i_o, i_dq, i_dk, i_dv, i_qraw, i_kraw, i_heads, i_own, i_got, i_dn = refs[5:18]
    i_sums = (refs[18 : 18 + wide], refs[18 + wide : 18 + 2 * wide])
    o_dn, o_dn_got, block_ref, qkv_ref, wo_ref, up_ref, down_ref, small_ref = refs[18 + 2 * wide : 26 + 2 * wide]
    scratch = refs[26 + 2 * wide :]
    x_par, dy_par, normed, s_o, s_dq, s_dk, s_dv, qraw, kraw, head_w, out_own, out_got, dn = scratch[:13]
    terms = scratch[13:15]
    mine, got_core, got_x = scratch[15:18]
    to_z, got_z, to_y, got_y = (scratch[18 + 3 * i : 21 + 3 * i] for i in range(4))
    d_proj, mixed, o_got = scratch[30:33]
    t_all, t_core, t_x, t_xgot, t_z, t_zgot, t_y, t_ygot = scratch[33:41]
    send, recv, tsend, trecv, lsem, gsem, osem = scratch[41:]
    (z, x, core, y), partner, along_z, along_x, sibling = neighbours(deep, wide)
    batch = 2 * deep * wide
    own_rows, width = tokens.shape
    rows = 2 * own_rows
    cols = qraw.shape[1]
    shard = to_y[0].shape[0]
    slots = own_rows // PATCHES
    places = [(b // (2 * wide), (b // 2) % wide, b % 2, s) for b in range(batch) for s in range(2)]
    own, other = slice(0, own_rows), slice(own_rows, rows)
    greet([partner, sibling] + along_z + along_x)

    theirs = pl.ds(pl.multiple_of((1 - y) * slots * SLOT, 16), slots * SLOT)
    rows_copy = [remote(i_o.at[theirs], o_got, tsend.at[deep + wide], trecv.at[deep + wide], partner)]
    rows_copy[0].start()
    held = {}
    for part in range(2):
        for s in range(wide):
            held[part, s] = pltpu.make_async_copy(i_sums[part][s], terms[part].at[s], gsem.at[part * wide + s])
            held[part, s].start()
    loads = {}
    for at, (name, src, dst) in enumerate((("qraw", i_qraw, qraw), ("dq", i_dq, s_dq), ("kraw", i_kraw, kraw), ("dk", i_dk, s_dk), ("dv", i_dv, s_dv), ("heads", i_heads, head_w), ("dn", i_dn, dn), ("normed", i_normed, normed), ("o", i_o, s_o), ("dy", i_dy, dy_par), ("x", i_x, x_par), ("own", i_own, out_own), ("got", i_got, out_got))):
        loads[name] = pltpu.make_async_copy(src, dst, lsem.at[at])
        loads[name].start()

    first, second, third, fourth = {}, {}, {}, {}

    def over_core(i):
        part, at = cuts[i]
        first[i] = remote(mine.at[:, :, 1 - core, :, at], got_core.at[:, :, :, at], send.at[i, 0], recv.at[i, 0], sibling)
        first[i].start()

    def over_x(i):
        part, at = cuts[i]
        first[i].wait_recv()

        @pl.loop(0, deep)
        def _(zz):
            for xx in range(wide):
                got_core[zz, xx, :, at] = (mine[zz, xx, core, :, at].astype(F32) + got_core[zz, xx, :, at].astype(F32)).astype(BF)

        second[i] = []
        for s, peer in enumerate(along_x):
            copy = remote(got_core.at[:, (x + s + 1) % wide, :, at], got_x.at[s, :, :, at], send.at[i, 1 + s], recv.at[i, 1 + s], peer)
            copy.start()
            second[i].append(copy)

    def over_z(i):
        part, at = cuts[i]
        if part == 2:
            for copy in second[i]:
                copy.wait_recv()

        @pl.loop(0, deep)
        def _(zz):
            if part == 2:
                total = got_core[zz, x, :, at].astype(F32)
                for s in range(wide - 1):
                    total += got_x[s, zz, :, at].astype(F32)
            else:
                total = terms[part][0, zz, :, at].astype(F32)
                for s in range(1, wide):
                    total += terms[part][s, zz, :, at].astype(F32)
            to_z[part][zz, :, at] = total.astype(BF)

        third[i] = []
        for s, peer in enumerate(along_z):
            copy = remote(to_z[part].at[(z + s + 1) % deep, :, at], got_z[part].at[s, :, at], send.at[i, wide + s], recv.at[i, wide + s], peer)
            copy.start()
            third[i].append(copy)

    def over_y(i):
        part, at = cuts[i]
        for copy in third[i]:
            copy.wait_recv()
        total = to_z[part][z, :, at].astype(F32)
        for s in range(deep - 1):
            total += got_z[part][s, :, at].astype(F32)
        low, high = total[:shard], total[shard:]
        to_y[part][:, at] = jnp.where(y == 0, high, low).astype(BF)
        fourth[i] = remote(to_y[part].at[:, at], got_y[part].at[:, at], send.at[i, wide + deep - 1], recv.at[i, wide + deep - 1], partner)
        fourth[i].start()
        deliver(part, y, at, jnp.where(y == 0, low, high))

    def deliver(part, half, at, values):
        if part < 2:
            ref = (up_ref, down_ref)[part]
            ref[:, pl.ds(pl.multiple_of(half * 4 * cols + at.start, LANES), at.stop - at.start)] = values
            return
        for piece in range(at.start // cols, at.stop // cols):
            some = values[:, piece * cols - at.start : (piece + 1) * cols - at.start]
            lanes = pl.ds(pl.multiple_of(half * cols, LANES), cols)
            if piece < 3:
                qkv_ref[piece, :, lanes] = some
            else:
                wo_ref[:, lanes] = some

    def last(i):
        part, at = cuts[i]
        fourth[i].wait_recv()
        deliver(part, 1 - y, at, got_y[part][:, at].astype(F32))

    def compact_rows(ref, base):
        parts = [ref[pl.ds(pl.multiple_of((base + at) * SLOT, 16), PATCHES), :].astype(F32) for at in range(slots)]
        return jnp.concatenate(parts, axis=0)

    bases = (y * slots, (1 - y) * slots)

    def head_weight(at):
        value = head_w[..., at]
        return value.reshape(width, value.shape[-1])

    for part in range(2):
        for s in range(wide):
            held[part, s].wait()
    for i in range(4):
        over_z(i)
    ones_low = head_ones()
    gains = []
    for names, grad_in, raw_ref, gain, at in ((("dq", "qraw"), s_dq, qraw, 3, 0), (("dk", "kraw"), s_dk, kraw, 4, 1)):
        for name in names:
            loads[name].wait()
        total = jnp.zeros((1, cols), F32)
        for side, part in ((1, other), (0, own)):
            hat, scale = head_stats(raw_ref[part, :].astype(F32), ones_low)
            grad = compact_rows(grad_in, bases[side])
            total += jnp.sum(grad * hat, axis=0, keepdims=True)
            scaled = grad * repeated(gains_ref[gain : gain + 1, :HD], cols // HD)
            d_raw = (scaled - head_means(scaled, ones_low) - hat * head_means(scaled * hat, ones_low)) * scale
            d_proj[part, at * cols : (at + 1) * cols] = d_raw.astype(BF)
        folded = total[:, :HD]
        for head in range(1, cols // HD):
            folded += total[:, head * HD : (head + 1) * HD]
        gains.append(folded)
    loads["dv"].wait()
    for side, part in ((1, other), (0, own)):
        d_proj[part, 2 * cols : 3 * cols] = compact_rows(s_dv, bases[side]).astype(BF)
    loads["dn"].wait()
    loads["heads"].wait()

    def add_dn(part):
        dn[part, :] = (dn[part, :].astype(F32) + dot(d_proj[part, :], head_weight(slice(0, 3 * cols)), NT)).astype(BF)

    add_dn(other)
    rows_copy.append(remote(dn.at[pl.ds(own_rows, own_rows)], o_dn_got, tsend.at[deep + wide + 1], trecv.at[deep + wide + 1], partner))
    rows_copy[1].start()

    def keep(at, values):
        for b in range(batch):
            mine[b // (2 * wide), (b // 2) % wide, b % 2, :, at] = values[2 * b * shard : 2 * (b + 1) * shard].astype(BF)

    loads["normed"].wait()
    keep(slice(0, 2 * cols), dot(normed[...], d_proj[:, : 2 * cols], TN))
    over_core(4)
    loads["o"].wait()
    loads["dy"].wait()
    for side, part in ((1, other), (0, own)):
        mixed[part, :] = compact_rows(s_o, bases[side]).astype(BF)
    over_y(0)
    keep(slice(2 * cols, 3 * cols), dot(normed[...], d_proj[:, 2 * cols : 3 * cols], TN))
    over_x(4)
    keep(slice(3 * cols, 4 * cols), dot(cotan[...], mixed[own, :], TN) + dot(dy_par[...], mixed[other, :], TN))
    over_core(5)
    add_dn(own)
    puts = [pltpu.make_async_copy(dn.at[pl.ds(0, own_rows)], o_dn, osem)]
    puts[0].start()
    over_x(5)
    over_y(1)
    loads["x"].wait()
    grad_g = jnp.zeros((1, width), F32)
    for side, part in ((tokens, own), (x_par, other)):
        vhat, _ = norm_stats(side[...].astype(F32))
        grad_g += jnp.sum(dn[part, :].astype(F32) * vhat, axis=0, keepdims=True)
    grad_db = jnp.sum(cotan[...].astype(F32), axis=0, keepdims=True)
    per = gb_ref.shape[1] // batch
    both = jnp.concatenate(gains, axis=1)
    bias = gb_ref[...]
    t_all[...] = jnp.zeros(t_all.shape, F32)
    for b, (zz, xx, cc, s) in enumerate(places):
        inside = jnp.where(y == b // batch, 1.0, 0.0)
        t_all[zz, xx, cc, s, 0:1, :shard] = grad_g[:, b * shard : (b + 1) * shard]
        t_all[zz, xx, cc, s, 1:2, :shard] = grad_db[:, b * shard : (b + 1) * shard]
        t_all[zz, xx, cc, s, 2:3, :per] = bias[:, (b % batch) * per : (b % batch + 1) * per] * inside
        t_all[zz, xx, cc, s, 3:4, : 2 * HD] = both
    tiny = [remote(t_all.at[:, :, 1 - core], t_core, tsend.at[0], trecv.at[0], sibling)]
    tiny[0].start()
    for name in ("own", "got"):
        loads[name].wait()
    rows_copy[0].wait_recv()
    mixed_got = compact_rows(o_got, 0).astype(BF)
    mixed_own = mixed[own, :]
    all_heads = jnp.concatenate([jnp.where(y == 0, mixed_own, mixed_got), jnp.where(y == 0, mixed_got, mixed_own)], axis=1)
    attended = dot(all_heads, head_weight(slice(3 * cols, 5 * cols)), NT)
    block_ref[...] = (tokens[...].astype(F32) + attended + out_own[...].astype(F32) + out_got[...].astype(F32) + bias_ref[...]).astype(BF)
    tiny[0].wait_recv()
    t_x[...] = t_all[:, :, core] + t_core[...]
    group = []
    for s, peer in enumerate(along_x):
        group.append(remote(t_x.at[:, (x + s + 1) % wide], t_xgot.at[x], tsend.at[1 + s], trecv.at[1 + s], peer))
        group[s].start()
    tiny += group
    t_xgot[x] = t_x[:, x]
    over_y(2)
    over_z(4)
    for copy in group:
        copy.wait_recv()
    total = t_xgot[0]
    for xx in range(1, wide):
        total += t_xgot[xx]
    t_z[...] = total
    group = []
    for s, peer in enumerate(along_z):
        group.append(remote(t_z.at[(z + s + 1) % deep], t_zgot.at[z], tsend.at[wide + s], trecv.at[wide + s], peer))
        group[s].start()
    tiny += group
    t_zgot[z] = t_z[z]
    over_y(3)
    over_z(5)
    for copy in group:
        copy.wait_recv()
    total = t_zgot[0]
    for zz in range(1, deep):
        total += t_zgot[zz]
    t_y[...] = total
    tiny.append(remote(t_y.at[1 - y], t_ygot, tsend.at[wide + deep - 1], trecv.at[wide + deep - 1], partner))
    tiny[-1].start()
    for i in range(4):
        last(i)
    over_y(4)
    tiny[-1].wait_recv()
    small_ref[...] = t_y[y] + t_ygot[...]
    over_y(5)
    last(4)
    last(5)
    puts[0].wait()
    rows_copy[1].wait_recv()
    for copy in list(first.values()) + [c for group in list(second.values()) + list(third.values()) for c in group] + list(fourth.values()) + tiny + rows_copy:
        copy.wait_send()


def last_half(tokens, cotan, bias, gb, gains, kept, sums, batch):
    deep, wide = grid_of(batch)
    own_rows, width = tokens.shape
    rows = 2 * own_rows
    hidden = gb.shape[1]
    cols = hidden // 4
    block = hidden // 2
    shard = width // (2 * batch)
    slots = own_rows // PATCHES
    cuts = [(part, slice(at, at + block)) for part in range(3) for at in (0, block)]
    vm = pl.BlockSpec(memory_space=pltpu.VMEM)
    hbm = pl.BlockSpec(memory_space=pl.ANY)
    buf = lambda *shape: pltpu.VMEM(shape, BF)
    tile = lambda *lead: pltpu.VMEM(lead + TINY, F32)
    scratch = [buf(*k.shape) for k in kept]
    scratch += [buf(wide, deep, 2 * shard, hidden)] * 2
    scratch += [buf(deep, wide, 2, 2 * shard, hidden), buf(deep, wide, 2 * shard, hidden), buf(wide - 1, deep, 2 * shard, hidden)]
    scratch += [buf(deep, 2 * shard, hidden)] * 3 + [buf(deep - 1, 2 * shard, hidden)] * 3 + [buf(shard, hidden)] * 6
    scratch += [buf(rows, 3 * cols), buf(rows, cols), buf(slots * SLOT, cols)]
    scratch += [tile(deep, wide, 2, 2), tile(deep, wide, 2), tile(deep, wide, 2), tile(wide, deep, 2), tile(deep, 2), tile(deep, 2), tile(2), tile()]
    scratch += [pltpu.SemaphoreType.DMA((len(cuts), deep + wide))] * 2 + [pltpu.SemaphoreType.DMA((deep + wide + 2,))] * 2 + [pltpu.SemaphoreType.DMA((len(kept),)), pltpu.SemaphoreType.DMA((2 * wide,)), pltpu.SemaphoreType.DMA]
    full = lambda *shape: jax.ShapeDtypeStruct(shape, F32)
    low = jax.ShapeDtypeStruct((own_rows, width), BF)
    return pl.pallas_call(
        functools.partial(last_kernel, deep=deep, wide=wide, cuts=cuts),
        in_specs=[vm] * 5 + [hbm] * (len(kept) + 2 * wide),
        out_specs=[hbm] * 2 + [vm] * 6,
        out_shape=[low] * 3 + [full(3, shard, 2 * cols), full(shard, 2 * cols), full(shard, 2 * hidden), full(shard, 2 * hidden), full(*TINY)],
        scratch_shapes=scratch,
        compiler_params=pltpu.CompilerParams(collective_id=1, has_side_effects=True, vmem_limit_bytes=VMEM_CAP),
        name="head_gradients_and_scatter",
    )(tokens, cotan, bias, gb, gains, *kept, *sums)


def result_kernel(tokens, cotan, gain, dn_own, dn_got, block_in, qkv_in, wo_in, up_in, down_in, small, block, grad, qkv, wo, up, down, up_b, down_b, norm_g, query_g, key_g):
    vhat, scale = norm_stats(tokens[...].astype(F32))
    scaled = (dn_own[...].astype(F32) + dn_got[...].astype(F32)) * gain[...]
    d_tokens = (scaled - jnp.mean(scaled, axis=-1, keepdims=True) - vhat * jnp.mean(scaled * vhat, axis=-1, keepdims=True)) * scale
    grad[...] = (cotan[...].astype(F32) + d_tokens).astype(BF)
    block[...] = block_in[...]

    @pl.when(pl.program_id(0) == 0)
    def _():
        qkv[...] = qkv_in[...]
        wo[...] = wo_in[...]
        up[...] = up_in[...]
        down[...] = down_in[...]
        norm_g[...] = small[0:1, : norm_g.shape[1]]
        down_b[...] = small[1:2, : down_b.shape[1]]
        up_b[...] = small[2:3, : up_b.shape[1]]
        query_g[...] = small[3:4, :HD]
        key_g[...] = small[3:4, HD : 2 * HD]


def results(tokens, cotan, gain, dn_own, dn_got, block_in, sums, small, per):
    rows, width = tokens.shape
    chunk = rows // 2
    shard = sums[1].shape[0]
    blk = pl.BlockSpec((chunk, width), lambda j: (j, 0))
    whole = lambda shape: pl.BlockSpec(shape, lambda j: (0,) * len(shape))
    vectors = [(1, per), (1, shard), (1, shard), (1, HD), (1, HD)]
    return pl.pallas_call(
        result_kernel,
        grid=(rows // chunk,),
        in_specs=[blk, blk, whole(gain.shape), blk, blk, blk] + [whole(s.shape) for s in sums] + [whole(small.shape)],
        out_specs=[blk, blk] + [whole(s.shape) for s in sums] + [whole(v) for v in vectors],
        out_shape=[jax.ShapeDtypeStruct((rows, width), BF)] * 2 + [jax.ShapeDtypeStruct(s.shape, F32) for s in sums] + [jax.ShapeDtypeStruct(v, F32) for v in vectors],
        compiler_params=pltpu.CompilerParams(vmem_limit_bytes=VMEM_CAP),
        name="results",
    )(tokens, cotan, gain, dn_own, dn_got, block_in, *sums, small)


def local(tokens, cotangent, image_tokens, w_qkv, w_out, w_up, bias_up, w_down, bias_down, norm_gain, query_gain, key_gain):
    batch = lax.axis_size("batch")
    deep, wide = grid_of(batch)
    row = lambda v: v.reshape(1, -1)
    weights = (w_qkv, w_out.T, w_up, w_down.T)
    vectors = (row(norm_gain), row(bias_down), row(bias_up), row(query_gain), row(key_gain))
    made = first_half(tokens, cotangent, weights, vectors, batch)
    x_par, dy_par, normed, q, k, v, d_o, qraw, kraw, head_w, out_own, out_other, dn = made[:13]
    up_sums, down_sums = made[13 : 13 + wide], made[13 + wide : 13 + 2 * wide]
    gb, gain, bias, gains = made[13 + 2 * wide :]
    at = lambda z, x, c: (z * wide + x) * 2 + c

    def over_x(terms):
        return [terms[0]] + [lax.ppermute(terms[s], "batch", [(at(z, x, c), at(z, (x + s) % wide, c)) for z in range(deep) for x in range(wide) for c in range(2)]) for s in range(1, wide)]

    up_sums = over_x(up_sums)
    out_got = lax.ppermute(out_other, "branch", [(0, 1), (1, 0)])
    down_sums = over_x(down_sums)
    o, dq, dk, dv = attention(image_tokens[0], q, k, v, d_o)
    kept = [x_par, dy_par, normed, o, dq, dk, dv, qraw, kraw, head_w, out_own, out_got, dn]
    dn_own, dn_got, block_in, g_qkv, g_out, g_up, g_down, small = last_half(tokens, cotangent, bias, gb, gains, kept, up_sums + down_sums, batch)
    block_out, grad_tokens, g_qkv, g_out, g_up, g_down, g_up_b, g_down_b, g_norm, g_query, g_key = results(tokens, cotangent, gain, dn_own, dn_got, block_in, [g_qkv, g_out, g_up, g_down], small, bias_up.shape[0])
    flat = lambda v: v.reshape(-1)
    return (block_out, grad_tokens, g_qkv, g_out.T, g_up, flat(g_up_b), g_down.T, flat(g_down_b), flat(g_norm), flat(g_query), flat(g_key))


def solution(mesh):
    both = ("batch", "branch")
    in_specs = (P(both, None), P(both, None), P("batch", None), P(None, both, None), P(None, both), P(both, None), P(both), P(None, both), P(both), P(both), P(), P())
    out_specs = (P(both, None), P(both, None), P(None, both, None), P(None, both), P(both, None), P(both), P(None, both), P(both), P(both), P(), P())
    return jax.shard_map(local, mesh=mesh, in_specs=in_specs, out_specs=out_specs, check_vma=False)
```

```python
import functools
import jax
import jax.numpy as jnp
from jax import lax
from jax.experimental import pallas as pl
from jax.experimental.pallas import tpu as pltpu
from jax.sharding import PartitionSpec as P

HD = 64
LANES = 128
NORM_EPS = 1e-06
LONGEST = 784
PATCHES = 196
SLOT = 208
VMEM_CAP = 66_000_000
BF = jnp.bfloat16
F32 = jnp.float32


def dot(a, b, dims=((1,), (0,))):
    return lax.dot_general(a, b, (dims, ((), ())), preferred_element_type=F32)


NT = ((1,), (1,))
TN = ((0,), (0,))


def norm_stats(values):
    centred = values - jnp.mean(values, axis=-1, keepdims=True)
    spread = jnp.mean(centred * centred, axis=-1, keepdims=True)
    scale = lax.rsqrt(spread + NORM_EPS)
    return centred * scale, scale


def head_means(values, ones_low):
    means = []
    for at in range(0, values.shape[1], LANES):
        some = values[:, at : at + LANES]
        high = some.astype(BF)
        low = (some - high.astype(F32)).astype(BF)
        means.append(dot(jnp.concatenate([high, low], axis=1), ones_low))
    return jnp.concatenate(means, axis=1)


def head_ones():
    row = lax.broadcasted_iota(jnp.int32, (2 * LANES, LANES), 0) % LANES // HD
    col = lax.broadcasted_iota(jnp.int32, (2 * LANES, LANES), 1) // HD
    return jnp.where(row == col, 1.0 / HD, 0.0).astype(BF)


def head_stats(raw, ones_low):
    centred = raw - head_means(raw, ones_low)
    scale = lax.rsqrt(head_means(centred * centred, ones_low) + NORM_EPS)
    return centred * scale, scale


MESH = pl.DeviceIdType.MESH


def place():
    return lax.axis_index("batch"), lax.axis_index("branch")


def grid_of(batch):
    chips = batch // 2
    across = 1
    while across * across * 4 <= chips:
        across *= 2
    return chips // across, across


def greet(peers):
    barrier = pltpu.get_barrier_semaphore()
    for peer in peers:
        pl.semaphore_signal(barrier, inc=1, device_id=peer, device_id_type=MESH)
    pl.semaphore_wait(barrier, len(peers))


def neighbours(deep, wide):
    batch, branch = place()
    core, x, z = batch % 2, (batch // 2) % wide, batch // (2 * wide)
    at = lambda zz, xx, cc: (zz * wide + xx) * 2 + cc
    partner = (batch, 1 - branch)
    along_z = [(at((z + s) % deep, x, core), branch) for s in range(1, deep)]
    along_x = [(at(z, (x + s) % wide, core), branch) for s in range(1, wide)]
    sibling = (at(z, x, 1 - core), branch)
    return (z, x, core, branch), partner, along_z, along_x, sibling


def remote(src, dst, send, recv, peer):
    return pltpu.make_async_remote_copy(src_ref=src, dst_ref=dst, send_sem=send, recv_sem=recv, device_id=peer, device_id_type=MESH)


TINY = (8, LANES)
STRIP = 112


def gelu_parts(hidden):
    square = hidden * hidden
    tanh = jnp.tanh(hidden * (0.7978845608028654 + 0.035677408136300125 * square))
    half = 0.5 + 0.5 * tanh
    act = hidden * half
    slope = half + (act * (1.0 - tanh)) * (0.7978845608028654 + 0.1070322244089 * square)
    return act.astype(BF), slope


def repeated(values, count):
    return jnp.concatenate([values] * count, axis=1)


def first_kernel(*refs, deep, wide, cuts, block):
    tokens, cotan, qkv_ref, wo_ref, up_ref, down_ref, nb_ref, db_ref, ub_ref, qg_ref, kg_ref = refs[:11]
    o_x, o_dy, o_normed, o_q, o_k, o_v, o_do, o_qraw, o_kraw, o_heads, o_own, o_other, o_dn = refs[11:24]
    o_sums = (refs[24 : 24 + wide], refs[24 + wide : 24 + 2 * wide])
    gb_ref, gain_ref, bias_ref, tiny = refs[24 + 2 * wide : 28 + 2 * wide]
    scratch = refs[28 + 2 * wide :]
    packs, lands, wires = scratch[:3], scratch[3:6], scratch[6:9]
    rounded, tiny_all, x_par, dy_par, normed, act, d_hid, s_q, s_k, s_v, s_do, s_qraw, s_kraw, s_out, s_dn = scratch[9:24]
    grads, got_core, flats = scratch[24:26], scratch[26:28], scratch[28:31]
    send, recv, tsend, trecv, csend, crecv, osem = scratch[31:]
    (z, x, core, y), partner, along_z, along_x, sibling = neighbours(deep, wide)
    batch = 2 * deep * wide
    own_rows, width = tokens.shape
    shard, hidden = packs[0].shape[1:]
    cols = hidden // 4
    pair = 2 * shard
    direct = pair % 16 == 0
    places = [(b // (2 * wide), (b // 2) % wide, b % 2, s) for b in range(batch) for s in range(2)]

    for half in range(2):
        some = slice(half * cols, (half + 1) * cols)
        packs[0][half] = up_ref[:, half * hidden : (half + 1) * hidden].astype(BF)
        packs[1][half] = down_ref[:, half * hidden : (half + 1) * hidden].astype(BF)
        for at in range(3):
            packs[2][half, :, at * cols : (at + 1) * cols] = qkv_ref[at, :, some].astype(BF)
        packs[2][half, :, 3 * cols :] = wo_ref[...].astype(BF)
    rounded[...] = jnp.zeros(TINY, BF)
    for row, ref in enumerate((nb_ref, db_ref, ub_ref, qg_ref, kg_ref)):
        rounded[row : row + 1, : ref.shape[1]] = ref[...].astype(BF)
    tiny[...] = rounded[...].astype(F32)
    tiny_all[z, x, core, y] = tiny[...]
    greet([partner, sibling] + along_z + along_x)
    outs = []

    def put(src, dst):
        copy = pltpu.make_async_copy(src, dst, osem.at[len(outs)])
        copy.start()
        outs.append(copy)

    spread_tiny = [remote(tiny, tiny_all.at[z, x, core, y], tsend.at[0], trecv.at[0], partner)]
    spread_tiny[0].start()
    over_y = []
    for i, (part, at) in enumerate(cuts):
        over_y.append(remote(packs[part].at[1 - y, :, at], lands[part].at[:, at], send.at[i, 0], recv.at[i, 0], partner))
        over_y[i].start()
    rows_copy = [remote(tokens, x_par, tsend.at[deep + wide], trecv.at[deep + wide], partner), remote(cotan, dy_par, tsend.at[deep + wide + 1], trecv.at[deep + wide + 1], partner)]
    for copy in rows_copy:
        copy.start()

    def tiny_stage(block, peers, first):
        group = [remote(block, block, tsend.at[first + s], trecv.at[first + s], peer) for s, peer in enumerate(peers)]
        for copy in group:
            copy.start()
        for copy in group:
            copy.wait_recv()
        spread_tiny.extend(group)

    over_z, over_x, over_core = [], [], []

    def start_z(i):
        part, at = cuts[i]
        over_y[i].wait_recv()
        mine, other = packs[part][y, :, at].astype(F32), lands[part][:, at].astype(F32)
        pair = jnp.concatenate([jnp.where(y == 0, mine, other), jnp.where(y == 0, other, mine)], axis=0)
        wires[part][z, x, core, :, at] = pair.astype(BF)
        block = wires[part].at[z, x, core, :, at]
        over_z.append([remote(block, block, send.at[i, 1 + s], recv.at[i, 1 + s], peer) for s, peer in enumerate(along_z)])
        for copy in over_z[i]:
            copy.start()

    def start_x(i):
        part, at = cuts[i]
        for copy in over_z[i]:
            copy.wait_recv()
        block = wires[part].at[:, x, core, :, at]
        over_x.append([remote(block, block, send.at[i, deep + s], recv.at[i, deep + s], peer) for s, peer in enumerate(along_x)])
        for copy in over_x[i]:
            copy.start()

    def start_core(i):
        part, at = cuts[i]
        for copy in over_x[i]:
            copy.wait_recv()
        block = wires[part].at[:, :, core, :, at]
        over_core.append(remote(block, block, send.at[i, deep + wide - 1], recv.at[i, deep + wide - 1], sibling))
        over_core[i].start()

    def arrive(i):
        part, at = cuts[i]
        over_core[i].wait_recv()
        if not direct:
            for b in range(batch):
                flats[part][2 * shard * b : 2 * shard * (b + 1), at] = wires[part][b // (2 * wide), (b // 2) % wide, b % 2, :, at]

    def weight(part, at):
        if direct:
            value = wires[part][:, :, :, :, at]
            return value.reshape(width, value.shape[-1])
        return flats[part][:, at]

    for i in range(len(cuts)):
        start_z(i)
        if i == 0:
            spread_tiny[0].wait_recv()
            tiny_stage(tiny_all.at[z, x, core], along_z, 1)
        if i == 1:
            tiny_stage(tiny_all.at[:, x, core], along_x, deep)
        if i == 2:
            tiny_stage(tiny_all.at[:, :, core], [sibling], deep + wide - 1)
    per = ub_ref.shape[1]
    gain_ref[...] = jnp.concatenate([tiny_all[p][0:1, :shard] for p in places], axis=1)
    bias_ref[...] = jnp.concatenate([tiny_all[p][1:2, :shard] for p in places], axis=1)
    low_b = jnp.concatenate([tiny_all[p][2:3, :per] for p in places[:batch]], axis=1)
    high_b = jnp.concatenate([tiny_all[p][2:3, :per] for p in places[batch:]], axis=1)
    gb_ref[...] = jnp.where(y == 0, low_b, high_b)

    sides = ((tokens, cotan, slice(0, own_rows)), (x_par, dy_par, slice(own_rows, 2 * own_rows)))

    def normalise(side):
        @pl.loop(0, own_rows // STRIP)
        def _(turn):
            strip = pl.ds(pl.multiple_of(turn * STRIP, 16), STRIP)
            vhat, _ = norm_stats(sides[side][0][strip, :].astype(F32))
            normed[pl.ds(pl.multiple_of(side * own_rows + turn * STRIP, 16), STRIP), :] = (vhat * gain_ref[...]).astype(BF)

    def expand(side, at, back):
        rows = sides[side][2]

        turns = 3 if back else 6

        @pl.loop(0, turns)
        def _(turn):
            size = (at.stop - at.start) // turns
            some = pl.ds(pl.multiple_of(at.start + turn * size, LANES), size)
            act[rows, some], slope = gelu_parts(dot(normed[rows, :], weight(0, some)) + gb_ref[:, some])
            if back:
                slope *= dot(sides[side][1][...], weight(1, some))
            d_hid[rows, some] = slope.astype(BF)

    def apply_back(side):
        rows = sides[side][2]

        @pl.loop(0, 2)
        def _(turn):
            at = pl.ds(pl.multiple_of(turn * block, LANES), block)
            d_hid[rows, at] = (d_hid[rows, at].astype(F32) * dot(sides[side][1][...], weight(1, at))).astype(BF)

    def contract(side, low, kept, part):
        rows = sides[side][2]
        size = width // 2

        @pl.loop(0, 2)
        def _(turn):
            if direct:
                value = wires[part][pl.ds(turn * (deep // 2), deep // 2)].reshape(size, hidden)
            else:
                value = flats[part][pl.ds(pl.multiple_of(turn * size, 16), size), :]
            kept[rows, pl.ds(pl.multiple_of(turn * size, LANES), size)] = dot(low[rows, :], value, NT).astype(BF)

    def place_rows(base, ref, values):
        for at in range(own_rows // PATCHES):
            ref[pl.ds(pl.multiple_of((base + at) * SLOT, 16), PATCHES), :] = values[at * PATCHES : (at + 1) * PATCHES].astype(BF)

    def queries_keys():
        ones_low = head_ones()

        @pl.loop(0, 2)
        def _(side):
            rows = pl.ds(pl.multiple_of(side * own_rows, 16), own_rows)
            base = jnp.where(side == 0, y, 1 - y) * (own_rows // PATCHES)
            for at, (raw_ref, low_ref, gain) in enumerate(((s_qraw, s_q, 3), (s_kraw, s_k, 4))):
                raw = dot(normed[rows, :], weight(2, slice(at * cols, (at + 1) * cols)))
                raw_ref[rows, :] = raw.astype(BF)
                hat, _ = head_stats(raw, ones_low)
                place_rows(base, low_ref, hat * repeated(tiny[gain : gain + 1, :HD], cols // HD))

    def values_of():
        @pl.loop(0, 2)
        def _(side):
            rows = pl.ds(pl.multiple_of(side * own_rows, 16), own_rows)
            place_rows(jnp.where(side == 0, y, 1 - y) * (own_rows // PATCHES), s_v, dot(normed[rows, :], weight(2, slice(2 * cols, 3 * cols))))

    def back_of(side):
        place_rows((y if side == 0 else 1 - y) * (own_rows // PATCHES), s_do, dot(sides[side][1][...], weight(2, pl.ds(pl.multiple_of((3 + y) * cols, LANES), cols))))

    over_sib = []

    def grad_own(part, at):
        rows = sides[0][2]

        @pl.loop(0, 3)
        def _(turn):
            size = (at.stop - at.start) // 3
            some = pl.ds(pl.multiple_of(at.start + turn * size, LANES), size)
            value = dot(normed[rows, :], d_hid[rows, some], TN) if part == 0 else dot(cotan[...], act[rows, some], TN)
            for b in range(batch):
                grads[part][b // (2 * wide), (b // 2) % wide, b % 2, :, some] = value[b * pair : (b + 1) * pair].astype(BF)

    def grad_rest(part, at):
        rows = sides[1][2]

        @pl.loop(0, 2)
        def _(turn):
            size = (at.stop - at.start) // 2
            some = pl.ds(pl.multiple_of(at.start + turn * size, LANES), size)
            value = dot(normed[rows, :], d_hid[rows, some], TN) if part == 0 else dot(dy_par[...], act[rows, some], TN)
            for b in range(batch):
                block_at = (b // (2 * wide), (b // 2) % wide, b % 2, slice(None), some)
                grads[part][block_at] = (grads[part][block_at].astype(F32) + value[b * pair : (b + 1) * pair]).astype(BF)

        i = len(over_sib)
        over_sib.append(remote(grads[part].at[:, :, 1 - core, :, at], got_core[part].at[:, :, :, at], csend.at[i], crecv.at[i], sibling))
        over_sib[i].start()

    def add_core(i, part, at):
        over_sib[i].wait_recv()

        @pl.loop(0, deep)
        def _(zz):
            for xx in range(wide):
                total = grads[part][zz, xx, core, :, at].astype(F32) + got_core[part][zz, xx, :, at].astype(F32)
                got_core[part][zz, xx, :, at] = total.astype(BF)

    first, second = slice(0, block), slice(block, 2 * block)
    start_x(0)
    normalise(0)
    start_x(1)
    start_core(0)
    start_x(2)
    start_core(1)
    arrive(0)
    arrive(1)
    expand(0, first, True)
    start_x(3)
    start_core(2)
    rows_copy[0].wait_recv()
    normalise(1)
    put(x_par, o_x)
    put(normed, o_normed)
    expand(1, first, False)
    start_x(4)
    grad_own(0, first)
    start_core(3)
    grad_own(1, first)
    arrive(2)
    arrive(3)
    expand(0, second, True)
    start_core(4)
    expand(1, second, False)
    start_x(5)
    contract(0, act, s_out, 1)
    contract(0, d_hid, s_dn, 0)
    grad_own(0, second)
    grad_own(1, second)
    contract(1, act, s_out, 1)
    put(s_out.at[pl.ds(0, own_rows)], o_own)
    put(s_out.at[pl.ds(own_rows, own_rows)], o_other)
    arrive(4)
    start_core(5)
    queries_keys()
    for src, dst in ((s_q, o_q), (s_k, o_k), (s_qraw, o_qraw), (s_kraw, o_kraw)):
        put(src, dst)
    arrive(5)
    put(wires[2] if direct else flats[2], o_heads)
    values_of()
    put(s_v, o_v)
    back_of(0)
    rows_copy[1].wait_recv()
    put(dy_par, o_dy)
    back_of(1)
    put(s_do, o_do)
    apply_back(1)
    contract(1, d_hid, s_dn, 0)
    put(s_dn, o_dn)
    grad_rest(0, first)
    grad_rest(0, second)
    add_core(0, 0, first)
    grad_rest(1, first)
    add_core(1, 0, second)
    for s in range(wide):
        put(got_core[0].at[:, (x + s) % wide], o_sums[0][s])
    grad_rest(1, second)
    add_core(2, 1, first)

    @pl.loop(0, 6)
    def _(turn):
        some = pl.ds(pl.multiple_of(turn * (hidden // 6), LANES), hidden // 6)
        gb_ref[:, some] = dot(jnp.ones((8, 2 * own_rows), BF), d_hid[:, some])[:1]

    add_core(3, 1, second)
    for s in range(wide):
        put(got_core[1].at[:, (x + s) % wide], o_sums[1][s])
    for copy in outs:
        copy.wait()
    for copy in spread_tiny + over_y + rows_copy + [c for group in over_z + over_x for c in group] + over_core + over_sib:
        copy.wait_send()


def first_half(tokens, cotan, weights, vectors, batch):
    deep, wide = grid_of(batch)
    own_rows, width = tokens.shape
    shard, hidden = weights[2].shape[0], weights[2].shape[1] // 2
    cols = hidden // 4
    block = hidden // 2
    rows = 2 * own_rows
    spread_rows = rows // PATCHES * SLOT
    widths = (hidden, hidden, 5 * cols)
    first, second = slice(0, block), slice(block, hidden)
    cuts = [(0, first), (1, first), (0, second), (1, second), (2, slice(0, 2 * cols)), (2, slice(2 * cols, 5 * cols))]
    vm = pl.BlockSpec(memory_space=pltpu.VMEM)
    hbm = pl.BlockSpec(memory_space=pl.ANY)
    direct = (2 * shard) % 16 == 0
    wire_shapes = [(deep, wide, 2, 2 * shard, w) for w in widths]
    flat_shapes = [(width, w) for w in widths]
    low = lambda *shape: jax.ShapeDtypeStruct(shape, BF)
    outs = [low(own_rows, width)] * 2 + [low(rows, width)] + [low(spread_rows, cols)] * 4 + [low(rows, cols)] * 2
    outs += [low(*(wire_shapes if direct else flat_shapes)[2])] + [low(own_rows, width)] * 2 + [low(rows, width)] + [low(deep, 2 * shard, hidden)] * (2 * wide)
    tiny_outs = [jax.ShapeDtypeStruct((1, hidden), F32), jax.ShapeDtypeStruct((1, width), F32), jax.ShapeDtypeStruct((1, width), F32), jax.ShapeDtypeStruct(TINY, F32)]
    buf = lambda *shape: pltpu.VMEM(shape, BF)
    scratch = [buf(2, shard, w) for w in widths] + [buf(shard, w) for w in widths] + [buf(*s) for s in wire_shapes]
    scratch += [buf(*TINY), pltpu.VMEM((deep, wide, 2, 2) + TINY, F32), buf(own_rows, width), buf(own_rows, width), buf(rows, width), buf(rows, hidden), buf(rows, hidden)]
    scratch += [buf(spread_rows, cols)] * 4 + [buf(rows, cols)] * 2 + [buf(rows, width)] * 2
    scratch += [buf(deep, wide, 2, 2 * shard, hidden)] * 2 + [buf(deep, wide, 2 * shard, hidden)] * 2
    scratch += [buf(16, LANES) if direct else buf(*s) for s in flat_shapes]
    scratch += [pltpu.SemaphoreType.DMA((len(cuts), deep + wide))] * 2 + [pltpu.SemaphoreType.DMA((deep + wide + 2,))] * 2 + [pltpu.SemaphoreType.DMA((4,))] * 2 + [pltpu.SemaphoreType.DMA((len(outs),))]
    return pl.pallas_call(
        functools.partial(first_kernel, deep=deep, wide=wide, cuts=cuts, block=block),
        in_specs=[vm] * 11,
        out_specs=[hbm] * len(outs) + [vm] * 4,
        out_shape=outs + tiny_outs,
        scratch_shapes=scratch,
        compiler_params=pltpu.CompilerParams(collective_id=0, has_side_effects=True, vmem_limit_bytes=VMEM_CAP),
        name="gather_and_feed_forward",
    )(tokens, cotan, *weights, *vectors)


def load_rows(ref, block, blocks):
    parts = [ref[pl.ds(pl.multiple_of((block + at) * SLOT, 16), PATCHES), :] for at in range(blocks)]
    return parts[0] if blocks == 1 else jnp.concatenate([p.astype(F32) for p in parts], axis=0).astype(BF)

def attend_pair(pair_q, pair_k, pair_v, pair_do, pieces):
    count = pair_q.shape[0]
    lane = lax.broadcasted_iota(jnp.int32, (count, 2 * HD), 1)
    pair_q = pair_q * jnp.asarray(0.125, BF)
    zero = jnp.zeros_like(pair_q)
    v_t, k_t = pair_v.T, pair_k.T
    mixed, grads_q, grad_k, grad_v = [], [], None, None
    for head in range(2):
        mine = (lane < HD) if head == 0 else (lane >= HD)
        q_m, do_m = jnp.where(mine, pair_q, zero), jnp.where(mine, pair_do, zero)
        part = slice(head * HD, (head + 1) * HD)
        outs, gqs = [], []
        for first, size in pieces:
            q, d_o = q_m[first : first + size], do_m[first : first + size]
            shifted = jnp.exp(dot(pair_k, q, NT))
            total = jnp.sum(shifted, axis=0, keepdims=True)
            weights = shifted * (1.0 / total)
            low = weights.astype(BF)
            d_weights = dot(pair_v, d_o, NT)
            inner = jnp.sum(weights * d_weights, axis=0, keepdims=True)
            d_scores = (weights * (d_weights - inner)).astype(BF)
            outs.append(dot(v_t[part], low))
            gqs.append(dot(k_t[part], d_scores))
            gv, gk = dot(low, d_o), dot(d_scores, q)
            grad_v = gv if grad_v is None else grad_v + gv
            grad_k = gk if grad_k is None else grad_k + gk
        join = lambda parts: parts[0] if len(parts) == 1 else jnp.concatenate(parts, axis=1)
        mixed.append(join(outs))
        grads_q.append(join(gqs))
    turn = lambda parts: jnp.concatenate(parts, axis=0).T
    return turn(mixed), turn(grads_q) * 0.125, grad_k, grad_v

def attention_kernel(count_ref, *refs, pieces, together):
    ins, outs, (small_ref,) = refs[:4], refs[4:8], refs[8:]
    place, smalls, bigs, big_at = 0, 0, 0, 0
    for slot in range(count_ref.shape[0]):
        count = count_ref[slot]
        is_small = (count == PATCHES).astype(jnp.int32)
        is_big = (count == LONGEST).astype(jnp.int32)
        small_ref[smalls] = place
        big_at = jnp.where(is_big == 1, place, big_at)
        smalls, bigs = smalls + is_small, bigs + is_big
        place = place + is_small + (LONGEST // PATCHES) * is_big

    def images(firsts, blocks, pieces):
        loaded = [[load_rows(ref, block, blocks) for ref in ins] for block in firsts]
        results = [attend_pair(*values, pieces) for values in loaded]
        for block, result in zip(firsts, results):
            for ref, values in zip(outs, result):
                for at in range(blocks):
                    ref[pl.ds(pl.multiple_of((block + at) * SLOT, 16), PATCHES), :] = values[at * PATCHES : (at + 1) * PATCHES].astype(ref.dtype)

    @pl.when(bigs > 0)
    def _():
        images([big_at], LONGEST // PATCHES, pieces)

    @pl.loop(0, smalls // together)
    def _(turn):
        images([small_ref[turn * together + at] for at in range(together)], 1, ((0, PATCHES),))

def attention(counts, q, k, v, d_o, pieces=((0, 784),), together=4):
    rows, cols = q.shape
    sm = pl.BlockSpec(memory_space=pltpu.SMEM)
    blk = pl.BlockSpec((rows, 2 * HD), lambda j: (0, j))
    return pl.pallas_call(
        functools.partial(attention_kernel, pieces=pieces, together=together),
        grid=(cols // (2 * HD),),
        in_specs=[sm] + [blk] * 4,
        out_specs=[blk] * 4,
        out_shape=[jax.ShapeDtypeStruct((rows, cols), t) for t in (BF, BF, BF, BF)],
        scratch_shapes=[pltpu.SMEM((counts.shape[0] + 1,), jnp.int32)],
        compiler_params=pltpu.CompilerParams(vmem_limit_bytes=VMEM_CAP),
        cost_estimate=pl.CostEstimate(flops=20_000_000_000, bytes_accessed=20_000_000, transcendentals=rows * LONGEST * cols // HD),
        name="attention",
    )(counts, q, k, v, d_o)


def last_kernel(*refs, deep, wide, cuts):
    tokens, cotan, bias_ref, gb_ref, gains_ref = refs[:5]
    i_x, i_dy, i_normed, i_o, i_dq, i_dk, i_dv, i_qraw, i_kraw, i_heads, i_own, i_got, i_dn = refs[5:18]
    i_sums = (refs[18 : 18 + wide], refs[18 + wide : 18 + 2 * wide])
    o_dn, o_dn_got, block_ref, qkv_ref, wo_ref, up_ref, down_ref, small_ref = refs[18 + 2 * wide : 26 + 2 * wide]
    scratch = refs[26 + 2 * wide :]
    x_par, dy_par, normed, s_o, s_dq, s_dk, s_dv, qraw, kraw, head_w, out_own, out_got, dn = scratch[:13]
    terms = scratch[13:15]
    mine, got_core, got_x = scratch[15:18]
    to_z, got_z, to_y, got_y = (scratch[18 + 3 * i : 21 + 3 * i] for i in range(4))
    d_proj, mixed, o_got = scratch[30:33]
    t_all, t_core, t_x, t_xgot, t_z, t_zgot, t_y, t_ygot = scratch[33:41]
    send, recv, tsend, trecv, lsem, gsem, osem = scratch[41:]
    (z, x, core, y), partner, along_z, along_x, sibling = neighbours(deep, wide)
    batch = 2 * deep * wide
    own_rows, width = tokens.shape
    rows = 2 * own_rows
    cols = qraw.shape[1]
    shard = to_y[0].shape[0]
    slots = own_rows // PATCHES
    places = [(b // (2 * wide), (b // 2) % wide, b % 2, s) for b in range(batch) for s in range(2)]
    own, other = slice(0, own_rows), slice(own_rows, rows)
    greet([partner, sibling] + along_z + along_x)

    theirs = pl.ds(pl.multiple_of((1 - y) * slots * SLOT, 16), slots * SLOT)
    rows_copy = [remote(i_o.at[theirs], o_got, tsend.at[deep + wide], trecv.at[deep + wide], partner)]
    rows_copy[0].start()
    held = {}
    for part in range(2):
        for s in range(wide):
            held[part, s] = pltpu.make_async_copy(i_sums[part][s], terms[part].at[s], gsem.at[part * wide + s])
            held[part, s].start()
    loads = {}
    for at, (name, src, dst) in enumerate((("qraw", i_qraw, qraw), ("dq", i_dq, s_dq), ("kraw", i_kraw, kraw), ("dk", i_dk, s_dk), ("dv", i_dv, s_dv), ("heads", i_heads, head_w), ("dn", i_dn, dn), ("normed", i_normed, normed), ("o", i_o, s_o), ("dy", i_dy, dy_par), ("x", i_x, x_par), ("own", i_own, out_own), ("got", i_got, out_got))):
        loads[name] = pltpu.make_async_copy(src, dst, lsem.at[at])
        loads[name].start()

    first, second, third, fourth = {}, {}, {}, {}

    def over_core(i):
        part, at = cuts[i]
        first[i] = remote(mine.at[:, :, 1 - core, :, at], got_core.at[:, :, :, at], send.at[i, 0], recv.at[i, 0], sibling)
        first[i].start()

    def over_x(i):
        part, at = cuts[i]
        first[i].wait_recv()

        @pl.loop(0, deep)
        def _(zz):
            for xx in range(wide):
                got_core[zz, xx, :, at] = (mine[zz, xx, core, :, at].astype(F32) + got_core[zz, xx, :, at].astype(F32)).astype(BF)

        second[i] = []
        for s, peer in enumerate(along_x):
            copy = remote(got_core.at[:, (x + s + 1) % wide, :, at], got_x.at[s, :, :, at], send.at[i, 1 + s], recv.at[i, 1 + s], peer)
            copy.start()
            second[i].append(copy)

    def over_z(i):
        part, at = cuts[i]
        if part == 2:
            for copy in second[i]:
                copy.wait_recv()

        @pl.loop(0, deep)
        def _(zz):
            if part == 2:
                total = got_core[zz, x, :, at].astype(F32)
                for s in range(wide - 1):
                    total += got_x[s, zz, :, at].astype(F32)
            else:
                total = terms[part][0, zz, :, at].astype(F32)
                for s in range(1, wide):
                    total += terms[part][s, zz, :, at].astype(F32)
            to_z[part][zz, :, at] = total.astype(BF)

        third[i] = []
        for s, peer in enumerate(along_z):
            copy = remote(to_z[part].at[(z + s + 1) % deep, :, at], got_z[part].at[s, :, at], send.at[i, wide + s], recv.at[i, wide + s], peer)
            copy.start()
            third[i].append(copy)

    def over_y(i):
        part, at = cuts[i]
        for copy in third[i]:
            copy.wait_recv()
        total = to_z[part][z, :, at].astype(F32)
        for s in range(deep - 1):
            total += got_z[part][s, :, at].astype(F32)
        low, high = total[:shard], total[shard:]
        to_y[part][:, at] = jnp.where(y == 0, high, low).astype(BF)
        fourth[i] = remote(to_y[part].at[:, at], got_y[part].at[:, at], send.at[i, wide + deep - 1], recv.at[i, wide + deep - 1], partner)
        fourth[i].start()
        deliver(part, y, at, jnp.where(y == 0, low, high))

    def deliver(part, half, at, values):
        if part < 2:
            ref = (up_ref, down_ref)[part]
            ref[:, pl.ds(pl.multiple_of(half * 4 * cols + at.start, LANES), at.stop - at.start)] = values
            return
        for piece in range(at.start // cols, at.stop // cols):
            some = values[:, piece * cols - at.start : (piece + 1) * cols - at.start]
            lanes = pl.ds(pl.multiple_of(half * cols, LANES), cols)
            if piece < 3:
                qkv_ref[piece, :, lanes] = some
            else:
                wo_ref[:, lanes] = some

    def last(i):
        part, at = cuts[i]
        fourth[i].wait_recv()
        deliver(part, 1 - y, at, got_y[part][:, at].astype(F32))

    def compact_rows(ref, base):
        parts = [ref[pl.ds(pl.multiple_of((base + at) * SLOT, 16), PATCHES), :].astype(F32) for at in range(slots)]
        return jnp.concatenate(parts, axis=0)

    bases = (y * slots, (1 - y) * slots)

    def head_rows(turn, at):
        if len(head_w.shape) > 2:
            value = head_w[pl.ds(turn * (deep // 2), deep // 2), :, :, :, at]
            return value.reshape(width // 2, value.shape[-1])
        return head_w[pl.ds(pl.multiple_of(turn * (width // 2), 16), width // 2), at]

    for part in range(2):
        for s in range(wide):
            held[part, s].wait()
    for i in range(4):
        over_z(i)
    ones_low = head_ones()
    gains = []
    for names, grad_in, raw_ref, gain, at in ((("dq", "qraw"), s_dq, qraw, 3, 0), (("dk", "kraw"), s_dk, kraw, 4, 1)):
        for name in names:
            loads[name].wait()

        def one_side(side, total):
            part = pl.ds(pl.multiple_of(side * own_rows, 16), own_rows)
            hat, scale = head_stats(raw_ref[part, :].astype(F32), ones_low)
            grad = compact_rows(grad_in, jnp.where(side == 0, *bases))
            scaled = grad * repeated(gains_ref[gain : gain + 1, :HD], cols // HD)
            d_raw = (scaled - head_means(scaled, ones_low) - hat * head_means(scaled * hat, ones_low)) * scale
            d_proj[part, at * cols : (at + 1) * cols] = d_raw.astype(BF)
            return total + jnp.sum(grad * hat, axis=0, keepdims=True)

        total = lax.fori_loop(0, 2, one_side, jnp.zeros((1, cols), F32))
        folded = total[:, :HD]
        for head in range(1, cols // HD):
            folded += total[:, head * HD : (head + 1) * HD]
        gains.append(folded)
    loads["dv"].wait()

    @pl.loop(0, 2)
    def _(side):
        d_proj[pl.ds(pl.multiple_of(side * own_rows, 16), own_rows), 2 * cols : 3 * cols] = compact_rows(s_dv, jnp.where(side == 0, *bases)).astype(BF)

    loads["dn"].wait()
    loads["heads"].wait()

    def add_dn(part):
        size = width // 2

        @pl.loop(0, 2)
        def _(turn):
            some = pl.ds(pl.multiple_of(turn * size, LANES), size)
            dn[part, some] = (dn[part, some].astype(F32) + dot(d_proj[part, :], head_rows(turn, slice(0, 3 * cols)), NT)).astype(BF)

    add_dn(other)
    rows_copy.append(remote(dn.at[pl.ds(own_rows, own_rows)], o_dn_got, tsend.at[deep + wide + 1], trecv.at[deep + wide + 1], partner))
    rows_copy[1].start()

    def keep(at, values):
        for b in range(batch):
            mine[b // (2 * wide), (b // 2) % wide, b % 2, :, at] = values[2 * b * shard : 2 * (b + 1) * shard].astype(BF)

    loads["normed"].wait()

    @pl.loop(0, 3)
    def _(piece):
        at = pl.ds(pl.multiple_of(piece * cols, LANES), cols)
        keep(at, dot(normed[...], d_proj[:, at], TN))

    over_core(4)
    loads["o"].wait()
    loads["dy"].wait()

    @pl.loop(0, 2)
    def _(side):
        mixed[pl.ds(pl.multiple_of(side * own_rows, 16), own_rows), :] = compact_rows(s_o, jnp.where(side == 0, *bases)).astype(BF)

    over_y(0)
    over_x(4)
    keep(slice(3 * cols, 4 * cols), dot(cotan[...], mixed[own, :], TN) + dot(dy_par[...], mixed[other, :], TN))
    over_core(5)
    add_dn(own)
    puts = [pltpu.make_async_copy(dn.at[pl.ds(0, own_rows)], o_dn, osem)]
    puts[0].start()
    over_x(5)
    over_y(1)
    loads["x"].wait()
    grad_g = jnp.zeros((1, width), F32)
    for side, ref in enumerate((tokens, x_par)):

        def one_strip(turn, total):
            vhat, _ = norm_stats(ref[pl.ds(pl.multiple_of(turn * STRIP, 16), STRIP), :].astype(F32))
            some = dn[pl.ds(pl.multiple_of(side * own_rows + turn * STRIP, 16), STRIP), :].astype(F32)
            return total + jnp.sum(some * vhat, axis=0, keepdims=True)

        grad_g = lax.fori_loop(0, own_rows // STRIP, one_strip, grad_g)
    grad_db = jnp.sum(cotan[...].astype(F32), axis=0, keepdims=True)
    per = gb_ref.shape[1] // batch
    both = jnp.concatenate(gains, axis=1)
    bias = gb_ref[...]
    t_all[...] = jnp.zeros(t_all.shape, F32)
    for b, (zz, xx, cc, s) in enumerate(places):
        inside = jnp.where(y == b // batch, 1.0, 0.0)
        t_all[zz, xx, cc, s, 0:1, :shard] = grad_g[:, b * shard : (b + 1) * shard]
        t_all[zz, xx, cc, s, 1:2, :shard] = grad_db[:, b * shard : (b + 1) * shard]
        t_all[zz, xx, cc, s, 2:3, :per] = bias[:, (b % batch) * per : (b % batch + 1) * per] * inside
        t_all[zz, xx, cc, s, 3:4, : 2 * HD] = both
    tiny = [remote(t_all.at[:, :, 1 - core], t_core, tsend.at[0], trecv.at[0], sibling)]
    tiny[0].start()
    for name in ("own", "got"):
        loads[name].wait()
    rows_copy[0].wait_recv()
    mixed_got = compact_rows(o_got, 0).astype(BF)
    mixed_own = mixed[own, :]
    all_heads = jnp.concatenate([jnp.where(y == 0, mixed_own, mixed_got), jnp.where(y == 0, mixed_got, mixed_own)], axis=1)

    @pl.loop(0, 2)
    def _(turn):
        some = pl.ds(pl.multiple_of(turn * (width // 2), LANES), width // 2)
        attended = dot(all_heads, head_rows(turn, slice(3 * cols, 5 * cols)), NT)
        block_ref[:, some] = (tokens[:, some].astype(F32) + attended + out_own[:, some].astype(F32) + out_got[:, some].astype(F32) + bias_ref[:, some]).astype(BF)

    tiny[0].wait_recv()
    t_x[...] = t_all[:, :, core] + t_core[...]
    group = []
    for s, peer in enumerate(along_x):
        group.append(remote(t_x.at[:, (x + s + 1) % wide], t_xgot.at[x], tsend.at[1 + s], trecv.at[1 + s], peer))
        group[s].start()
    tiny += group
    t_xgot[x] = t_x[:, x]
    over_y(2)
    over_z(4)
    for copy in group:
        copy.wait_recv()
    total = t_xgot[0]
    for xx in range(1, wide):
        total += t_xgot[xx]
    t_z[...] = total
    group = []
    for s, peer in enumerate(along_z):
        group.append(remote(t_z.at[(z + s + 1) % deep], t_zgot.at[z], tsend.at[wide + s], trecv.at[wide + s], peer))
        group[s].start()
    tiny += group
    t_zgot[z] = t_z[z]
    over_y(3)
    over_z(5)
    for copy in group:
        copy.wait_recv()
    total = t_zgot[0]
    for zz in range(1, deep):
        total += t_zgot[zz]
    t_y[...] = total
    tiny.append(remote(t_y.at[1 - y], t_ygot, tsend.at[wide + deep - 1], trecv.at[wide + deep - 1], partner))
    tiny[-1].start()
    for i in range(4):
        last(i)
    over_y(4)
    tiny[-1].wait_recv()
    small_ref[...] = t_y[y] + t_ygot[...]
    over_y(5)
    last(4)
    last(5)
    puts[0].wait()
    rows_copy[1].wait_recv()
    for copy in list(first.values()) + [c for group in list(second.values()) + list(third.values()) for c in group] + list(fourth.values()) + tiny + rows_copy:
        copy.wait_send()


def last_half(tokens, cotan, bias, gb, gains, kept, sums, batch):
    deep, wide = grid_of(batch)
    own_rows, width = tokens.shape
    rows = 2 * own_rows
    hidden = gb.shape[1]
    cols = hidden // 4
    block = hidden // 2
    shard = width // (2 * batch)
    slots = own_rows // PATCHES
    cuts = [(part, slice(at, at + block)) for part in range(3) for at in (0, block)]
    vm = pl.BlockSpec(memory_space=pltpu.VMEM)
    hbm = pl.BlockSpec(memory_space=pl.ANY)
    buf = lambda *shape: pltpu.VMEM(shape, BF)
    tile = lambda *lead: pltpu.VMEM(lead + TINY, F32)
    scratch = [buf(*k.shape) for k in kept]
    scratch += [buf(wide, deep, 2 * shard, hidden)] * 2
    scratch += [buf(deep, wide, 2, 2 * shard, hidden), buf(deep, wide, 2 * shard, hidden), buf(wide - 1, deep, 2 * shard, hidden)]
    scratch += [buf(deep, 2 * shard, hidden)] * 3 + [buf(deep - 1, 2 * shard, hidden)] * 3 + [buf(shard, hidden)] * 6
    scratch += [buf(rows, 3 * cols), buf(rows, cols), buf(slots * SLOT, cols)]
    scratch += [tile(deep, wide, 2, 2), tile(deep, wide, 2), tile(deep, wide, 2), tile(wide, deep, 2), tile(deep, 2), tile(deep, 2), tile(2), tile()]
    scratch += [pltpu.SemaphoreType.DMA((len(cuts), deep + wide))] * 2 + [pltpu.SemaphoreType.DMA((deep + wide + 2,))] * 2 + [pltpu.SemaphoreType.DMA((len(kept),)), pltpu.SemaphoreType.DMA((2 * wide,)), pltpu.SemaphoreType.DMA]
    full = lambda *shape: jax.ShapeDtypeStruct(shape, F32)
    low = jax.ShapeDtypeStruct((own_rows, width), BF)
    return pl.pallas_call(
        functools.partial(last_kernel, deep=deep, wide=wide, cuts=cuts),
        in_specs=[vm] * 5 + [hbm] * (len(kept) + 2 * wide),
        out_specs=[hbm] * 2 + [vm] * 6,
        out_shape=[low] * 3 + [full(3, shard, 2 * cols), full(shard, 2 * cols), full(shard, 2 * hidden), full(shard, 2 * hidden), full(*TINY)],
        scratch_shapes=scratch,
        compiler_params=pltpu.CompilerParams(collective_id=1, has_side_effects=True, vmem_limit_bytes=VMEM_CAP),
        name="head_gradients_and_scatter",
    )(tokens, cotan, bias, gb, gains, *kept, *sums)


def result_kernel(tokens, cotan, gain, dn_own, dn_got, block_in, qkv_in, wo_in, up_in, down_in, small, block, grad, qkv, wo, up, down, up_b, down_b, norm_g, query_g, key_g):
    vhat, scale = norm_stats(tokens[...].astype(F32))
    scaled = (dn_own[...].astype(F32) + dn_got[...].astype(F32)) * gain[...]
    d_tokens = (scaled - jnp.mean(scaled, axis=-1, keepdims=True) - vhat * jnp.mean(scaled * vhat, axis=-1, keepdims=True)) * scale
    grad[...] = (cotan[...].astype(F32) + d_tokens).astype(BF)
    block[...] = block_in[...]

    @pl.when(pl.program_id(0) == 0)
    def _():
        qkv[...] = qkv_in[...]
        wo[...] = wo_in[...]
        up[...] = up_in[...]
        down[...] = down_in[...]
        norm_g[...] = small[0:1, : norm_g.shape[1]]
        down_b[...] = small[1:2, : down_b.shape[1]]
        up_b[...] = small[2:3, : up_b.shape[1]]
        query_g[...] = small[3:4, :HD]
        key_g[...] = small[3:4, HD : 2 * HD]


def results(tokens, cotan, gain, dn_own, dn_got, block_in, sums, small, per):
    rows, width = tokens.shape
    chunk = rows // 2
    shard = sums[1].shape[0]
    blk = pl.BlockSpec((chunk, width), lambda j: (j, 0))
    whole = lambda shape: pl.BlockSpec(shape, lambda j: (0,) * len(shape))
    vectors = [(1, per), (1, shard), (1, shard), (1, HD), (1, HD)]
    return pl.pallas_call(
        result_kernel,
        grid=(rows // chunk,),
        in_specs=[blk, blk, whole(gain.shape), blk, blk, blk] + [whole(s.shape) for s in sums] + [whole(small.shape)],
        out_specs=[blk, blk] + [whole(s.shape) for s in sums] + [whole(v) for v in vectors],
        out_shape=[jax.ShapeDtypeStruct((rows, width), BF)] * 2 + [jax.ShapeDtypeStruct(s.shape, F32) for s in sums] + [jax.ShapeDtypeStruct(v, F32) for v in vectors],
        compiler_params=pltpu.CompilerParams(vmem_limit_bytes=VMEM_CAP),
        name="results",
    )(tokens, cotan, gain, dn_own, dn_got, block_in, *sums, small)


def local(tokens, cotangent, image_tokens, w_qkv, w_out, w_up, bias_up, w_down, bias_down, norm_gain, query_gain, key_gain):
    batch = lax.axis_size("batch")
    deep, wide = grid_of(batch)
    row = lambda v: v.reshape(1, -1)
    weights = (w_qkv, w_out.T, w_up, w_down.T)
    vectors = (row(norm_gain), row(bias_down), row(bias_up), row(query_gain), row(key_gain))
    made = first_half(tokens, cotangent, weights, vectors, batch)
    x_par, dy_par, normed, q, k, v, d_o, qraw, kraw, head_w, out_own, out_other, dn = made[:13]
    up_sums, down_sums = made[13 : 13 + wide], made[13 + wide : 13 + 2 * wide]
    gb, gain, bias, gains = made[13 + 2 * wide :]
    at = lambda z, x, c: (z * wide + x) * 2 + c

    def over_x(terms):
        return [terms[0]] + [lax.ppermute(terms[s], "batch", [(at(z, x, c), at(z, (x + s) % wide, c)) for z in range(deep) for x in range(wide) for c in range(2)]) for s in range(1, wide)]

    up_sums = over_x(up_sums)
    out_got = lax.ppermute(out_other, "branch", [(0, 1), (1, 0)])
    down_sums = over_x(down_sums)
    o, dq, dk, dv = attention(image_tokens[0], q, k, v, d_o)
    kept = [x_par, dy_par, normed, o, dq, dk, dv, qraw, kraw, head_w, out_own, out_got, dn]
    dn_own, dn_got, block_in, g_qkv, g_out, g_up, g_down, small = last_half(tokens, cotangent, bias, gb, gains, kept, up_sums + down_sums, batch)
    block_out, grad_tokens, g_qkv, g_out, g_up, g_down, g_up_b, g_down_b, g_norm, g_query, g_key = results(tokens, cotangent, gain, dn_own, dn_got, block_in, [g_qkv, g_out, g_up, g_down], small, bias_up.shape[0])
    flat = lambda v: v.reshape(-1)
    return (block_out, grad_tokens, g_qkv, g_out.T, g_up, flat(g_up_b), g_down.T, flat(g_down_b), flat(g_norm), flat(g_query), flat(g_key))


def solution(mesh):
    both = ("batch", "branch")
    in_specs = (P(both, None), P(both, None), P("batch", None), P(None, both, None), P(None, both), P(both, None), P(both), P(None, both), P(both), P(both), P(), P())
    out_specs = (P(both, None), P(both, None), P(None, both, None), P(None, both), P(both, None), P(both), P(None, both), P(both), P(both), P(), P())
    return jax.shard_map(local, mesh=mesh, in_specs=in_specs, out_specs=out_specs, check_vma=False)
```

```python
import functools
import jax
import jax.numpy as jnp
from jax import lax
from jax.experimental import pallas as pl
from jax.experimental.pallas import tpu as pltpu
from jax.sharding import PartitionSpec as P

HD = 64
LANES = 128
NORM_EPS = 1e-06
LONGEST = 784
PATCHES = 196
SLOT = 208
VMEM_CAP = 66_000_000
BF = jnp.bfloat16
F32 = jnp.float32


def dot(a, b, dims=((1,), (0,))):
    return lax.dot_general(a, b, (dims, ((), ())), preferred_element_type=F32)


NT = ((1,), (1,))
TN = ((0,), (0,))


def norm_stats(values):
    centred = values - jnp.mean(values, axis=-1, keepdims=True)
    spread = jnp.mean(centred * centred, axis=-1, keepdims=True)
    scale = lax.rsqrt(spread + NORM_EPS)
    return centred * scale, scale


def head_means(values, ones_low):
    means = []
    for at in range(0, values.shape[1], LANES):
        some = values[:, at : at + LANES]
        high = some.astype(BF)
        low = (some - high.astype(F32)).astype(BF)
        means.append(dot(jnp.concatenate([high, low], axis=1), ones_low))
    return jnp.concatenate(means, axis=1)


def head_ones():
    row = lax.broadcasted_iota(jnp.int32, (2 * LANES, LANES), 0) % LANES // HD
    col = lax.broadcasted_iota(jnp.int32, (2 * LANES, LANES), 1) // HD
    return jnp.where(row == col, 1.0 / HD, 0.0).astype(BF)


def head_stats(raw, ones_low):
    centred = raw - head_means(raw, ones_low)
    scale = lax.rsqrt(head_means(centred * centred, ones_low) + NORM_EPS)
    return centred * scale, scale


MESH = pl.DeviceIdType.MESH


def place():
    return lax.axis_index("batch"), lax.axis_index("branch")


def grid_of(batch):
    chips = batch // 2
    across = 1
    while across * across * 4 <= chips:
        across *= 2
    return chips // across, across


def greet(peers):
    barrier = pltpu.get_barrier_semaphore()
    for peer in peers:
        pl.semaphore_signal(barrier, inc=1, device_id=peer, device_id_type=MESH)
    pl.semaphore_wait(barrier, len(peers))


def neighbours(deep, wide):
    batch, branch = place()
    core, x, z = batch % 2, (batch // 2) % wide, batch // (2 * wide)
    at = lambda zz, xx, cc: (zz * wide + xx) * 2 + cc
    partner = (batch, 1 - branch)
    along_z = [(at((z + s) % deep, x, core), branch) for s in range(1, deep)]
    along_x = [(at(z, (x + s) % wide, core), branch) for s in range(1, wide)]
    sibling = (at(z, x, 1 - core), branch)
    return (z, x, core, branch), partner, along_z, along_x, sibling


def remote(src, dst, send, recv, peer):
    return pltpu.make_async_remote_copy(src_ref=src, dst_ref=dst, send_sem=send, recv_sem=recv, device_id=peer, device_id_type=MESH)


TINY = (8, LANES)
STRIP = 112


def gelu_parts(hidden):
    square = hidden * hidden
    tanh = jnp.tanh(hidden * (0.7978845608028654 + 0.035677408136300125 * square))
    half = 0.5 + 0.5 * tanh
    act = hidden * half
    slope = half + (act * (1.0 - tanh)) * (0.7978845608028654 + 0.1070322244089 * square)
    return act.astype(BF), slope


def repeated(values, count):
    return jnp.concatenate([values] * count, axis=1)


def first_kernel(*refs, deep, wide, cuts, block):
    tokens, cotan, qkv_ref, wo_ref, up_ref, down_ref, nb_ref, db_ref, ub_ref, qg_ref, kg_ref = refs[:11]
    o_x, o_dy, o_normed, o_q, o_k, o_v, o_do, o_qraw, o_kraw, o_heads, o_own, o_other, o_dn = refs[11:24]
    o_sums = (refs[24 : 24 + wide], refs[24 + wide : 24 + 2 * wide])
    gb_ref, gain_ref, bias_ref, tiny = refs[24 + 2 * wide : 28 + 2 * wide]
    scratch = refs[28 + 2 * wide :]
    packs, lands, wires = scratch[:3], scratch[3:6], scratch[6:9]
    rounded, tiny_all, x_par, dy_par, normed, act, d_hid, s_q, s_k, s_v, s_do, s_qraw, s_kraw, s_out, s_dn = scratch[9:24]
    grads, got_core, flats = scratch[24:26], scratch[26:28], scratch[28:31]
    send, recv, tsend, trecv, csend, crecv, osem = scratch[31:]
    (z, x, core, y), partner, along_z, along_x, sibling = neighbours(deep, wide)
    batch = 2 * deep * wide
    own_rows, width = tokens.shape
    shard, hidden = packs[0].shape[1:]
    cols = hidden // 4
    pair = 2 * shard
    direct = pair % 16 == 0
    places = [(b // (2 * wide), (b // 2) % wide, b % 2, s) for b in range(batch) for s in range(2)]

    for half in range(2):
        some = slice(half * cols, (half + 1) * cols)
        packs[0][half] = up_ref[:, half * hidden : (half + 1) * hidden].astype(BF)
        packs[1][half] = down_ref[:, half * hidden : (half + 1) * hidden].astype(BF)
        for at in range(3):
            packs[2][half, :, at * cols : (at + 1) * cols] = qkv_ref[at, :, some].astype(BF)
        packs[2][half, :, 3 * cols :] = wo_ref[...].astype(BF)
    rounded[...] = jnp.zeros(TINY, BF)
    for row, ref in enumerate((nb_ref, db_ref, ub_ref, qg_ref, kg_ref)):
        rounded[row : row + 1, : ref.shape[1]] = ref[...].astype(BF)
    tiny[...] = rounded[...].astype(F32)
    tiny_all[z, x, core, y] = tiny[...]
    greet([partner, sibling] + along_z + along_x)
    outs = []

    def put(src, dst):
        copy = pltpu.make_async_copy(src, dst, osem.at[len(outs)])
        copy.start()
        outs.append(copy)

    spread_tiny = [remote(tiny, tiny_all.at[z, x, core, y], tsend.at[0], trecv.at[0], partner)]
    spread_tiny[0].start()
    over_y = []
    for i, (part, at) in enumerate(cuts):
        over_y.append(remote(packs[part].at[1 - y, :, at], lands[part].at[:, at], send.at[i, 0], recv.at[i, 0], partner))
        over_y[i].start()
    rows_copy = [remote(tokens, x_par, tsend.at[deep + wide], trecv.at[deep + wide], partner), remote(cotan, dy_par, tsend.at[deep + wide + 1], trecv.at[deep + wide + 1], partner)]
    for copy in rows_copy:
        copy.start()

    def tiny_stage(block, peers, first):
        group = [remote(block, block, tsend.at[first + s], trecv.at[first + s], peer) for s, peer in enumerate(peers)]
        for copy in group:
            copy.start()
        for copy in group:
            copy.wait_recv()
        spread_tiny.extend(group)

    over_z, over_x, over_core = [], [], []

    def start_z(i):
        part, at = cuts[i]
        over_y[i].wait_recv()
        mine, other = packs[part][y, :, at].astype(F32), lands[part][:, at].astype(F32)
        pair = jnp.concatenate([jnp.where(y == 0, mine, other), jnp.where(y == 0, other, mine)], axis=0)
        wires[part][z, x, core, :, at] = pair.astype(BF)
        block = wires[part].at[z, x, core, :, at]
        over_z.append([remote(block, block, send.at[i, 1 + s], recv.at[i, 1 + s], peer) for s, peer in enumerate(along_z)])
        for copy in over_z[i]:
            copy.start()

    def start_x(i):
        part, at = cuts[i]
        for copy in over_z[i]:
            copy.wait_recv()
        block = wires[part].at[:, x, core, :, at]
        over_x.append([remote(block, block, send.at[i, deep + s], recv.at[i, deep + s], peer) for s, peer in enumerate(along_x)])
        for copy in over_x[i]:
            copy.start()

    def start_core(i):
        part, at = cuts[i]
        for copy in over_x[i]:
            copy.wait_recv()
        block = wires[part].at[:, :, core, :, at]
        over_core.append(remote(block, block, send.at[i, deep + wide - 1], recv.at[i, deep + wide - 1], sibling))
        over_core[i].start()

    def arrive(i):
        part, at = cuts[i]
        over_core[i].wait_recv()
        if not direct:
            for b in range(batch):
                flats[part][2 * shard * b : 2 * shard * (b + 1), at] = wires[part][b // (2 * wide), (b // 2) % wide, b % 2, :, at]

    def weight(part, at):
        if direct:
            value = wires[part][:, :, :, :, at]
            return value.reshape(width, value.shape[-1])
        return flats[part][:, at]

    for i in range(len(cuts)):
        start_z(i)
        if i == 0:
            spread_tiny[0].wait_recv()
            tiny_stage(tiny_all.at[z, x, core], along_z, 1)
        if i == 1:
            tiny_stage(tiny_all.at[:, x, core], along_x, deep)
        if i == 2:
            tiny_stage(tiny_all.at[:, :, core], [sibling], deep + wide - 1)
    per = ub_ref.shape[1]
    gain_ref[...] = jnp.concatenate([tiny_all[p][0:1, :shard] for p in places], axis=1)
    bias_ref[...] = jnp.concatenate([tiny_all[p][1:2, :shard] for p in places], axis=1)
    low_b = jnp.concatenate([tiny_all[p][2:3, :per] for p in places[:batch]], axis=1)
    high_b = jnp.concatenate([tiny_all[p][2:3, :per] for p in places[batch:]], axis=1)
    gb_ref[...] = jnp.where(y == 0, low_b, high_b)

    sides = ((tokens, cotan, slice(0, own_rows)), (x_par, dy_par, slice(own_rows, 2 * own_rows)))

    def normalise(side):
        @pl.loop(0, own_rows // STRIP)
        def _(turn):
            strip = pl.ds(pl.multiple_of(turn * STRIP, 16), STRIP)
            vhat, _ = norm_stats(sides[side][0][strip, :].astype(F32))
            normed[pl.ds(pl.multiple_of(side * own_rows + turn * STRIP, 16), STRIP), :] = (vhat * gain_ref[...]).astype(BF)

    def expand(side, at, back):
        rows = sides[side][2]

        turns = 3 if back else 12

        @pl.loop(0, turns)
        def _(turn):
            size = (at.stop - at.start) // turns
            some = pl.ds(pl.multiple_of(at.start + turn * size, LANES), size)
            act[rows, some], slope = gelu_parts(dot(normed[rows, :], weight(0, some)) + gb_ref[:, some])
            if back:
                slope *= dot(sides[side][1][...], weight(1, some))
            d_hid[rows, some] = slope.astype(BF)

    def apply_back(side):
        rows = sides[side][2]

        @pl.loop(0, 2)
        def _(turn):
            at = pl.ds(pl.multiple_of(turn * block, LANES), block)
            d_hid[rows, at] = (d_hid[rows, at].astype(F32) * dot(sides[side][1][...], weight(1, at))).astype(BF)

    def contract(side, low, kept, part):
        rows = sides[side][2]
        size = width // 2

        @pl.loop(0, 2)
        def _(turn):
            if direct:
                value = wires[part][pl.ds(turn * (deep // 2), deep // 2)].reshape(size, hidden)
            else:
                value = flats[part][pl.ds(pl.multiple_of(turn * size, 16), size), :]
            kept[rows, pl.ds(pl.multiple_of(turn * size, LANES), size)] = dot(low[rows, :], value, NT).astype(BF)

    def place_rows(base, ref, values):
        for at in range(own_rows // PATCHES):
            ref[pl.ds(pl.multiple_of((base + at) * SLOT, 16), PATCHES), :] = values[at * PATCHES : (at + 1) * PATCHES].astype(BF)

    def queries_keys():
        ones_low = head_ones()

        @pl.loop(0, 2)
        def _(side):
            rows = pl.ds(pl.multiple_of(side * own_rows, 16), own_rows)
            base = jnp.where(side == 0, y, 1 - y) * (own_rows // PATCHES)
            for at, (raw_ref, low_ref, gain) in enumerate(((s_qraw, s_q, 3), (s_kraw, s_k, 4))):
                raw = dot(normed[rows, :], weight(2, slice(at * cols, (at + 1) * cols)))
                raw_ref[rows, :] = raw.astype(BF)
                hat, _ = head_stats(raw, ones_low)
                place_rows(base, low_ref, hat * repeated(tiny[gain : gain + 1, :HD], cols // HD))

    def values_of():
        @pl.loop(0, 2)
        def _(side):
            rows = pl.ds(pl.multiple_of(side * own_rows, 16), own_rows)
            place_rows(jnp.where(side == 0, y, 1 - y) * (own_rows // PATCHES), s_v, dot(normed[rows, :], weight(2, slice(2 * cols, 3 * cols))))

    def back_of(side):
        place_rows((y if side == 0 else 1 - y) * (own_rows // PATCHES), s_do, dot(sides[side][1][...], weight(2, pl.ds(pl.multiple_of((3 + y) * cols, LANES), cols))))

    over_sib = []

    def grad_own(part):
        rows = sides[0][2]

        @pl.loop(0, 6)
        def _(turn):
            size = hidden // 6
            some = pl.ds(pl.multiple_of(turn * size, LANES), size)
            value = dot(normed[rows, :], d_hid[rows, some], TN) if part == 0 else dot(cotan[...], act[rows, some], TN)
            for b in range(batch):
                grads[part][b // (2 * wide), (b // 2) % wide, b % 2, :, some] = value[b * pair : (b + 1) * pair].astype(BF)

    def grad_rest(part, at):
        rows = sides[1][2]

        @pl.loop(0, 2)
        def _(turn):
            size = (at.stop - at.start) // 2
            some = pl.ds(pl.multiple_of(at.start + turn * size, LANES), size)
            value = dot(normed[rows, :], d_hid[rows, some], TN) if part == 0 else dot(dy_par[...], act[rows, some], TN)
            for b in range(batch):
                block_at = (b // (2 * wide), (b // 2) % wide, b % 2, slice(None), some)
                grads[part][block_at] = (grads[part][block_at].astype(F32) + value[b * pair : (b + 1) * pair]).astype(BF)

        i = len(over_sib)
        over_sib.append(remote(grads[part].at[:, :, 1 - core, :, at], got_core[part].at[:, :, :, at], csend.at[i], crecv.at[i], sibling))
        over_sib[i].start()

    def add_core(i, part, at):
        over_sib[i].wait_recv()

        @pl.loop(0, deep)
        def _(zz):
            for xx in range(wide):
                total = grads[part][zz, xx, core, :, at].astype(F32) + got_core[part][zz, xx, :, at].astype(F32)
                got_core[part][zz, xx, :, at] = total.astype(BF)

    first, second = slice(0, block), slice(block, 2 * block)
    start_x(0)
    normalise(0)
    start_x(1)
    start_core(0)
    start_x(2)
    start_core(1)
    arrive(0)
    arrive(1)
    expand(0, first, True)
    start_x(3)
    start_core(2)
    rows_copy[0].wait_recv()
    normalise(1)
    put(x_par, o_x)
    put(normed, o_normed)
    start_x(4)
    start_core(3)
    arrive(2)
    arrive(3)
    expand(0, second, True)
    start_core(4)
    expand(1, slice(0, hidden), False)
    start_x(5)
    contract(0, act, s_out, 1)
    contract(0, d_hid, s_dn, 0)
    grad_own(0)
    grad_own(1)
    contract(1, act, s_out, 1)
    put(s_out.at[pl.ds(0, own_rows)], o_own)
    put(s_out.at[pl.ds(own_rows, own_rows)], o_other)
    arrive(4)
    start_core(5)
    queries_keys()
    for src, dst in ((s_q, o_q), (s_k, o_k), (s_qraw, o_qraw), (s_kraw, o_kraw)):
        put(src, dst)
    arrive(5)
    put(wires[2] if direct else flats[2], o_heads)
    values_of()
    put(s_v, o_v)
    back_of(0)
    rows_copy[1].wait_recv()
    put(dy_par, o_dy)
    back_of(1)
    put(s_do, o_do)
    apply_back(1)
    contract(1, d_hid, s_dn, 0)
    put(s_dn, o_dn)
    grad_rest(0, first)
    grad_rest(0, second)
    add_core(0, 0, first)
    grad_rest(1, first)
    add_core(1, 0, second)
    for s in range(wide):
        put(got_core[0].at[:, (x + s) % wide], o_sums[0][s])
    grad_rest(1, second)
    add_core(2, 1, first)

    @pl.loop(0, 6)
    def _(turn):
        some = pl.ds(pl.multiple_of(turn * (hidden // 6), LANES), hidden // 6)
        gb_ref[:, some] = dot(jnp.ones((8, 2 * own_rows), BF), d_hid[:, some])[:1]

    add_core(3, 1, second)
    for s in range(wide):
        put(got_core[1].at[:, (x + s) % wide], o_sums[1][s])
    for copy in outs:
        copy.wait()
    for copy in spread_tiny + over_y + rows_copy + [c for group in over_z + over_x for c in group] + over_core + over_sib:
        copy.wait_send()


def first_half(tokens, cotan, weights, vectors, batch):
    deep, wide = grid_of(batch)
    own_rows, width = tokens.shape
    shard, hidden = weights[2].shape[0], weights[2].shape[1] // 2
    cols = hidden // 4
    block = hidden // 2
    rows = 2 * own_rows
    spread_rows = rows // PATCHES * SLOT
    widths = (hidden, hidden, 5 * cols)
    first, second = slice(0, block), slice(block, hidden)
    cuts = [(0, first), (1, first), (0, second), (1, second), (2, slice(0, 2 * cols)), (2, slice(2 * cols, 5 * cols))]
    vm = pl.BlockSpec(memory_space=pltpu.VMEM)
    hbm = pl.BlockSpec(memory_space=pl.ANY)
    direct = (2 * shard) % 16 == 0
    wire_shapes = [(deep, wide, 2, 2 * shard, w) for w in widths]
    flat_shapes = [(width, w) for w in widths]
    low = lambda *shape: jax.ShapeDtypeStruct(shape, BF)
    outs = [low(own_rows, width)] * 2 + [low(rows, width)] + [low(spread_rows, cols)] * 4 + [low(rows, cols)] * 2
    outs += [low(*(wire_shapes if direct else flat_shapes)[2])] + [low(own_rows, width)] * 2 + [low(rows, width)] + [low(deep, 2 * shard, hidden)] * (2 * wide)
    tiny_outs = [jax.ShapeDtypeStruct((1, hidden), F32), jax.ShapeDtypeStruct((1, width), F32), jax.ShapeDtypeStruct((1, width), F32), jax.ShapeDtypeStruct(TINY, F32)]
    buf = lambda *shape: pltpu.VMEM(shape, BF)
    scratch = [buf(2, shard, w) for w in widths] + [buf(shard, w) for w in widths] + [buf(*s) for s in wire_shapes]
    scratch += [buf(*TINY), pltpu.VMEM((deep, wide, 2, 2) + TINY, F32), buf(own_rows, width), buf(own_rows, width), buf(rows, width), buf(rows, hidden), buf(rows, hidden)]
    scratch += [buf(spread_rows, cols)] * 4 + [buf(rows, cols)] * 2 + [buf(rows, width)] * 2
    scratch += [buf(deep, wide, 2, 2 * shard, hidden)] * 2 + [buf(deep, wide, 2 * shard, hidden)] * 2
    scratch += [buf(16, LANES) if direct else buf(*s) for s in flat_shapes]
    scratch += [pltpu.SemaphoreType.DMA((len(cuts), deep + wide))] * 2 + [pltpu.SemaphoreType.DMA((deep + wide + 2,))] * 2 + [pltpu.SemaphoreType.DMA((4,))] * 2 + [pltpu.SemaphoreType.DMA((len(outs),))]
    return pl.pallas_call(
        functools.partial(first_kernel, deep=deep, wide=wide, cuts=cuts, block=block),
        in_specs=[vm] * 11,
        out_specs=[hbm] * len(outs) + [vm] * 4,
        out_shape=outs + tiny_outs,
        scratch_shapes=scratch,
        compiler_params=pltpu.CompilerParams(collective_id=0, has_side_effects=True, vmem_limit_bytes=VMEM_CAP),
        name="gather_and_feed_forward",
    )(tokens, cotan, *weights, *vectors)


def load_rows(ref, block, blocks):
    parts = [ref[pl.ds(pl.multiple_of((block + at) * SLOT, 16), PATCHES), :] for at in range(blocks)]
    return parts[0] if blocks == 1 else jnp.concatenate([p.astype(F32) for p in parts], axis=0).astype(BF)

def attend_pair(pair_q, pair_k, pair_v, pair_do, pieces):
    count = pair_q.shape[0]
    lane = lax.broadcasted_iota(jnp.int32, (count, 2 * HD), 1)
    pair_q = pair_q * jnp.asarray(0.125, BF)
    zero = jnp.zeros_like(pair_q)
    v_t, k_t = pair_v.T, pair_k.T
    mixed, grads_q, grad_k, grad_v = [], [], None, None
    for head in range(2):
        mine = (lane < HD) if head == 0 else (lane >= HD)
        q_m, do_m = jnp.where(mine, pair_q, zero), jnp.where(mine, pair_do, zero)
        part = slice(head * HD, (head + 1) * HD)
        outs, gqs = [], []
        for first, size in pieces:
            q, d_o = q_m[first : first + size], do_m[first : first + size]
            shifted = jnp.exp(dot(pair_k, q, NT))
            total = jnp.sum(shifted, axis=0, keepdims=True)
            weights = shifted * (1.0 / total)
            low = weights.astype(BF)
            d_weights = dot(pair_v, d_o, NT)
            inner = jnp.sum(weights * d_weights, axis=0, keepdims=True)
            d_scores = (weights * (d_weights - inner)).astype(BF)
            outs.append(dot(v_t[part], low))
            gqs.append(dot(k_t[part], d_scores))
            gv, gk = dot(low, d_o), dot(d_scores, q)
            grad_v = gv if grad_v is None else grad_v + gv
            grad_k = gk if grad_k is None else grad_k + gk
        join = lambda parts: parts[0] if len(parts) == 1 else jnp.concatenate(parts, axis=1)
        mixed.append(join(outs))
        grads_q.append(join(gqs))
    turn = lambda parts: jnp.concatenate(parts, axis=0).T
    return turn(mixed), turn(grads_q) * 0.125, grad_k, grad_v

def attention_kernel(count_ref, *refs, pieces, together):
    ins, outs, (small_ref,) = refs[:4], refs[4:8], refs[8:]
    place, smalls, bigs, big_at = 0, 0, 0, 0
    for slot in range(count_ref.shape[0]):
        count = count_ref[slot]
        is_small = (count == PATCHES).astype(jnp.int32)
        is_big = (count == LONGEST).astype(jnp.int32)
        small_ref[smalls] = place
        big_at = jnp.where(is_big == 1, place, big_at)
        smalls, bigs = smalls + is_small, bigs + is_big
        place = place + is_small + (LONGEST // PATCHES) * is_big

    def images(firsts, blocks, pieces):
        loaded = [[load_rows(ref, block, blocks) for ref in ins] for block in firsts]
        results = [attend_pair(*values, pieces) for values in loaded]
        for block, result in zip(firsts, results):
            for ref, values in zip(outs, result):
                for at in range(blocks):
                    ref[pl.ds(pl.multiple_of((block + at) * SLOT, 16), PATCHES), :] = values[at * PATCHES : (at + 1) * PATCHES].astype(ref.dtype)

    @pl.when(bigs > 0)
    def _():
        images([big_at], LONGEST // PATCHES, pieces)

    @pl.loop(0, smalls // together)
    def _(turn):
        images([small_ref[turn * together + at] for at in range(together)], 1, ((0, PATCHES),))

def attention(counts, q, k, v, d_o, pieces=((0, 784),), together=4):
    rows, cols = q.shape
    sm = pl.BlockSpec(memory_space=pltpu.SMEM)
    blk = pl.BlockSpec((rows, 2 * HD), lambda j: (0, j))
    return pl.pallas_call(
        functools.partial(attention_kernel, pieces=pieces, together=together),
        grid=(cols // (2 * HD),),
        in_specs=[sm] + [blk] * 4,
        out_specs=[blk] * 4,
        out_shape=[jax.ShapeDtypeStruct((rows, cols), t) for t in (BF, BF, BF, BF)],
        scratch_shapes=[pltpu.SMEM((counts.shape[0] + 1,), jnp.int32)],
        compiler_params=pltpu.CompilerParams(vmem_limit_bytes=VMEM_CAP),
        cost_estimate=pl.CostEstimate(flops=20_000_000_000, bytes_accessed=20_000_000, transcendentals=rows * LONGEST * cols // HD),
        name="attention",
    )(counts, q, k, v, d_o)


def last_kernel(*refs, deep, wide, cuts):
    tokens, cotan, bias_ref, gb_ref, gains_ref = refs[:5]
    i_x, i_dy, i_normed, i_o, i_dq, i_dk, i_dv, i_qraw, i_kraw, i_heads, i_own, i_got, i_dn = refs[5:18]
    i_sums = (refs[18 : 18 + wide], refs[18 + wide : 18 + 2 * wide])
    o_dn, o_dn_got, block_ref, qkv_ref, wo_ref, up_ref, down_ref, small_ref = refs[18 + 2 * wide : 26 + 2 * wide]
    scratch = refs[26 + 2 * wide :]
    x_par, dy_par, normed, s_o, s_dq, s_dk, s_dv, qraw, kraw, head_w, out_own, out_got, dn = scratch[:13]
    terms = scratch[13:15]
    mine, got_core, got_x = scratch[15:18]
    to_z, got_z, to_y, got_y = (scratch[18 + 3 * i : 21 + 3 * i] for i in range(4))
    d_proj, mixed, o_got = scratch[30:33]
    t_all, t_core, t_x, t_xgot, t_z, t_zgot, t_y, t_ygot = scratch[33:41]
    send, recv, tsend, trecv, lsem, gsem, osem = scratch[41:]
    (z, x, core, y), partner, along_z, along_x, sibling = neighbours(deep, wide)
    batch = 2 * deep * wide
    own_rows, width = tokens.shape
    rows = 2 * own_rows
    cols = qraw.shape[1]
    shard = to_y[0].shape[0]
    slots = own_rows // PATCHES
    places = [(b // (2 * wide), (b // 2) % wide, b % 2, s) for b in range(batch) for s in range(2)]
    own, other = slice(0, own_rows), slice(own_rows, rows)
    greet([partner, sibling] + along_z + along_x)

    theirs = pl.ds(pl.multiple_of((1 - y) * slots * SLOT, 16), slots * SLOT)
    rows_copy = [remote(i_o.at[theirs], o_got, tsend.at[deep + wide], trecv.at[deep + wide], partner)]
    rows_copy[0].start()
    held = {}
    for part in range(2):
        for s in range(wide):
            held[part, s] = pltpu.make_async_copy(i_sums[part][s], terms[part].at[s], gsem.at[part * wide + s])
            held[part, s].start()
    loads = {}
    for at, (name, src, dst) in enumerate((("qraw", i_qraw, qraw), ("dq", i_dq, s_dq), ("kraw", i_kraw, kraw), ("dk", i_dk, s_dk), ("dv", i_dv, s_dv), ("heads", i_heads, head_w), ("dn", i_dn, dn), ("normed", i_normed, normed), ("o", i_o, s_o), ("dy", i_dy, dy_par), ("x", i_x, x_par), ("own", i_own, out_own), ("got", i_got, out_got))):
        loads[name] = pltpu.make_async_copy(src, dst, lsem.at[at])
        loads[name].start()

    first, second, third, fourth = {}, {}, {}, {}

    def over_core(i):
        part, at = cuts[i]
        first[i] = remote(mine.at[:, :, 1 - core, :, at], got_core.at[:, :, :, at], send.at[i, 0], recv.at[i, 0], sibling)
        first[i].start()

    def over_x(i):
        part, at = cuts[i]
        first[i].wait_recv()

        @pl.loop(0, deep)
        def _(zz):
            for xx in range(wide):
                got_core[zz, xx, :, at] = (mine[zz, xx, core, :, at].astype(F32) + got_core[zz, xx, :, at].astype(F32)).astype(BF)

        second[i] = []
        for s, peer in enumerate(along_x):
            copy = remote(got_core.at[:, (x + s + 1) % wide, :, at], got_x.at[s, :, :, at], send.at[i, 1 + s], recv.at[i, 1 + s], peer)
            copy.start()
            second[i].append(copy)

    def over_z(i):
        part, at = cuts[i]
        if part == 2:
            for copy in second[i]:
                copy.wait_recv()

        @pl.loop(0, deep)
        def _(zz):
            if part == 2:
                total = got_core[zz, x, :, at].astype(F32)
                for s in range(wide - 1):
                    total += got_x[s, zz, :, at].astype(F32)
            else:
                total = terms[part][0, zz, :, at].astype(F32)
                for s in range(1, wide):
                    total += terms[part][s, zz, :, at].astype(F32)
            to_z[part][zz, :, at] = total.astype(BF)

        third[i] = []
        for s, peer in enumerate(along_z):
            copy = remote(to_z[part].at[(z + s + 1) % deep, :, at], got_z[part].at[s, :, at], send.at[i, wide + s], recv.at[i, wide + s], peer)
            copy.start()
            third[i].append(copy)

    def over_y(i):
        part, at = cuts[i]
        for copy in third[i]:
            copy.wait_recv()
        total = to_z[part][z, :, at].astype(F32)
        for s in range(deep - 1):
            total += got_z[part][s, :, at].astype(F32)
        low, high = total[:shard], total[shard:]
        to_y[part][:, at] = jnp.where(y == 0, high, low).astype(BF)
        fourth[i] = remote(to_y[part].at[:, at], got_y[part].at[:, at], send.at[i, wide + deep - 1], recv.at[i, wide + deep - 1], partner)
        fourth[i].start()
        deliver(part, y, at, jnp.where(y == 0, low, high))

    def deliver(part, half, at, values):
        if part < 2:
            ref = (up_ref, down_ref)[part]
            ref[:, pl.ds(pl.multiple_of(half * 4 * cols + at.start, LANES), at.stop - at.start)] = values
            return
        for piece in range(at.start // cols, at.stop // cols):
            some = values[:, piece * cols - at.start : (piece + 1) * cols - at.start]
            lanes = pl.ds(pl.multiple_of(half * cols, LANES), cols)
            if piece < 3:
                qkv_ref[piece, :, lanes] = some
            else:
                wo_ref[:, lanes] = some

    def last(i):
        part, at = cuts[i]
        fourth[i].wait_recv()
        deliver(part, 1 - y, at, got_y[part][:, at].astype(F32))

    def compact_rows(ref, base):
        parts = [ref[pl.ds(pl.multiple_of((base + at) * SLOT, 16), PATCHES), :].astype(F32) for at in range(slots)]
        return jnp.concatenate(parts, axis=0)

    bases = (y * slots, (1 - y) * slots)

    def head_rows(turn, at):
        if len(head_w.shape) > 2:
            value = head_w[pl.ds(turn * (deep // 2), deep // 2), :, :, :, at]
            return value.reshape(width // 2, value.shape[-1])
        return head_w[pl.ds(pl.multiple_of(turn * (width // 2), 16), width // 2), at]

    for part in range(2):
        for s in range(wide):
            held[part, s].wait()
    for i in range(4):
        over_z(i)
    ones_low = head_ones()
    gains = []
    for names, grad_in, raw_ref, gain, at in ((("dq", "qraw"), s_dq, qraw, 3, 0), (("dk", "kraw"), s_dk, kraw, 4, 1)):
        for name in names:
            loads[name].wait()

        def one_side(side, total):
            part = pl.ds(pl.multiple_of(side * own_rows, 16), own_rows)
            hat, scale = head_stats(raw_ref[part, :].astype(F32), ones_low)
            grad = compact_rows(grad_in, jnp.where(side == 0, *bases))
            scaled = grad * repeated(gains_ref[gain : gain + 1, :HD], cols // HD)
            d_raw = (scaled - head_means(scaled, ones_low) - hat * head_means(scaled * hat, ones_low)) * scale
            d_proj[part, at * cols : (at + 1) * cols] = d_raw.astype(BF)
            return total + jnp.sum(grad * hat, axis=0, keepdims=True)

        total = lax.fori_loop(0, 2, one_side, jnp.zeros((1, cols), F32))
        folded = total[:, :HD]
        for head in range(1, cols // HD):
            folded += total[:, head * HD : (head + 1) * HD]
        gains.append(folded)
    loads["dv"].wait()

    @pl.loop(0, 2)
    def _(side):
        d_proj[pl.ds(pl.multiple_of(side * own_rows, 16), own_rows), 2 * cols : 3 * cols] = compact_rows(s_dv, jnp.where(side == 0, *bases)).astype(BF)

    loads["dn"].wait()
    loads["heads"].wait()

    def add_dn(part):
        size = width // 2

        @pl.loop(0, 2)
        def _(turn):
            some = pl.ds(pl.multiple_of(turn * size, LANES), size)
            dn[part, some] = (dn[part, some].astype(F32) + dot(d_proj[part, :], head_rows(turn, slice(0, 3 * cols)), NT)).astype(BF)

    add_dn(other)
    rows_copy.append(remote(dn.at[pl.ds(own_rows, own_rows)], o_dn_got, tsend.at[deep + wide + 1], trecv.at[deep + wide + 1], partner))
    rows_copy[1].start()

    def keep(at, values):
        for b in range(batch):
            mine[b // (2 * wide), (b // 2) % wide, b % 2, :, at] = values[2 * b * shard : 2 * (b + 1) * shard].astype(BF)

    loads["normed"].wait()

    @pl.loop(0, 3)
    def _(piece):
        at = pl.ds(pl.multiple_of(piece * cols, LANES), cols)
        keep(at, dot(normed[...], d_proj[:, at], TN))

    over_core(4)
    loads["o"].wait()
    loads["dy"].wait()

    @pl.loop(0, 2)
    def _(side):
        mixed[pl.ds(pl.multiple_of(side * own_rows, 16), own_rows), :] = compact_rows(s_o, jnp.where(side == 0, *bases)).astype(BF)

    over_y(0)
    over_x(4)
    keep(slice(3 * cols, 4 * cols), dot(cotan[...], mixed[own, :], TN) + dot(dy_par[...], mixed[other, :], TN))
    over_core(5)
    add_dn(own)
    puts = [pltpu.make_async_copy(dn.at[pl.ds(0, own_rows)], o_dn, osem)]
    puts[0].start()
    over_x(5)
    over_y(1)
    loads["x"].wait()
    grad_g = jnp.zeros((1, width), F32)
    for side, ref in enumerate((tokens, x_par)):

        def one_strip(turn, total):
            vhat, _ = norm_stats(ref[pl.ds(pl.multiple_of(turn * STRIP, 16), STRIP), :].astype(F32))
            some = dn[pl.ds(pl.multiple_of(side * own_rows + turn * STRIP, 16), STRIP), :].astype(F32)
            return total + jnp.sum(some * vhat, axis=0, keepdims=True)

        grad_g = lax.fori_loop(0, own_rows // STRIP, one_strip, grad_g)

    def add_strip(turn, total):
        return total + jnp.sum(cotan[pl.ds(pl.multiple_of(turn * STRIP, 16), STRIP), :].astype(F32), axis=0, keepdims=True)

    grad_db = lax.fori_loop(0, own_rows // STRIP, add_strip, jnp.zeros((1, width), F32))
    per = gb_ref.shape[1] // batch
    both = jnp.concatenate(gains, axis=1)
    bias = gb_ref[...]
    t_all[...] = jnp.zeros(t_all.shape, F32)
    for b, (zz, xx, cc, s) in enumerate(places):
        inside = jnp.where(y == b // batch, 1.0, 0.0)
        t_all[zz, xx, cc, s, 0:1, :shard] = grad_g[:, b * shard : (b + 1) * shard]
        t_all[zz, xx, cc, s, 1:2, :shard] = grad_db[:, b * shard : (b + 1) * shard]
        t_all[zz, xx, cc, s, 2:3, :per] = bias[:, (b % batch) * per : (b % batch + 1) * per] * inside
        t_all[zz, xx, cc, s, 3:4, : 2 * HD] = both
    tiny = [remote(t_all.at[:, :, 1 - core], t_core, tsend.at[0], trecv.at[0], sibling)]
    tiny[0].start()
    for name in ("own", "got"):
        loads[name].wait()
    rows_copy[0].wait_recv()
    mixed_got = compact_rows(o_got, 0).astype(BF)
    mixed_own = mixed[own, :]
    all_heads = jnp.concatenate([jnp.where(y == 0, mixed_own, mixed_got), jnp.where(y == 0, mixed_got, mixed_own)], axis=1)

    @pl.loop(0, 2)
    def _(turn):
        some = pl.ds(pl.multiple_of(turn * (width // 2), LANES), width // 2)
        attended = dot(all_heads, head_rows(turn, slice(3 * cols, 5 * cols)), NT)
        block_ref[:, some] = (tokens[:, some].astype(F32) + attended + out_own[:, some].astype(F32) + out_got[:, some].astype(F32) + bias_ref[:, some]).astype(BF)

    tiny[0].wait_recv()
    t_x[...] = t_all[:, :, core] + t_core[...]
    group = []
    for s, peer in enumerate(along_x):
        group.append(remote(t_x.at[:, (x + s + 1) % wide], t_xgot.at[x], tsend.at[1 + s], trecv.at[1 + s], peer))
        group[s].start()
    tiny += group
    t_xgot[x] = t_x[:, x]
    over_y(2)
    over_z(4)
    for copy in group:
        copy.wait_recv()
    total = t_xgot[0]
    for xx in range(1, wide):
        total += t_xgot[xx]
    t_z[...] = total
    group = []
    for s, peer in enumerate(along_z):
        group.append(remote(t_z.at[(z + s + 1) % deep], t_zgot.at[z], tsend.at[wide + s], trecv.at[wide + s], peer))
        group[s].start()
    tiny += group
    t_zgot[z] = t_z[z]
    over_y(3)
    over_z(5)
    for copy in group:
        copy.wait_recv()
    total = t_zgot[0]
    for zz in range(1, deep):
        total += t_zgot[zz]
    t_y[...] = total
    tiny.append(remote(t_y.at[1 - y], t_ygot, tsend.at[wide + deep - 1], trecv.at[wide + deep - 1], partner))
    tiny[-1].start()
    for i in range(4):
        last(i)
    over_y(4)
    tiny[-1].wait_recv()
    small_ref[...] = t_y[y] + t_ygot[...]
    over_y(5)
    last(4)
    last(5)
    puts[0].wait()
    rows_copy[1].wait_recv()
    for copy in list(first.values()) + [c for group in list(second.values()) + list(third.values()) for c in group] + list(fourth.values()) + tiny + rows_copy:
        copy.wait_send()


def last_half(tokens, cotan, bias, gb, gains, kept, sums, batch):
    deep, wide = grid_of(batch)
    own_rows, width = tokens.shape
    rows = 2 * own_rows
    hidden = gb.shape[1]
    cols = hidden // 4
    block = hidden // 2
    shard = width // (2 * batch)
    slots = own_rows // PATCHES
    cuts = [(part, slice(at, at + block)) for part in range(3) for at in (0, block)]
    vm = pl.BlockSpec(memory_space=pltpu.VMEM)
    hbm = pl.BlockSpec(memory_space=pl.ANY)
    buf = lambda *shape: pltpu.VMEM(shape, BF)
    tile = lambda *lead: pltpu.VMEM(lead + TINY, F32)
    scratch = [buf(*k.shape) for k in kept]
    scratch += [buf(wide, deep, 2 * shard, hidden)] * 2
    scratch += [buf(deep, wide, 2, 2 * shard, hidden), buf(deep, wide, 2 * shard, hidden), buf(wide - 1, deep, 2 * shard, hidden)]
    scratch += [buf(deep, 2 * shard, hidden)] * 3 + [buf(deep - 1, 2 * shard, hidden)] * 3 + [buf(shard, hidden)] * 6
    scratch += [buf(rows, 3 * cols), buf(rows, cols), buf(slots * SLOT, cols)]
    scratch += [tile(deep, wide, 2, 2), tile(deep, wide, 2), tile(deep, wide, 2), tile(wide, deep, 2), tile(deep, 2), tile(deep, 2), tile(2), tile()]
    scratch += [pltpu.SemaphoreType.DMA((len(cuts), deep + wide))] * 2 + [pltpu.SemaphoreType.DMA((deep + wide + 2,))] * 2 + [pltpu.SemaphoreType.DMA((len(kept),)), pltpu.SemaphoreType.DMA((2 * wide,)), pltpu.SemaphoreType.DMA]
    full = lambda *shape: jax.ShapeDtypeStruct(shape, F32)
    low = jax.ShapeDtypeStruct((own_rows, width), BF)
    return pl.pallas_call(
        functools.partial(last_kernel, deep=deep, wide=wide, cuts=cuts),
        in_specs=[vm] * 5 + [hbm] * (len(kept) + 2 * wide),
        out_specs=[hbm] * 2 + [vm] * 6,
        out_shape=[low] * 3 + [full(3, shard, 2 * cols), full(shard, 2 * cols), full(shard, 2 * hidden), full(shard, 2 * hidden), full(*TINY)],
        scratch_shapes=scratch,
        compiler_params=pltpu.CompilerParams(collective_id=1, has_side_effects=True, vmem_limit_bytes=VMEM_CAP),
        name="head_gradients_and_scatter",
    )(tokens, cotan, bias, gb, gains, *kept, *sums)


def result_kernel(tokens, cotan, gain, dn_own, dn_got, block_in, qkv_in, wo_in, up_in, down_in, small, block, grad, qkv, wo, up, down, up_b, down_b, norm_g, query_g, key_g):
    vhat, scale = norm_stats(tokens[...].astype(F32))
    scaled = (dn_own[...].astype(F32) + dn_got[...].astype(F32)) * gain[...]
    d_tokens = (scaled - jnp.mean(scaled, axis=-1, keepdims=True) - vhat * jnp.mean(scaled * vhat, axis=-1, keepdims=True)) * scale
    grad[...] = (cotan[...].astype(F32) + d_tokens).astype(BF)
    block[...] = block_in[...]

    @pl.when(pl.program_id(0) == 0)
    def _():
        qkv[...] = qkv_in[...]
        wo[...] = wo_in[...]
        up[...] = up_in[...]
        down[...] = down_in[...]
        norm_g[...] = small[0:1, : norm_g.shape[1]]
        down_b[...] = small[1:2, : down_b.shape[1]]
        up_b[...] = small[2:3, : up_b.shape[1]]
        query_g[...] = small[3:4, :HD]
        key_g[...] = small[3:4, HD : 2 * HD]


def results(tokens, cotan, gain, dn_own, dn_got, block_in, sums, small, per):
    rows, width = tokens.shape
    chunk = rows // 2
    shard = sums[1].shape[0]
    blk = pl.BlockSpec((chunk, width), lambda j: (j, 0))
    whole = lambda shape: pl.BlockSpec(shape, lambda j: (0,) * len(shape))
    vectors = [(1, per), (1, shard), (1, shard), (1, HD), (1, HD)]
    return pl.pallas_call(
        result_kernel,
        grid=(rows // chunk,),
        in_specs=[blk, blk, whole(gain.shape), blk, blk, blk] + [whole(s.shape) for s in sums] + [whole(small.shape)],
        out_specs=[blk, blk] + [whole(s.shape) for s in sums] + [whole(v) for v in vectors],
        out_shape=[jax.ShapeDtypeStruct((rows, width), BF)] * 2 + [jax.ShapeDtypeStruct(s.shape, F32) for s in sums] + [jax.ShapeDtypeStruct(v, F32) for v in vectors],
        compiler_params=pltpu.CompilerParams(vmem_limit_bytes=VMEM_CAP),
        name="results",
    )(tokens, cotan, gain, dn_own, dn_got, block_in, *sums, small)


def local(tokens, cotangent, image_tokens, w_qkv, w_out, w_up, bias_up, w_down, bias_down, norm_gain, query_gain, key_gain):
    batch = lax.axis_size("batch")
    deep, wide = grid_of(batch)
    row = lambda v: v.reshape(1, -1)
    weights = (w_qkv, w_out.T, w_up, w_down.T)
    vectors = (row(norm_gain), row(bias_down), row(bias_up), row(query_gain), row(key_gain))
    made = first_half(tokens, cotangent, weights, vectors, batch)
    x_par, dy_par, normed, q, k, v, d_o, qraw, kraw, head_w, out_own, out_other, dn = made[:13]
    up_sums, down_sums = made[13 : 13 + wide], made[13 + wide : 13 + 2 * wide]
    gb, gain, bias, gains = made[13 + 2 * wide :]
    at = lambda z, x, c: (z * wide + x) * 2 + c

    def over_x(terms):
        return [terms[0]] + [lax.ppermute(terms[s], "batch", [(at(z, x, c), at(z, (x + s) % wide, c)) for z in range(deep) for x in range(wide) for c in range(2)]) for s in range(1, wide)]

    up_sums = over_x(up_sums)
    out_got = lax.ppermute(out_other, "branch", [(0, 1), (1, 0)])
    down_sums = over_x(down_sums)
    o, dq, dk, dv = attention(image_tokens[0], q, k, v, d_o)
    kept = [x_par, dy_par, normed, o, dq, dk, dv, qraw, kraw, head_w, out_own, out_got, dn]
    dn_own, dn_got, block_in, g_qkv, g_out, g_up, g_down, small = last_half(tokens, cotangent, bias, gb, gains, kept, up_sums + down_sums, batch)
    block_out, grad_tokens, g_qkv, g_out, g_up, g_down, g_up_b, g_down_b, g_norm, g_query, g_key = results(tokens, cotangent, gain, dn_own, dn_got, block_in, [g_qkv, g_out, g_up, g_down], small, bias_up.shape[0])
    flat = lambda v: v.reshape(-1)
    return (block_out, grad_tokens, g_qkv, g_out.T, g_up, flat(g_up_b), g_down.T, flat(g_down_b), flat(g_norm), flat(g_query), flat(g_key))


def solution(mesh):
    both = ("batch", "branch")
    in_specs = (P(both, None), P(both, None), P("batch", None), P(None, both, None), P(None, both), P(both, None), P(both), P(None, both), P(both), P(both), P(), P())
    out_specs = (P(both, None), P(both, None), P(None, both, None), P(None, both), P(both, None), P(both), P(None, both), P(both), P(both), P(), P())
    return jax.shard_map(local, mesh=mesh, in_specs=in_specs, out_specs=out_specs, check_vma=False)
```

```python
import functools
import jax
import jax.numpy as jnp
from jax import lax
from jax.experimental import pallas as pl
from jax.experimental.pallas import tpu as pltpu
from jax.sharding import PartitionSpec as P

HD = 64
LANES = 128
NORM_EPS = 1e-06
LONGEST = 784
PATCHES = 196
SLOT = 208
VMEM_CAP = 66_000_000
BF = jnp.bfloat16
F32 = jnp.float32


def dot(a, b, dims=((1,), (0,))):
    return lax.dot_general(a, b, (dims, ((), ())), preferred_element_type=F32)


NT = ((1,), (1,))
TN = ((0,), (0,))


def norm_stats(values):
    centred = values - jnp.mean(values, axis=-1, keepdims=True)
    spread = jnp.mean(centred * centred, axis=-1, keepdims=True)
    scale = lax.rsqrt(spread + NORM_EPS)
    return centred * scale, scale


def head_means(values, ones_low):
    means = []
    for at in range(0, values.shape[1], LANES):
        some = values[:, at : at + LANES]
        high = some.astype(BF)
        low = (some - high.astype(F32)).astype(BF)
        means.append(dot(jnp.concatenate([high, low], axis=1), ones_low))
    return jnp.concatenate(means, axis=1)


def head_ones():
    row = lax.broadcasted_iota(jnp.int32, (2 * LANES, LANES), 0) % LANES // HD
    col = lax.broadcasted_iota(jnp.int32, (2 * LANES, LANES), 1) // HD
    return jnp.where(row == col, 1.0 / HD, 0.0).astype(BF)


def head_stats(raw, ones_low):
    centred = raw - head_means(raw, ones_low)
    scale = lax.rsqrt(head_means(centred * centred, ones_low) + NORM_EPS)
    return centred * scale, scale


MESH = pl.DeviceIdType.MESH


def place():
    return lax.axis_index("batch"), lax.axis_index("branch")


def grid_of(batch):
    chips = batch // 2
    across = 1
    while across * across * 4 <= chips:
        across *= 2
    return chips // across, across


def greet(peers):
    barrier = pltpu.get_barrier_semaphore()
    for peer in peers:
        pl.semaphore_signal(barrier, inc=1, device_id=peer, device_id_type=MESH)
    pl.semaphore_wait(barrier, len(peers))


def neighbours(deep, wide):
    batch, branch = place()
    core, x, z = batch % 2, (batch // 2) % wide, batch // (2 * wide)
    at = lambda zz, xx, cc: (zz * wide + xx) * 2 + cc
    partner = (batch, 1 - branch)
    along_z = [(at((z + s) % deep, x, core), branch) for s in range(1, deep)]
    along_x = [(at(z, (x + s) % wide, core), branch) for s in range(1, wide)]
    sibling = (at(z, x, 1 - core), branch)
    return (z, x, core, branch), partner, along_z, along_x, sibling


def remote(src, dst, send, recv, peer):
    return pltpu.make_async_remote_copy(src_ref=src, dst_ref=dst, send_sem=send, recv_sem=recv, device_id=peer, device_id_type=MESH)


TINY = (8, LANES)
STRIP = 112


def gelu_parts(hidden):
    square = hidden * hidden
    tanh = jnp.tanh(hidden * (0.7978845608028654 + 0.035677408136300125 * square))
    half = 0.5 + 0.5 * tanh
    act = hidden * half
    slope = half + (act * (1.0 - tanh)) * (0.7978845608028654 + 0.1070322244089 * square)
    return act.astype(BF), slope


def repeated(values, count):
    return jnp.concatenate([values] * count, axis=1)


def first_kernel(*refs, deep, wide, cuts, block):
    tokens, cotan, qkv_ref, wo_ref, up_ref, down_ref, nb_ref, db_ref, ub_ref, qg_ref, kg_ref = refs[:11]
    o_x, o_dy, o_normed, o_q, o_k, o_v, o_do, o_qraw, o_kraw, o_heads, o_own, o_other, o_dn = refs[11:24]
    o_sums = (refs[24 : 24 + wide], refs[24 + wide : 24 + 2 * wide])
    gb_ref, gain_ref, bias_ref, tiny = refs[24 + 2 * wide : 28 + 2 * wide]
    scratch = refs[28 + 2 * wide :]
    packs, lands, wires = scratch[:3], scratch[3:6], scratch[6:9]
    rounded, tiny_all, x_par, dy_par, normed, act, d_hid, s_q, s_k, s_v, s_do, s_qraw, s_kraw, s_out, s_dn = scratch[9:24]
    grads, got_core, flats = scratch[24:26], scratch[26:28], scratch[28:31]
    send, recv, tsend, trecv, csend, crecv, osem = scratch[31:]
    (z, x, core, y), partner, along_z, along_x, sibling = neighbours(deep, wide)
    batch = 2 * deep * wide
    own_rows, width = tokens.shape
    shard, hidden = packs[0].shape[1:]
    cols = hidden // 4
    pair = 2 * shard
    direct = pair % 16 == 0
    places = [(b // (2 * wide), (b // 2) % wide, b % 2, s) for b in range(batch) for s in range(2)]

    for half in range(2):
        some = slice(half * cols, (half + 1) * cols)
        packs[0][half] = up_ref[:, half * hidden : (half + 1) * hidden].astype(BF)
        packs[1][half] = down_ref[:, half * hidden : (half + 1) * hidden].astype(BF)
        for at in range(3):
            packs[2][half, :, at * cols : (at + 1) * cols] = qkv_ref[at, :, some].astype(BF)
        packs[2][half, :, 3 * cols :] = wo_ref[...].astype(BF)
    rounded[...] = jnp.zeros(TINY, BF)
    for row, ref in enumerate((nb_ref, db_ref, ub_ref, qg_ref, kg_ref)):
        rounded[row : row + 1, : ref.shape[1]] = ref[...].astype(BF)
    tiny[...] = rounded[...].astype(F32)
    tiny_all[z, x, core, y] = tiny[...]
    greet([partner, sibling] + along_z + along_x)
    outs = []

    def put(src, dst):
        copy = pltpu.make_async_copy(src, dst, osem.at[len(outs)])
        copy.start()
        outs.append(copy)

    spread_tiny = [remote(tiny, tiny_all.at[z, x, core, y], tsend.at[0], trecv.at[0], partner)]
    spread_tiny[0].start()
    over_y = []
    for i, (part, at) in enumerate(cuts):
        over_y.append(remote(packs[part].at[1 - y, :, at], lands[part].at[:, at], send.at[i, 0], recv.at[i, 0], partner))
        over_y[i].start()
    rows_copy = [remote(tokens, x_par, tsend.at[deep + wide], trecv.at[deep + wide], partner), remote(cotan, dy_par, tsend.at[deep + wide + 1], trecv.at[deep + wide + 1], partner)]
    for copy in rows_copy:
        copy.start()

    def tiny_stage(block, peers, first):
        group = [remote(block, block, tsend.at[first + s], trecv.at[first + s], peer) for s, peer in enumerate(peers)]
        for copy in group:
            copy.start()
        for copy in group:
            copy.wait_recv()
        spread_tiny.extend(group)

    over_z, over_x, over_core = [], [], []

    def start_z(i):
        part, at = cuts[i]
        over_y[i].wait_recv()
        mine, other = packs[part][y, :, at].astype(F32), lands[part][:, at].astype(F32)
        pair = jnp.concatenate([jnp.where(y == 0, mine, other), jnp.where(y == 0, other, mine)], axis=0)
        wires[part][z, x, core, :, at] = pair.astype(BF)
        block = wires[part].at[z, x, core, :, at]
        over_z.append([remote(block, block, send.at[i, 1 + s], recv.at[i, 1 + s], peer) for s, peer in enumerate(along_z)])
        for copy in over_z[i]:
            copy.start()

    def start_x(i):
        part, at = cuts[i]
        for copy in over_z[i]:
            copy.wait_recv()
        block = wires[part].at[:, x, core, :, at]
        over_x.append([remote(block, block, send.at[i, deep + s], recv.at[i, deep + s], peer) for s, peer in enumerate(along_x)])
        for copy in over_x[i]:
            copy.start()

    def start_core(i):
        part, at = cuts[i]
        for copy in over_x[i]:
            copy.wait_recv()
        block = wires[part].at[:, :, core, :, at]
        over_core.append(remote(block, block, send.at[i, deep + wide - 1], recv.at[i, deep + wide - 1], sibling))
        over_core[i].start()

    def arrive(i):
        part, at = cuts[i]
        over_core[i].wait_recv()
        if not direct:
            for b in range(batch):
                flats[part][2 * shard * b : 2 * shard * (b + 1), at] = wires[part][b // (2 * wide), (b // 2) % wide, b % 2, :, at]

    def weight(part, at):
        if direct:
            value = wires[part][:, :, :, :, at]
            return value.reshape(width, value.shape[-1])
        return flats[part][:, at]

    for i in range(len(cuts)):
        start_z(i)
        if i == 0:
            spread_tiny[0].wait_recv()
            tiny_stage(tiny_all.at[z, x, core], along_z, 1)
        if i == 1:
            tiny_stage(tiny_all.at[:, x, core], along_x, deep)
        if i == 2:
            tiny_stage(tiny_all.at[:, :, core], [sibling], deep + wide - 1)
    per = ub_ref.shape[1]
    gain_ref[...] = jnp.concatenate([tiny_all[p][0:1, :shard] for p in places], axis=1)
    bias_ref[...] = jnp.concatenate([tiny_all[p][1:2, :shard] for p in places], axis=1)
    low_b = jnp.concatenate([tiny_all[p][2:3, :per] for p in places[:batch]], axis=1)
    high_b = jnp.concatenate([tiny_all[p][2:3, :per] for p in places[batch:]], axis=1)
    gb_ref[...] = jnp.where(y == 0, low_b, high_b)

    sides = ((tokens, cotan, slice(0, own_rows)), (x_par, dy_par, slice(own_rows, 2 * own_rows)))

    def normalise(side):
        @pl.loop(0, own_rows // STRIP)
        def _(turn):
            strip = pl.ds(pl.multiple_of(turn * STRIP, 16), STRIP)
            vhat, _ = norm_stats(sides[side][0][strip, :].astype(F32))
            normed[pl.ds(pl.multiple_of(side * own_rows + turn * STRIP, 16), STRIP), :] = (vhat * gain_ref[...]).astype(BF)

    def expand(side, at, back):
        rows = sides[side][2]

        turns = 3 if back else 12

        @pl.loop(0, turns)
        def _(turn):
            size = (at.stop - at.start) // turns
            some = pl.ds(pl.multiple_of(at.start + turn * size, LANES), size)
            act[rows, some], slope = gelu_parts(dot(normed[rows, :], weight(0, some)) + gb_ref[:, some])
            if back:
                slope *= dot(sides[side][1][...], weight(1, some))
            d_hid[rows, some] = slope.astype(BF)

    def apply_back(side):
        rows = sides[side][2]

        @pl.loop(0, 2)
        def _(turn):
            at = pl.ds(pl.multiple_of(turn * block, LANES), block)
            d_hid[rows, at] = (d_hid[rows, at].astype(F32) * dot(sides[side][1][...], weight(1, at))).astype(BF)

    def contract(side, low, kept, part):
        rows = sides[side][2]
        size = width // 2

        @pl.loop(0, 2)
        def _(turn):
            if direct:
                value = wires[part][pl.ds(turn * (deep // 2), deep // 2)].reshape(size, hidden)
            else:
                value = flats[part][pl.ds(pl.multiple_of(turn * size, 16), size), :]
            kept[rows, pl.ds(pl.multiple_of(turn * size, LANES), size)] = dot(low[rows, :], value, NT).astype(BF)

    def place_rows(base, ref, values):
        for at in range(own_rows // PATCHES):
            ref[pl.ds(pl.multiple_of((base + at) * SLOT, 16), PATCHES), :] = values[at * PATCHES : (at + 1) * PATCHES].astype(BF)

    def queries_keys():
        ones_low = head_ones()

        @pl.loop(0, 2)
        def _(side):
            rows = pl.ds(pl.multiple_of(side * own_rows, 16), own_rows)
            base = jnp.where(side == 0, y, 1 - y) * (own_rows // PATCHES)
            for at, (raw_ref, low_ref, gain) in enumerate(((s_qraw, s_q, 3), (s_kraw, s_k, 4))):
                raw = dot(normed[rows, :], weight(2, slice(at * cols, (at + 1) * cols)))
                raw_ref[rows, :] = raw.astype(BF)
                hat, _ = head_stats(raw, ones_low)
                place_rows(base, low_ref, hat * repeated(tiny[gain : gain + 1, :HD], cols // HD))

    def values_of():
        @pl.loop(0, 2)
        def _(side):
            rows = pl.ds(pl.multiple_of(side * own_rows, 16), own_rows)
            place_rows(jnp.where(side == 0, y, 1 - y) * (own_rows // PATCHES), s_v, dot(normed[rows, :], weight(2, slice(2 * cols, 3 * cols))))

    def back_of(side):
        place_rows((y if side == 0 else 1 - y) * (own_rows // PATCHES), s_do, dot(sides[side][1][...], weight(2, pl.ds(pl.multiple_of((3 + y) * cols, LANES), cols))))

    over_sib = []

    def grad_own(part):
        rows = sides[0][2]

        @pl.loop(0, 6)
        def _(turn):
            size = hidden // 6
            some = pl.ds(pl.multiple_of(turn * size, LANES), size)
            value = dot(normed[rows, :], d_hid[rows, some], TN) if part == 0 else dot(cotan[...], act[rows, some], TN)
            for b in range(batch):
                grads[part][b // (2 * wide), (b // 2) % wide, b % 2, :, some] = value[b * pair : (b + 1) * pair].astype(BF)

    def grad_rest(part, at):
        rows = sides[1][2]

        @pl.loop(0, 2)
        def _(turn):
            size = (at.stop - at.start) // 2
            some = pl.ds(pl.multiple_of(at.start + turn * size, LANES), size)
            value = dot(normed[rows, :], d_hid[rows, some], TN) if part == 0 else dot(dy_par[...], act[rows, some], TN)
            for b in range(batch):
                block_at = (b // (2 * wide), (b // 2) % wide, b % 2, slice(None), some)
                grads[part][block_at] = (grads[part][block_at].astype(F32) + value[b * pair : (b + 1) * pair]).astype(BF)

        i = len(over_sib)
        over_sib.append(remote(grads[part].at[:, :, 1 - core, :, at], got_core[part].at[:, :, :, at], csend.at[i], crecv.at[i], sibling))
        over_sib[i].start()

    def add_core(i, part, at):
        over_sib[i].wait_recv()

        @pl.loop(0, deep)
        def _(zz):
            for xx in range(wide):
                total = grads[part][zz, xx, core, :, at].astype(F32) + got_core[part][zz, xx, :, at].astype(F32)
                got_core[part][zz, xx, :, at] = total.astype(BF)

    first, second = slice(0, block), slice(block, 2 * block)
    start_x(0)
    normalise(0)
    start_x(1)
    start_core(0)
    start_x(2)
    start_core(1)
    arrive(0)
    arrive(1)
    expand(0, first, True)
    start_x(3)
    start_core(2)
    rows_copy[0].wait_recv()
    normalise(1)
    put(x_par, o_x)
    put(normed, o_normed)
    start_x(4)
    start_core(3)
    arrive(2)
    arrive(3)
    expand(0, second, True)
    start_core(4)
    expand(1, slice(0, hidden), False)
    start_x(5)
    contract(0, act, s_out, 1)
    start_x(6)
    contract(0, d_hid, s_dn, 0)
    grad_own(0)
    start_core(5)
    grad_own(1)
    contract(1, act, s_out, 1)
    put(s_out.at[pl.ds(0, own_rows)], o_own)
    put(s_out.at[pl.ds(own_rows, own_rows)], o_other)
    arrive(4)
    start_core(6)
    queries_keys()
    for src, dst in ((s_q, o_q), (s_k, o_k), (s_qraw, o_qraw), (s_kraw, o_kraw)):
        put(src, dst)
    arrive(5)
    arrive(6)
    put(wires[2] if direct else flats[2], o_heads)
    values_of()
    put(s_v, o_v)
    back_of(0)
    rows_copy[1].wait_recv()
    put(dy_par, o_dy)
    back_of(1)
    put(s_do, o_do)
    apply_back(1)
    contract(1, d_hid, s_dn, 0)
    put(s_dn, o_dn)
    grad_rest(0, first)
    grad_rest(0, second)
    add_core(0, 0, first)
    grad_rest(1, first)
    add_core(1, 0, second)
    for s in range(wide):
        put(got_core[0].at[:, (x + s) % wide], o_sums[0][s])
    grad_rest(1, second)
    add_core(2, 1, first)

    @pl.loop(0, 6)
    def _(turn):
        some = pl.ds(pl.multiple_of(turn * (hidden // 6), LANES), hidden // 6)
        gb_ref[:, some] = dot(jnp.ones((8, 2 * own_rows), BF), d_hid[:, some])[:1]

    add_core(3, 1, second)
    for s in range(wide):
        put(got_core[1].at[:, (x + s) % wide], o_sums[1][s])
    for copy in outs:
        copy.wait()
    for copy in spread_tiny + over_y + rows_copy + [c for group in over_z + over_x for c in group] + over_core + over_sib:
        copy.wait_send()


def first_half(tokens, cotan, weights, vectors, batch):
    deep, wide = grid_of(batch)
    own_rows, width = tokens.shape
    shard, hidden = weights[2].shape[0], weights[2].shape[1] // 2
    cols = hidden // 4
    block = hidden // 2
    rows = 2 * own_rows
    spread_rows = rows // PATCHES * SLOT
    widths = (hidden, hidden, 5 * cols)
    first, second = slice(0, block), slice(block, hidden)
    cuts = [(0, first), (1, first), (0, second), (1, second), (2, slice(0, 2 * cols)), (2, slice(3 * cols, 5 * cols)), (2, slice(2 * cols, 3 * cols))]
    vm = pl.BlockSpec(memory_space=pltpu.VMEM)
    hbm = pl.BlockSpec(memory_space=pl.ANY)
    direct = (2 * shard) % 16 == 0
    wire_shapes = [(deep, wide, 2, 2 * shard, w) for w in widths]
    flat_shapes = [(width, w) for w in widths]
    low = lambda *shape: jax.ShapeDtypeStruct(shape, BF)
    outs = [low(own_rows, width)] * 2 + [low(rows, width)] + [low(spread_rows, cols)] * 4 + [low(rows, cols)] * 2
    outs += [low(*(wire_shapes if direct else flat_shapes)[2])] + [low(own_rows, width)] * 2 + [low(rows, width)] + [low(deep, 2 * shard, hidden)] * (2 * wide)
    tiny_outs = [jax.ShapeDtypeStruct((1, hidden), F32), jax.ShapeDtypeStruct((1, width), F32), jax.ShapeDtypeStruct((1, width), F32), jax.ShapeDtypeStruct(TINY, F32)]
    buf = lambda *shape: pltpu.VMEM(shape, BF)
    scratch = [buf(2, shard, w) for w in widths] + [buf(shard, w) for w in widths] + [buf(*s) for s in wire_shapes]
    scratch += [buf(*TINY), pltpu.VMEM((deep, wide, 2, 2) + TINY, F32), buf(own_rows, width), buf(own_rows, width), buf(rows, width), buf(rows, hidden), buf(rows, hidden)]
    scratch += [buf(spread_rows, cols)] * 4 + [buf(rows, cols)] * 2 + [buf(rows, width)] * 2
    scratch += [buf(deep, wide, 2, 2 * shard, hidden)] * 2 + [buf(deep, wide, 2 * shard, hidden)] * 2
    scratch += [buf(16, LANES) if direct else buf(*s) for s in flat_shapes]
    scratch += [pltpu.SemaphoreType.DMA((len(cuts), deep + wide))] * 2 + [pltpu.SemaphoreType.DMA((deep + wide + 2,))] * 2 + [pltpu.SemaphoreType.DMA((4,))] * 2 + [pltpu.SemaphoreType.DMA((len(outs),))]
    return pl.pallas_call(
        functools.partial(first_kernel, deep=deep, wide=wide, cuts=cuts, block=block),
        in_specs=[vm] * 11,
        out_specs=[hbm] * len(outs) + [vm] * 4,
        out_shape=outs + tiny_outs,
        scratch_shapes=scratch,
        compiler_params=pltpu.CompilerParams(collective_id=0, has_side_effects=True, vmem_limit_bytes=VMEM_CAP),
        name="gather_and_feed_forward",
    )(tokens, cotan, *weights, *vectors)


def load_rows(ref, block, blocks):
    parts = [ref[pl.ds(pl.multiple_of((block + at) * SLOT, 16), PATCHES), :] for at in range(blocks)]
    return parts[0] if blocks == 1 else jnp.concatenate([p.astype(F32) for p in parts], axis=0).astype(BF)

def attend_pair(pair_q, pair_k, pair_v, pair_do, pieces):
    count = pair_q.shape[0]
    lane = lax.broadcasted_iota(jnp.int32, (count, 2 * HD), 1)
    pair_q = pair_q * jnp.asarray(0.125, BF)
    zero = jnp.zeros_like(pair_q)
    v_t, k_t = pair_v.T, pair_k.T
    mixed, grads_q, grad_k, grad_v = [], [], None, None
    for head in range(2):
        mine = (lane < HD) if head == 0 else (lane >= HD)
        q_m, do_m = jnp.where(mine, pair_q, zero), jnp.where(mine, pair_do, zero)
        part = slice(head * HD, (head + 1) * HD)
        outs, gqs = [], []
        for first, size in pieces:
            q, d_o = q_m[first : first + size], do_m[first : first + size]
            shifted = jnp.exp(dot(pair_k, q, NT))
            total = jnp.sum(shifted, axis=0, keepdims=True)
            weights = shifted * (1.0 / total)
            low = weights.astype(BF)
            d_weights = dot(pair_v, d_o, NT)
            inner = jnp.sum(weights * d_weights, axis=0, keepdims=True)
            d_scores = (weights * (d_weights - inner)).astype(BF)
            outs.append(dot(v_t[part], low))
            gqs.append(dot(k_t[part], d_scores))
            gv, gk = dot(low, d_o), dot(d_scores, q)
            grad_v = gv if grad_v is None else grad_v + gv
            grad_k = gk if grad_k is None else grad_k + gk
        join = lambda parts: parts[0] if len(parts) == 1 else jnp.concatenate(parts, axis=1)
        mixed.append(join(outs))
        grads_q.append(join(gqs))
    turn = lambda parts: jnp.concatenate(parts, axis=0).T
    return turn(mixed), turn(grads_q) * 0.125, grad_k, grad_v

def attention_kernel(count_ref, *refs, pieces, together):
    ins, outs, (small_ref,) = refs[:4], refs[4:8], refs[8:]
    place, smalls, bigs, big_at = 0, 0, 0, 0
    for slot in range(count_ref.shape[0]):
        count = count_ref[slot]
        is_small = (count == PATCHES).astype(jnp.int32)
        is_big = (count == LONGEST).astype(jnp.int32)
        small_ref[smalls] = place
        big_at = jnp.where(is_big == 1, place, big_at)
        smalls, bigs = smalls + is_small, bigs + is_big
        place = place + is_small + (LONGEST // PATCHES) * is_big

    def images(firsts, blocks, pieces):
        loaded = [[load_rows(ref, block, blocks) for ref in ins] for block in firsts]
        results = [attend_pair(*values, pieces) for values in loaded]
        for block, result in zip(firsts, results):
            for ref, values in zip(outs, result):
                for at in range(blocks):
                    ref[pl.ds(pl.multiple_of((block + at) * SLOT, 16), PATCHES), :] = values[at * PATCHES : (at + 1) * PATCHES].astype(ref.dtype)

    @pl.when(bigs > 0)
    def _():
        images([big_at], LONGEST // PATCHES, pieces)

    @pl.loop(0, smalls // together)
    def _(turn):
        images([small_ref[turn * together + at] for at in range(together)], 1, ((0, PATCHES),))

def attention(counts, q, k, v, d_o, pieces=((0, 784),), together=4):
    rows, cols = q.shape
    sm = pl.BlockSpec(memory_space=pltpu.SMEM)
    blk = pl.BlockSpec((rows, 2 * HD), lambda j: (0, j))
    return pl.pallas_call(
        functools.partial(attention_kernel, pieces=pieces, together=together),
        grid=(cols // (2 * HD),),
        in_specs=[sm] + [blk] * 4,
        out_specs=[blk] * 4,
        out_shape=[jax.ShapeDtypeStruct((rows, cols), t) for t in (BF, BF, BF, BF)],
        scratch_shapes=[pltpu.SMEM((counts.shape[0] + 1,), jnp.int32)],
        compiler_params=pltpu.CompilerParams(vmem_limit_bytes=VMEM_CAP),
        cost_estimate=pl.CostEstimate(flops=20_000_000_000, bytes_accessed=20_000_000, transcendentals=rows * LONGEST * cols // HD),
        name="attention",
    )(counts, q, k, v, d_o)


def last_kernel(*refs, deep, wide, cuts):
    tokens, cotan, bias_ref, gb_ref, gains_ref = refs[:5]
    i_x, i_dy, i_normed, i_o, i_dq, i_dk, i_dv, i_qraw, i_kraw, i_heads, i_own, i_got, i_dn = refs[5:18]
    i_sums = (refs[18 : 18 + wide], refs[18 + wide : 18 + 2 * wide])
    o_dn, o_dn_got, block_ref, qkv_ref, wo_ref, up_ref, down_ref, small_ref = refs[18 + 2 * wide : 26 + 2 * wide]
    scratch = refs[26 + 2 * wide :]
    x_par, dy_par, normed, s_o, s_dq, s_dk, s_dv, qraw, kraw, head_w, out_own, out_got, dn = scratch[:13]
    terms = scratch[13:15]
    mine, got_core, got_x = scratch[15:18]
    to_z, got_z, to_y, got_y = (scratch[18 + 3 * i : 21 + 3 * i] for i in range(4))
    d_proj, mixed, o_got = scratch[30:33]
    t_all, t_core, t_x, t_xgot, t_z, t_zgot, t_y, t_ygot = scratch[33:41]
    send, recv, tsend, trecv, lsem, gsem, osem = scratch[41:]
    (z, x, core, y), partner, along_z, along_x, sibling = neighbours(deep, wide)
    batch = 2 * deep * wide
    own_rows, width = tokens.shape
    rows = 2 * own_rows
    cols = qraw.shape[1]
    shard = to_y[0].shape[0]
    slots = own_rows // PATCHES
    places = [(b // (2 * wide), (b // 2) % wide, b % 2, s) for b in range(batch) for s in range(2)]
    own, other = slice(0, own_rows), slice(own_rows, rows)
    greet([partner, sibling] + along_z + along_x)

    theirs = pl.ds(pl.multiple_of((1 - y) * slots * SLOT, 16), slots * SLOT)
    rows_copy = [remote(i_o.at[theirs], o_got, tsend.at[deep + wide], trecv.at[deep + wide], partner)]
    rows_copy[0].start()
    held = {}
    for part in range(2):
        for s in range(wide):
            held[part, s] = pltpu.make_async_copy(i_sums[part][s], terms[part].at[s], gsem.at[part * wide + s])
            held[part, s].start()
    loads = {}
    for at, (name, src, dst) in enumerate((("qraw", i_qraw, qraw), ("dq", i_dq, s_dq), ("kraw", i_kraw, kraw), ("dk", i_dk, s_dk), ("dv", i_dv, s_dv), ("heads", i_heads, head_w), ("dn", i_dn, dn), ("normed", i_normed, normed), ("o", i_o, s_o), ("dy", i_dy, dy_par), ("x", i_x, x_par), ("own", i_own, out_own), ("got", i_got, out_got))):
        loads[name] = pltpu.make_async_copy(src, dst, lsem.at[at])
        loads[name].start()

    first, second, third, fourth = {}, {}, {}, {}

    def over_core(i):
        part, at = cuts[i]
        first[i] = remote(mine.at[:, :, 1 - core, :, at], got_core.at[:, :, :, at], send.at[i, 0], recv.at[i, 0], sibling)
        first[i].start()

    def over_x(i):
        part, at = cuts[i]
        first[i].wait_recv()

        @pl.loop(0, deep)
        def _(zz):
            for xx in range(wide):
                got_core[zz, xx, :, at] = (mine[zz, xx, core, :, at].astype(F32) + got_core[zz, xx, :, at].astype(F32)).astype(BF)

        second[i] = []
        for s, peer in enumerate(along_x):
            copy = remote(got_core.at[:, (x + s + 1) % wide, :, at], got_x.at[s, :, :, at], send.at[i, 1 + s], recv.at[i, 1 + s], peer)
            copy.start()
            second[i].append(copy)

    def over_z(i):
        part, at = cuts[i]
        if part == 2:
            for copy in second[i]:
                copy.wait_recv()

        @pl.loop(0, deep)
        def _(zz):
            if part == 2:
                total = got_core[zz, x, :, at].astype(F32)
                for s in range(wide - 1):
                    total += got_x[s, zz, :, at].astype(F32)
            else:
                total = terms[part][0, zz, :, at].astype(F32)
                for s in range(1, wide):
                    total += terms[part][s, zz, :, at].astype(F32)
            to_z[part][zz, :, at] = total.astype(BF)

        third[i] = []
        for s, peer in enumerate(along_z):
            copy = remote(to_z[part].at[(z + s + 1) % deep, :, at], got_z[part].at[s, :, at], send.at[i, wide + s], recv.at[i, wide + s], peer)
            copy.start()
            third[i].append(copy)

    def over_y(i):
        part, at = cuts[i]
        for copy in third[i]:
            copy.wait_recv()
        total = to_z[part][z, :, at].astype(F32)
        for s in range(deep - 1):
            total += got_z[part][s, :, at].astype(F32)
        low, high = total[:shard], total[shard:]
        to_y[part][:, at] = jnp.where(y == 0, high, low).astype(BF)
        fourth[i] = remote(to_y[part].at[:, at], got_y[part].at[:, at], send.at[i, wide + deep - 1], recv.at[i, wide + deep - 1], partner)
        fourth[i].start()
        deliver(part, y, at, jnp.where(y == 0, low, high))

    def deliver(part, half, at, values):
        if part < 2:
            ref = (up_ref, down_ref)[part]
            ref[:, pl.ds(pl.multiple_of(half * 4 * cols + at.start, LANES), at.stop - at.start)] = values
            return
        for piece in range(at.start // cols, at.stop // cols):
            some = values[:, piece * cols - at.start : (piece + 1) * cols - at.start]
            lanes = pl.ds(pl.multiple_of(half * cols, LANES), cols)
            if piece < 3:
                qkv_ref[piece, :, lanes] = some
            else:
                wo_ref[:, lanes] = some

    def last(i):
        part, at = cuts[i]
        fourth[i].wait_recv()
        deliver(part, 1 - y, at, got_y[part][:, at].astype(F32))

    def compact_rows(ref, base):
        parts = [ref[pl.ds(pl.multiple_of((base + at) * SLOT, 16), PATCHES), :].astype(F32) for at in range(slots)]
        return jnp.concatenate(parts, axis=0)

    bases = (y * slots, (1 - y) * slots)

    def head_rows(turn, at):
        if len(head_w.shape) > 2:
            value = head_w[pl.ds(turn * (deep // 2), deep // 2), :, :, :, at]
            return value.reshape(width // 2, value.shape[-1])
        return head_w[pl.ds(pl.multiple_of(turn * (width // 2), 16), width // 2), at]

    for part in range(2):
        for s in range(wide):
            held[part, s].wait()
    for i in range(4):
        over_z(i)
    ones_low = head_ones()
    gains = []
    for names, grad_in, raw_ref, gain, at in ((("dq", "qraw"), s_dq, qraw, 3, 0), (("dk", "kraw"), s_dk, kraw, 4, 1)):
        for name in names:
            loads[name].wait()

        def one_side(side, total):
            part = pl.ds(pl.multiple_of(side * own_rows, 16), own_rows)
            hat, scale = head_stats(raw_ref[part, :].astype(F32), ones_low)
            grad = compact_rows(grad_in, jnp.where(side == 0, *bases))
            scaled = grad * repeated(gains_ref[gain : gain + 1, :HD], cols // HD)
            d_raw = (scaled - head_means(scaled, ones_low) - hat * head_means(scaled * hat, ones_low)) * scale
            d_proj[part, at * cols : (at + 1) * cols] = d_raw.astype(BF)
            return total + jnp.sum(grad * hat, axis=0, keepdims=True)

        total = lax.fori_loop(0, 2, one_side, jnp.zeros((1, cols), F32))
        folded = total[:, :HD]
        for head in range(1, cols // HD):
            folded += total[:, head * HD : (head + 1) * HD]
        gains.append(folded)
    loads["dv"].wait()

    @pl.loop(0, 2)
    def _(side):
        d_proj[pl.ds(pl.multiple_of(side * own_rows, 16), own_rows), 2 * cols : 3 * cols] = compact_rows(s_dv, jnp.where(side == 0, *bases)).astype(BF)

    loads["dn"].wait()
    loads["heads"].wait()

    def add_dn(part):
        size = width // 2

        @pl.loop(0, 2)
        def _(turn):
            some = pl.ds(pl.multiple_of(turn * size, LANES), size)
            dn[part, some] = (dn[part, some].astype(F32) + dot(d_proj[part, :], head_rows(turn, slice(0, 3 * cols)), NT)).astype(BF)

    add_dn(other)
    rows_copy.append(remote(dn.at[pl.ds(own_rows, own_rows)], o_dn_got, tsend.at[deep + wide + 1], trecv.at[deep + wide + 1], partner))
    rows_copy[1].start()

    def keep(at, values):
        for b in range(batch):
            mine[b // (2 * wide), (b // 2) % wide, b % 2, :, at] = values[2 * b * shard : 2 * (b + 1) * shard].astype(BF)

    loads["normed"].wait()

    @pl.loop(0, 3)
    def _(piece):
        at = pl.ds(pl.multiple_of(piece * cols, LANES), cols)
        keep(at, dot(normed[...], d_proj[:, at], TN))

    over_core(4)
    loads["o"].wait()
    loads["dy"].wait()

    @pl.loop(0, 2)
    def _(side):
        mixed[pl.ds(pl.multiple_of(side * own_rows, 16), own_rows), :] = compact_rows(s_o, jnp.where(side == 0, *bases)).astype(BF)

    over_y(0)
    over_x(4)
    keep(slice(3 * cols, 4 * cols), dot(cotan[...], mixed[own, :], TN) + dot(dy_par[...], mixed[other, :], TN))
    over_core(5)
    add_dn(own)
    puts = [pltpu.make_async_copy(dn.at[pl.ds(0, own_rows)], o_dn, osem)]
    puts[0].start()
    over_x(5)
    over_y(1)
    loads["x"].wait()
    grad_g = jnp.zeros((1, width), F32)
    for side, ref in enumerate((tokens, x_par)):

        def one_strip(turn, total):
            vhat, _ = norm_stats(ref[pl.ds(pl.multiple_of(turn * STRIP, 16), STRIP), :].astype(F32))
            some = dn[pl.ds(pl.multiple_of(side * own_rows + turn * STRIP, 16), STRIP), :].astype(F32)
            return total + jnp.sum(some * vhat, axis=0, keepdims=True)

        grad_g = lax.fori_loop(0, own_rows // STRIP, one_strip, grad_g)

    def add_strip(turn, total):
        return total + jnp.sum(cotan[pl.ds(pl.multiple_of(turn * STRIP, 16), STRIP), :].astype(F32), axis=0, keepdims=True)

    grad_db = lax.fori_loop(0, own_rows // STRIP, add_strip, jnp.zeros((1, width), F32))
    per = gb_ref.shape[1] // batch
    both = jnp.concatenate(gains, axis=1)
    bias = gb_ref[...]
    t_all[...] = jnp.zeros(t_all.shape, F32)
    for b, (zz, xx, cc, s) in enumerate(places):
        inside = jnp.where(y == b // batch, 1.0, 0.0)
        t_all[zz, xx, cc, s, 0:1, :shard] = grad_g[:, b * shard : (b + 1) * shard]
        t_all[zz, xx, cc, s, 1:2, :shard] = grad_db[:, b * shard : (b + 1) * shard]
        t_all[zz, xx, cc, s, 2:3, :per] = bias[:, (b % batch) * per : (b % batch + 1) * per] * inside
        t_all[zz, xx, cc, s, 3:4, : 2 * HD] = both
    tiny = [remote(t_all.at[:, :, 1 - core], t_core, tsend.at[0], trecv.at[0], sibling)]
    tiny[0].start()
    for name in ("own", "got"):
        loads[name].wait()
    rows_copy[0].wait_recv()
    mixed_got = compact_rows(o_got, 0).astype(BF)
    mixed_own = mixed[own, :]
    all_heads = jnp.concatenate([jnp.where(y == 0, mixed_own, mixed_got), jnp.where(y == 0, mixed_got, mixed_own)], axis=1)

    @pl.loop(0, 2)
    def _(turn):
        some = pl.ds(pl.multiple_of(turn * (width // 2), LANES), width // 2)
        attended = dot(all_heads, head_rows(turn, slice(3 * cols, 5 * cols)), NT)
        block_ref[:, some] = (tokens[:, some].astype(F32) + attended + out_own[:, some].astype(F32) + out_got[:, some].astype(F32) + bias_ref[:, some]).astype(BF)

    tiny[0].wait_recv()
    t_x[...] = t_all[:, :, core] + t_core[...]
    group = []
    for s, peer in enumerate(along_x):
        group.append(remote(t_x.at[:, (x + s + 1) % wide], t_xgot.at[x], tsend.at[1 + s], trecv.at[1 + s], peer))
        group[s].start()
    tiny += group
    t_xgot[x] = t_x[:, x]
    over_y(2)
    over_z(4)
    for copy in group:
        copy.wait_recv()
    total = t_xgot[0]
    for xx in range(1, wide):
        total += t_xgot[xx]
    t_z[...] = total
    group = []
    for s, peer in enumerate(along_z):
        group.append(remote(t_z.at[(z + s + 1) % deep], t_zgot.at[z], tsend.at[wide + s], trecv.at[wide + s], peer))
        group[s].start()
    tiny += group
    t_zgot[z] = t_z[z]
    over_y(3)
    over_z(5)
    for copy in group:
        copy.wait_recv()
    total = t_zgot[0]
    for zz in range(1, deep):
        total += t_zgot[zz]
    t_y[...] = total
    tiny.append(remote(t_y.at[1 - y], t_ygot, tsend.at[wide + deep - 1], trecv.at[wide + deep - 1], partner))
    tiny[-1].start()
    for i in range(4):
        last(i)
    over_y(4)
    tiny[-1].wait_recv()
    small_ref[...] = t_y[y] + t_ygot[...]
    over_y(5)
    last(4)
    last(5)
    puts[0].wait()
    rows_copy[1].wait_recv()
    for copy in list(first.values()) + [c for group in list(second.values()) + list(third.values()) for c in group] + list(fourth.values()) + tiny + rows_copy:
        copy.wait_send()


def last_half(tokens, cotan, bias, gb, gains, kept, sums, batch):
    deep, wide = grid_of(batch)
    own_rows, width = tokens.shape
    rows = 2 * own_rows
    hidden = gb.shape[1]
    cols = hidden // 4
    block = hidden // 2
    shard = width // (2 * batch)
    slots = own_rows // PATCHES
    cuts = [(part, slice(at, at + block)) for part in range(3) for at in (0, block)]
    vm = pl.BlockSpec(memory_space=pltpu.VMEM)
    hbm = pl.BlockSpec(memory_space=pl.ANY)
    buf = lambda *shape: pltpu.VMEM(shape, BF)
    tile = lambda *lead: pltpu.VMEM(lead + TINY, F32)
    scratch = [buf(*k.shape) for k in kept]
    scratch += [buf(wide, deep, 2 * shard, hidden)] * 2
    scratch += [buf(deep, wide, 2, 2 * shard, hidden), buf(deep, wide, 2 * shard, hidden), buf(wide - 1, deep, 2 * shard, hidden)]
    scratch += [buf(deep, 2 * shard, hidden)] * 3 + [buf(deep - 1, 2 * shard, hidden)] * 3 + [buf(shard, hidden)] * 6
    scratch += [buf(rows, 3 * cols), buf(rows, cols), buf(slots * SLOT, cols)]
    scratch += [tile(deep, wide, 2, 2), tile(deep, wide, 2), tile(deep, wide, 2), tile(wide, deep, 2), tile(deep, 2), tile(deep, 2), tile(2), tile()]
    scratch += [pltpu.SemaphoreType.DMA((len(cuts), deep + wide))] * 2 + [pltpu.SemaphoreType.DMA((deep + wide + 2,))] * 2 + [pltpu.SemaphoreType.DMA((len(kept),)), pltpu.SemaphoreType.DMA((2 * wide,)), pltpu.SemaphoreType.DMA]
    full = lambda *shape: jax.ShapeDtypeStruct(shape, F32)
    low = jax.ShapeDtypeStruct((own_rows, width), BF)
    return pl.pallas_call(
        functools.partial(last_kernel, deep=deep, wide=wide, cuts=cuts),
        in_specs=[vm] * 5 + [hbm] * (len(kept) + 2 * wide),
        out_specs=[hbm] * 2 + [vm] * 6,
        out_shape=[low] * 3 + [full(3, shard, 2 * cols), full(shard, 2 * cols), full(shard, 2 * hidden), full(shard, 2 * hidden), full(*TINY)],
        scratch_shapes=scratch,
        compiler_params=pltpu.CompilerParams(collective_id=1, has_side_effects=True, vmem_limit_bytes=VMEM_CAP),
        name="head_gradients_and_scatter",
    )(tokens, cotan, bias, gb, gains, *kept, *sums)


def result_kernel(tokens, cotan, gain, dn_own, dn_got, block_in, qkv_in, wo_in, up_in, down_in, small, block, grad, qkv, wo, up, down, up_b, down_b, norm_g, query_g, key_g):
    vhat, scale = norm_stats(tokens[...].astype(F32))
    scaled = (dn_own[...].astype(F32) + dn_got[...].astype(F32)) * gain[...]
    d_tokens = (scaled - jnp.mean(scaled, axis=-1, keepdims=True) - vhat * jnp.mean(scaled * vhat, axis=-1, keepdims=True)) * scale
    grad[...] = (cotan[...].astype(F32) + d_tokens).astype(BF)
    block[...] = block_in[...]

    @pl.when(pl.program_id(0) == 0)
    def _():
        qkv[...] = qkv_in[...]
        wo[...] = wo_in[...]
        up[...] = up_in[...]
        down[...] = down_in[...]
        norm_g[...] = small[0:1, : norm_g.shape[1]]
        down_b[...] = small[1:2, : down_b.shape[1]]
        up_b[...] = small[2:3, : up_b.shape[1]]
        query_g[...] = small[3:4, :HD]
        key_g[...] = small[3:4, HD : 2 * HD]


def results(tokens, cotan, gain, dn_own, dn_got, block_in, sums, small, per):
    rows, width = tokens.shape
    chunk = rows // 2
    shard = sums[1].shape[0]
    blk = pl.BlockSpec((chunk, width), lambda j: (j, 0))
    whole = lambda shape: pl.BlockSpec(shape, lambda j: (0,) * len(shape))
    vectors = [(1, per), (1, shard), (1, shard), (1, HD), (1, HD)]
    return pl.pallas_call(
        result_kernel,
        grid=(rows // chunk,),
        in_specs=[blk, blk, whole(gain.shape), blk, blk, blk] + [whole(s.shape) for s in sums] + [whole(small.shape)],
        out_specs=[blk, blk] + [whole(s.shape) for s in sums] + [whole(v) for v in vectors],
        out_shape=[jax.ShapeDtypeStruct((rows, width), BF)] * 2 + [jax.ShapeDtypeStruct(s.shape, F32) for s in sums] + [jax.ShapeDtypeStruct(v, F32) for v in vectors],
        compiler_params=pltpu.CompilerParams(vmem_limit_bytes=VMEM_CAP),
        name="results",
    )(tokens, cotan, gain, dn_own, dn_got, block_in, *sums, small)


def local(tokens, cotangent, image_tokens, w_qkv, w_out, w_up, bias_up, w_down, bias_down, norm_gain, query_gain, key_gain):
    batch = lax.axis_size("batch")
    deep, wide = grid_of(batch)
    row = lambda v: v.reshape(1, -1)
    weights = (w_qkv, w_out.T, w_up, w_down.T)
    vectors = (row(norm_gain), row(bias_down), row(bias_up), row(query_gain), row(key_gain))
    made = first_half(tokens, cotangent, weights, vectors, batch)
    x_par, dy_par, normed, q, k, v, d_o, qraw, kraw, head_w, out_own, out_other, dn = made[:13]
    up_sums, down_sums = made[13 : 13 + wide], made[13 + wide : 13 + 2 * wide]
    gb, gain, bias, gains = made[13 + 2 * wide :]
    at = lambda z, x, c: (z * wide + x) * 2 + c

    def over_x(terms):
        return [terms[0]] + [lax.ppermute(terms[s], "batch", [(at(z, x, c), at(z, (x + s) % wide, c)) for z in range(deep) for x in range(wide) for c in range(2)]) for s in range(1, wide)]

    up_sums = over_x(up_sums)
    out_got = lax.ppermute(out_other, "branch", [(0, 1), (1, 0)])
    down_sums = over_x(down_sums)
    o, dq, dk, dv = attention(image_tokens[0], q, k, v, d_o)
    kept = [x_par, dy_par, normed, o, dq, dk, dv, qraw, kraw, head_w, out_own, out_got, dn]
    dn_own, dn_got, block_in, g_qkv, g_out, g_up, g_down, small = last_half(tokens, cotangent, bias, gb, gains, kept, up_sums + down_sums, batch)
    block_out, grad_tokens, g_qkv, g_out, g_up, g_down, g_up_b, g_down_b, g_norm, g_query, g_key = results(tokens, cotangent, gain, dn_own, dn_got, block_in, [g_qkv, g_out, g_up, g_down], small, bias_up.shape[0])
    flat = lambda v: v.reshape(-1)
    return (block_out, grad_tokens, g_qkv, g_out.T, g_up, flat(g_up_b), g_down.T, flat(g_down_b), flat(g_norm), flat(g_query), flat(g_key))


def solution(mesh):
    both = ("batch", "branch")
    in_specs = (P(both, None), P(both, None), P("batch", None), P(None, both, None), P(None, both), P(both, None), P(both), P(None, both), P(both), P(both), P(), P())
    out_specs = (P(both, None), P(both, None), P(None, both, None), P(None, both), P(both, None), P(both), P(None, both), P(both), P(both), P(), P())
    return jax.shard_map(local, mesh=mesh, in_specs=in_specs, out_specs=out_specs, check_vma=False)
```

```python
import functools
import jax
import jax.numpy as jnp
from jax import lax
from jax.experimental import pallas as pl
from jax.experimental.pallas import tpu as pltpu
from jax.sharding import PartitionSpec as P

HD = 64
LANES = 128
NORM_EPS = 1e-06
LONGEST = 784
PATCHES = 196
SLOT = 208
VMEM_CAP = 66_000_000
BF = jnp.bfloat16
F32 = jnp.float32


def dot(a, b, dims=((1,), (0,))):
    return lax.dot_general(a, b, (dims, ((), ())), preferred_element_type=F32)


NT = ((1,), (1,))
TN = ((0,), (0,))


def norm_stats(values):
    centred = values - jnp.mean(values, axis=-1, keepdims=True)
    spread = jnp.mean(centred * centred, axis=-1, keepdims=True)
    scale = lax.rsqrt(spread + NORM_EPS)
    return centred * scale, scale


def head_means(values, ones_low):
    means = []
    for at in range(0, values.shape[1], LANES):
        some = values[:, at : at + LANES]
        high = some.astype(BF)
        low = (some - high.astype(F32)).astype(BF)
        means.append(dot(jnp.concatenate([high, low], axis=1), ones_low))
    return jnp.concatenate(means, axis=1)


def head_ones():
    row = lax.broadcasted_iota(jnp.int32, (2 * LANES, LANES), 0) % LANES // HD
    col = lax.broadcasted_iota(jnp.int32, (2 * LANES, LANES), 1) // HD
    return jnp.where(row == col, 1.0 / HD, 0.0).astype(BF)


def head_stats(raw, ones_low):
    centred = raw - head_means(raw, ones_low)
    scale = lax.rsqrt(head_means(centred * centred, ones_low) + NORM_EPS)
    return centred * scale, scale


MESH = pl.DeviceIdType.MESH


def place():
    return lax.axis_index("batch"), lax.axis_index("branch")


def grid_of(batch):
    chips = batch // 2
    across = 1
    while across * across * 4 <= chips:
        across *= 2
    return chips // across, across


def greet(peers):
    barrier = pltpu.get_barrier_semaphore()
    for peer in peers:
        pl.semaphore_signal(barrier, inc=1, device_id=peer, device_id_type=MESH)
    pl.semaphore_wait(barrier, len(peers))


def neighbours(deep, wide):
    batch, branch = place()
    core, x, z = batch % 2, (batch // 2) % wide, batch // (2 * wide)
    at = lambda zz, xx, cc: (zz * wide + xx) * 2 + cc
    partner = (batch, 1 - branch)
    along_z = [(at((z + s) % deep, x, core), branch) for s in range(1, deep)]
    along_x = [(at(z, (x + s) % wide, core), branch) for s in range(1, wide)]
    sibling = (at(z, x, 1 - core), branch)
    return (z, x, core, branch), partner, along_z, along_x, sibling


def remote(src, dst, send, recv, peer):
    return pltpu.make_async_remote_copy(src_ref=src, dst_ref=dst, send_sem=send, recv_sem=recv, device_id=peer, device_id_type=MESH)


TINY = (8, LANES)
STRIP = 112


def gelu_parts(hidden):
    square = hidden * hidden
    tanh = jnp.tanh(hidden * (0.7978845608028654 + 0.035677408136300125 * square))
    half = 0.5 + 0.5 * tanh
    act = hidden * half
    slope = half + (act * (1.0 - tanh)) * (0.7978845608028654 + 0.1070322244089 * square)
    return act.astype(BF), slope


def repeated(values, count):
    return jnp.concatenate([values] * count, axis=1)


def first_kernel(*refs, deep, wide, cuts, block):
    tokens, cotan, qkv_ref, wo_ref, up_ref, down_ref, nb_ref, db_ref, ub_ref, qg_ref, kg_ref = refs[:11]
    o_x, o_dy, o_normed, o_q, o_k, o_v, o_do, o_qraw, o_kraw, o_heads, o_own, o_other, o_dn = refs[11:24]
    o_sums = (refs[24 : 24 + wide], refs[24 + wide : 24 + 2 * wide])
    gb_ref, gain_ref, bias_ref, tiny = refs[24 + 2 * wide : 28 + 2 * wide]
    scratch = refs[28 + 2 * wide :]
    packs, lands, wires = scratch[:3], scratch[3:6], scratch[6:9]
    rounded, tiny_all, x_par, dy_par, normed, act, d_hid, s_q, s_k, s_v, s_do, s_qraw, s_kraw, s_out, s_dn = scratch[9:24]
    grads, got_core, flats = scratch[24:26], scratch[26:28], scratch[28:31]
    send, recv, tsend, trecv, csend, crecv, osem = scratch[31:]
    (z, x, core, y), partner, along_z, along_x, sibling = neighbours(deep, wide)
    batch = 2 * deep * wide
    own_rows, width = tokens.shape
    shard, hidden = packs[0].shape[1:]
    cols = hidden // 4
    pair = 2 * shard
    direct = pair % 16 == 0
    places = [(b // (2 * wide), (b // 2) % wide, b % 2, s) for b in range(batch) for s in range(2)]

    for half in range(2):
        some = slice(half * cols, (half + 1) * cols)
        packs[0][half] = up_ref[:, half * hidden : (half + 1) * hidden].astype(BF)
        packs[1][half] = down_ref[:, half * hidden : (half + 1) * hidden].astype(BF)
        for at in range(3):
            packs[2][half, :, at * cols : (at + 1) * cols] = qkv_ref[at, :, some].astype(BF)
        packs[2][half, :, 3 * cols :] = wo_ref[...].astype(BF)
    rounded[...] = jnp.zeros(TINY, BF)
    for row, ref in enumerate((nb_ref, db_ref, ub_ref, qg_ref, kg_ref)):
        rounded[row : row + 1, : ref.shape[1]] = ref[...].astype(BF)
    tiny[...] = rounded[...].astype(F32)
    tiny_all[z, x, core, y] = tiny[...]
    greet([partner, sibling] + along_z + along_x)
    outs = []

    def put(src, dst):
        copy = pltpu.make_async_copy(src, dst, osem.at[len(outs)])
        copy.start()
        outs.append(copy)

    spread_tiny = [remote(tiny, tiny_all.at[z, x, core, y], tsend.at[0], trecv.at[0], partner)]
    spread_tiny[0].start()
    over_y = []
    for i, (part, at) in enumerate(cuts):
        over_y.append(remote(packs[part].at[1 - y, :, at], lands[part].at[:, at], send.at[i, 0], recv.at[i, 0], partner))
        over_y[i].start()
    rows_copy = [remote(tokens, x_par, tsend.at[deep + wide], trecv.at[deep + wide], partner), remote(cotan, dy_par, tsend.at[deep + wide + 1], trecv.at[deep + wide + 1], partner)]
    for copy in rows_copy:
        copy.start()

    def tiny_stage(block, peers, first):
        group = [remote(block, block, tsend.at[first + s], trecv.at[first + s], peer) for s, peer in enumerate(peers)]
        for copy in group:
            copy.start()
        for copy in group:
            copy.wait_recv()
        spread_tiny.extend(group)

    over_z, over_x, over_core = [], [], []

    def start_z(i):
        part, at = cuts[i]
        over_y[i].wait_recv()
        mine, other = packs[part][y, :, at].astype(F32), lands[part][:, at].astype(F32)
        pair = jnp.concatenate([jnp.where(y == 0, mine, other), jnp.where(y == 0, other, mine)], axis=0)
        wires[part][z, x, core, :, at] = pair.astype(BF)
        block = wires[part].at[z, x, core, :, at]
        over_z.append([remote(block, block, send.at[i, 1 + s], recv.at[i, 1 + s], peer) for s, peer in enumerate(along_z)])
        for copy in over_z[i]:
            copy.start()

    def start_x(i):
        part, at = cuts[i]
        for copy in over_z[i]:
            copy.wait_recv()
        block = wires[part].at[:, x, core, :, at]
        over_x.append([remote(block, block, send.at[i, deep + s], recv.at[i, deep + s], peer) for s, peer in enumerate(along_x)])
        for copy in over_x[i]:
            copy.start()

    def start_core(i):
        part, at = cuts[i]
        for copy in over_x[i]:
            copy.wait_recv()
        block = wires[part].at[:, :, core, :, at]
        over_core.append(remote(block, block, send.at[i, deep + wide - 1], recv.at[i, deep + wide - 1], sibling))
        over_core[i].start()

    def arrive(i):
        part, at = cuts[i]
        over_core[i].wait_recv()
        if not direct:
            for b in range(batch):
                flats[part][2 * shard * b : 2 * shard * (b + 1), at] = wires[part][b // (2 * wide), (b // 2) % wide, b % 2, :, at]

    def weight(part, at):
        if direct:
            value = wires[part][:, :, :, :, at]
            return value.reshape(width, value.shape[-1])
        return flats[part][:, at]

    for i in range(len(cuts)):
        start_z(i)
        if i == 0:
            spread_tiny[0].wait_recv()
            tiny_stage(tiny_all.at[z, x, core], along_z, 1)
        if i == 1:
            tiny_stage(tiny_all.at[:, x, core], along_x, deep)
        if i == 2:
            tiny_stage(tiny_all.at[:, :, core], [sibling], deep + wide - 1)
    per = ub_ref.shape[1]
    gain_ref[...] = jnp.concatenate([tiny_all[p][0:1, :shard] for p in places], axis=1)
    bias_ref[...] = jnp.concatenate([tiny_all[p][1:2, :shard] for p in places], axis=1)
    low_b = jnp.concatenate([tiny_all[p][2:3, :per] for p in places[:batch]], axis=1)
    high_b = jnp.concatenate([tiny_all[p][2:3, :per] for p in places[batch:]], axis=1)
    gb_ref[...] = jnp.where(y == 0, low_b, high_b)

    sides = ((tokens, cotan, slice(0, own_rows)), (x_par, dy_par, slice(own_rows, 2 * own_rows)))

    def normalise(side):
        @pl.loop(0, own_rows // STRIP)
        def _(turn):
            strip = pl.ds(pl.multiple_of(turn * STRIP, 16), STRIP)
            vhat, _ = norm_stats(sides[side][0][strip, :].astype(F32))
            normed[pl.ds(pl.multiple_of(side * own_rows + turn * STRIP, 16), STRIP), :] = (vhat * gain_ref[...]).astype(BF)

    def expand(side, at, back):
        rows = sides[side][2]

        turns = 3 if back else 12

        @pl.loop(0, turns)
        def _(turn):
            size = (at.stop - at.start) // turns
            some = pl.ds(pl.multiple_of(at.start + turn * size, LANES), size)
            act[rows, some], slope = gelu_parts(dot(normed[rows, :], weight(0, some)) + gb_ref[:, some])
            if back:
                slope *= dot(sides[side][1][...], weight(1, some))
            d_hid[rows, some] = slope.astype(BF)

    def apply_back(side):
        rows = sides[side][2]

        @pl.loop(0, 2)
        def _(turn):
            at = pl.ds(pl.multiple_of(turn * block, LANES), block)
            d_hid[rows, at] = (d_hid[rows, at].astype(F32) * dot(sides[side][1][...], weight(1, at))).astype(BF)

    def contract(side, low, kept, part):
        rows = sides[side][2]
        size = width // 2

        @pl.loop(0, 2)
        def _(turn):
            if direct:
                value = wires[part][pl.ds(turn * (deep // 2), deep // 2)].reshape(size, hidden)
            else:
                value = flats[part][pl.ds(pl.multiple_of(turn * size, 16), size), :]
            kept[rows, pl.ds(pl.multiple_of(turn * size, LANES), size)] = dot(low[rows, :], value, NT).astype(BF)

    def place_rows(base, ref, values):
        for at in range(own_rows // PATCHES):
            ref[pl.ds(pl.multiple_of((base + at) * SLOT, 16), PATCHES), :] = values[at * PATCHES : (at + 1) * PATCHES].astype(BF)

    def queries_keys():
        ones_low = head_ones()

        @pl.loop(0, 2)
        def _(side):
            rows = pl.ds(pl.multiple_of(side * own_rows, 16), own_rows)
            base = jnp.where(side == 0, y, 1 - y) * (own_rows // PATCHES)
            for at, (raw_ref, low_ref, gain) in enumerate(((s_qraw, s_q, 3), (s_kraw, s_k, 4))):
                raw = dot(normed[rows, :], weight(2, slice(at * cols, (at + 1) * cols)))
                raw_ref[rows, :] = raw.astype(BF)
                hat, _ = head_stats(raw, ones_low)
                place_rows(base, low_ref, hat * repeated(tiny[gain : gain + 1, :HD], cols // HD))

    def values_of():
        @pl.loop(0, 2)
        def _(side):
            rows = pl.ds(pl.multiple_of(side * own_rows, 16), own_rows)
            place_rows(jnp.where(side == 0, y, 1 - y) * (own_rows // PATCHES), s_v, dot(normed[rows, :], weight(2, slice(2 * cols, 3 * cols))))

    def back_of(side):
        place_rows((y if side == 0 else 1 - y) * (own_rows // PATCHES), s_do, dot(sides[side][1][...], weight(2, pl.ds(pl.multiple_of((3 + y) * cols, LANES), cols))))

    over_sib = []

    def grad_own(part):
        rows = sides[0][2]

        @pl.loop(0, 6)
        def _(turn):
            size = hidden // 6
            some = pl.ds(pl.multiple_of(turn * size, LANES), size)
            value = dot(normed[rows, :], d_hid[rows, some], TN) if part == 0 else dot(cotan[...], act[rows, some], TN)
            for b in range(batch):
                grads[part][b // (2 * wide), (b // 2) % wide, b % 2, :, some] = value[b * pair : (b + 1) * pair].astype(BF)

    def grad_rest(part, at):
        rows = sides[1][2]

        @pl.loop(0, 2)
        def _(turn):
            size = (at.stop - at.start) // 2
            some = pl.ds(pl.multiple_of(at.start + turn * size, LANES), size)
            value = dot(normed[rows, :], d_hid[rows, some], TN) if part == 0 else dot(dy_par[...], act[rows, some], TN)
            for b in range(batch):
                block_at = (b // (2 * wide), (b // 2) % wide, b % 2, slice(None), some)
                grads[part][block_at] = (grads[part][block_at].astype(F32) + value[b * pair : (b + 1) * pair]).astype(BF)

        i = len(over_sib)
        over_sib.append(remote(grads[part].at[:, :, 1 - core, :, at], got_core[part].at[:, :, :, at], csend.at[i], crecv.at[i], sibling))
        over_sib[i].start()

    def add_core(i, part, at):
        over_sib[i].wait_recv()

        @pl.loop(0, deep)
        def _(zz):
            for xx in range(wide):
                total = grads[part][zz, xx, core, :, at].astype(F32) + got_core[part][zz, xx, :, at].astype(F32)
                got_core[part][zz, xx, :, at] = total.astype(BF)

    first, second = slice(0, block), slice(block, 2 * block)
    start_x(0)
    normalise(0)
    start_x(1)
    start_core(0)
    start_x(2)
    start_core(1)
    arrive(0)
    arrive(1)
    expand(0, first, True)
    start_x(3)
    start_core(2)
    rows_copy[0].wait_recv()
    normalise(1)
    put(x_par, o_x)
    put(normed, o_normed)
    start_x(4)
    start_core(3)
    arrive(2)
    arrive(3)
    expand(0, second, True)
    start_core(4)
    expand(1, slice(0, hidden), False)
    start_x(5)
    contract(0, act, s_out, 1)
    contract(0, d_hid, s_dn, 0)
    grad_own(0)
    grad_own(1)
    contract(1, act, s_out, 1)
    put(s_out.at[pl.ds(0, own_rows)], o_own)
    put(s_out.at[pl.ds(own_rows, own_rows)], o_other)
    arrive(4)
    start_core(5)
    queries_keys()
    for src, dst in ((s_q, o_q), (s_k, o_k), (s_qraw, o_qraw), (s_kraw, o_kraw)):
        put(src, dst)
    arrive(5)
    put(wires[2] if direct else flats[2], o_heads)
    values_of()
    put(s_v, o_v)
    back_of(0)
    rows_copy[1].wait_recv()
    put(dy_par, o_dy)
    back_of(1)
    put(s_do, o_do)
    apply_back(1)
    grad_rest(0, first)
    grad_rest(0, second)
    add_core(0, 0, first)
    grad_rest(1, first)
    add_core(1, 0, second)
    for s in range(wide):
        put(got_core[0].at[:, (x + s) % wide], o_sums[0][s])
    grad_rest(1, second)
    contract(1, d_hid, s_dn, 0)
    put(s_dn, o_dn)
    add_core(2, 1, first)

    @pl.loop(0, 6)
    def _(turn):
        some = pl.ds(pl.multiple_of(turn * (hidden // 6), LANES), hidden // 6)
        gb_ref[:, some] = dot(jnp.ones((8, 2 * own_rows), BF), d_hid[:, some])[:1]

    add_core(3, 1, second)
    for s in range(wide):
        put(got_core[1].at[:, (x + s) % wide], o_sums[1][s])
    for copy in outs:
        copy.wait()
    for copy in spread_tiny + over_y + rows_copy + [c for group in over_z + over_x for c in group] + over_core + over_sib:
        copy.wait_send()


def first_half(tokens, cotan, weights, vectors, batch):
    deep, wide = grid_of(batch)
    own_rows, width = tokens.shape
    shard, hidden = weights[2].shape[0], weights[2].shape[1] // 2
    cols = hidden // 4
    block = hidden // 2
    rows = 2 * own_rows
    spread_rows = rows // PATCHES * SLOT
    widths = (hidden, hidden, 5 * cols)
    first, second = slice(0, block), slice(block, hidden)
    cuts = [(0, first), (1, first), (0, second), (1, second), (2, slice(0, 2 * cols)), (2, slice(2 * cols, 5 * cols))]
    vm = pl.BlockSpec(memory_space=pltpu.VMEM)
    hbm = pl.BlockSpec(memory_space=pl.ANY)
    direct = (2 * shard) % 16 == 0
    wire_shapes = [(deep, wide, 2, 2 * shard, w) for w in widths]
    flat_shapes = [(width, w) for w in widths]
    low = lambda *shape: jax.ShapeDtypeStruct(shape, BF)
    outs = [low(own_rows, width)] * 2 + [low(rows, width)] + [low(spread_rows, cols)] * 4 + [low(rows, cols)] * 2
    outs += [low(*(wire_shapes if direct else flat_shapes)[2])] + [low(own_rows, width)] * 2 + [low(rows, width)] + [low(deep, 2 * shard, hidden)] * (2 * wide)
    tiny_outs = [jax.ShapeDtypeStruct((1, hidden), F32), jax.ShapeDtypeStruct((1, width), F32), jax.ShapeDtypeStruct((1, width), F32), jax.ShapeDtypeStruct(TINY, F32)]
    buf = lambda *shape: pltpu.VMEM(shape, BF)
    scratch = [buf(2, shard, w) for w in widths] + [buf(shard, w) for w in widths] + [buf(*s) for s in wire_shapes]
    scratch += [buf(*TINY), pltpu.VMEM((deep, wide, 2, 2) + TINY, F32), buf(own_rows, width), buf(own_rows, width), buf(rows, width), buf(rows, hidden), buf(rows, hidden)]
    scratch += [buf(spread_rows, cols)] * 4 + [buf(rows, cols)] * 2 + [buf(rows, width)] * 2
    scratch += [buf(deep, wide, 2, 2 * shard, hidden)] * 2 + [buf(deep, wide, 2 * shard, hidden)] * 2
    scratch += [buf(16, LANES) if direct else buf(*s) for s in flat_shapes]
    scratch += [pltpu.SemaphoreType.DMA((len(cuts), deep + wide))] * 2 + [pltpu.SemaphoreType.DMA((deep + wide + 2,))] * 2 + [pltpu.SemaphoreType.DMA((4,))] * 2 + [pltpu.SemaphoreType.DMA((len(outs),))]
    return pl.pallas_call(
        functools.partial(first_kernel, deep=deep, wide=wide, cuts=cuts, block=block),
        in_specs=[vm] * 11,
        out_specs=[hbm] * len(outs) + [vm] * 4,
        out_shape=outs + tiny_outs,
        scratch_shapes=scratch,
        compiler_params=pltpu.CompilerParams(collective_id=0, has_side_effects=True, vmem_limit_bytes=VMEM_CAP),
        name="gather_and_feed_forward",
    )(tokens, cotan, *weights, *vectors)


def load_rows(ref, block, blocks):
    parts = [ref[pl.ds(pl.multiple_of((block + at) * SLOT, 16), PATCHES), :] for at in range(blocks)]
    return parts[0] if blocks == 1 else jnp.concatenate([p.astype(F32) for p in parts], axis=0).astype(BF)

def attend_pair(pair_q, pair_k, pair_v, pair_do, pieces):
    count = pair_q.shape[0]
    lane = lax.broadcasted_iota(jnp.int32, (count, 2 * HD), 1)
    pair_q = pair_q * jnp.asarray(0.125, BF)
    zero = jnp.zeros_like(pair_q)
    v_t, k_t = pair_v.T, pair_k.T
    mixed, grads_q, grad_k, grad_v = [], [], None, None
    for head in range(2):
        mine = (lane < HD) if head == 0 else (lane >= HD)
        q_m, do_m = jnp.where(mine, pair_q, zero), jnp.where(mine, pair_do, zero)
        part = slice(head * HD, (head + 1) * HD)
        outs, gqs = [], []
        for first, size in pieces:
            q, d_o = q_m[first : first + size], do_m[first : first + size]
            shifted = jnp.exp(dot(pair_k, q, NT))
            total = jnp.sum(shifted, axis=0, keepdims=True)
            weights = shifted * (1.0 / total)
            low = weights.astype(BF)
            d_weights = dot(pair_v, d_o, NT)
            inner = jnp.sum(weights * d_weights, axis=0, keepdims=True)
            d_scores = (weights * (d_weights - inner)).astype(BF)
            outs.append(dot(v_t[part], low))
            gqs.append(dot(k_t[part], d_scores))
            gv, gk = dot(low, d_o), dot(d_scores, q)
            grad_v = gv if grad_v is None else grad_v + gv
            grad_k = gk if grad_k is None else grad_k + gk
        join = lambda parts: parts[0] if len(parts) == 1 else jnp.concatenate(parts, axis=1)
        mixed.append(join(outs))
        grads_q.append(join(gqs))
    turn = lambda parts: jnp.concatenate(parts, axis=0).T
    return turn(mixed), turn(grads_q) * 0.125, grad_k, grad_v

def attention_kernel(count_ref, *refs, pieces, together):
    ins, outs, (small_ref,) = refs[:4], refs[4:8], refs[8:]
    place, smalls, bigs, big_at = 0, 0, 0, 0
    for slot in range(count_ref.shape[0]):
        count = count_ref[slot]
        is_small = (count == PATCHES).astype(jnp.int32)
        is_big = (count == LONGEST).astype(jnp.int32)
        small_ref[smalls] = place
        big_at = jnp.where(is_big == 1, place, big_at)
        smalls, bigs = smalls + is_small, bigs + is_big
        place = place + is_small + (LONGEST // PATCHES) * is_big

    def images(firsts, blocks, pieces):
        loaded = [[load_rows(ref, block, blocks) for ref in ins] for block in firsts]
        results = [attend_pair(*values, pieces) for values in loaded]
        for block, result in zip(firsts, results):
            for ref, values in zip(outs, result):
                for at in range(blocks):
                    ref[pl.ds(pl.multiple_of((block + at) * SLOT, 16), PATCHES), :] = values[at * PATCHES : (at + 1) * PATCHES].astype(ref.dtype)

    @pl.when(bigs > 0)
    def _():
        images([big_at], LONGEST // PATCHES, pieces)

    @pl.loop(0, smalls // together)
    def _(turn):
        images([small_ref[turn * together + at] for at in range(together)], 1, ((0, PATCHES),))

def attention(counts, q, k, v, d_o, pieces=((0, 784),), together=4):
    rows, cols = q.shape
    sm = pl.BlockSpec(memory_space=pltpu.SMEM)
    blk = pl.BlockSpec((rows, 2 * HD), lambda j: (0, j))
    return pl.pallas_call(
        functools.partial(attention_kernel, pieces=pieces, together=together),
        grid=(cols // (2 * HD),),
        in_specs=[sm] + [blk] * 4,
        out_specs=[blk] * 4,
        out_shape=[jax.ShapeDtypeStruct((rows, cols), t) for t in (BF, BF, BF, BF)],
        scratch_shapes=[pltpu.SMEM((counts.shape[0] + 1,), jnp.int32)],
        compiler_params=pltpu.CompilerParams(vmem_limit_bytes=VMEM_CAP),
        cost_estimate=pl.CostEstimate(flops=20_000_000_000, bytes_accessed=20_000_000, transcendentals=rows * LONGEST * cols // HD),
        name="attention",
    )(counts, q, k, v, d_o)


def last_kernel(*refs, deep, wide, cuts):
    tokens, cotan, bias_ref, gb_ref, gains_ref = refs[:5]
    i_x, i_dy, i_normed, i_o, i_dq, i_dk, i_dv, i_qraw, i_kraw, i_heads, i_own, i_got, i_dn = refs[5:18]
    i_sums = (refs[18 : 18 + wide], refs[18 + wide : 18 + 2 * wide])
    o_dn, o_dn_got, block_ref, qkv_ref, wo_ref, up_ref, down_ref, small_ref = refs[18 + 2 * wide : 26 + 2 * wide]
    scratch = refs[26 + 2 * wide :]
    x_par, dy_par, normed, s_o, s_dq, s_dk, s_dv, qraw, kraw, head_w, out_own, out_got, dn = scratch[:13]
    terms = scratch[13:15]
    mine, got_core, got_x = scratch[15:18]
    to_z, got_z, to_y, got_y = (scratch[18 + 3 * i : 21 + 3 * i] for i in range(4))
    d_proj, mixed, o_got = scratch[30:33]
    t_all, t_core, t_x, t_xgot, t_z, t_zgot, t_y, t_ygot = scratch[33:41]
    send, recv, tsend, trecv, lsem, gsem, osem = scratch[41:]
    (z, x, core, y), partner, along_z, along_x, sibling = neighbours(deep, wide)
    batch = 2 * deep * wide
    own_rows, width = tokens.shape
    rows = 2 * own_rows
    cols = qraw.shape[1]
    shard = to_y[0].shape[0]
    slots = own_rows // PATCHES
    places = [(b // (2 * wide), (b // 2) % wide, b % 2, s) for b in range(batch) for s in range(2)]
    own, other = slice(0, own_rows), slice(own_rows, rows)
    greet([partner, sibling] + along_z + along_x)

    theirs = pl.ds(pl.multiple_of((1 - y) * slots * SLOT, 16), slots * SLOT)
    rows_copy = [remote(i_o.at[theirs], o_got, tsend.at[deep + wide], trecv.at[deep + wide], partner)]
    rows_copy[0].start()
    held = {}
    for part in range(2):
        for s in range(wide):
            held[part, s] = pltpu.make_async_copy(i_sums[part][s], terms[part].at[s], gsem.at[part * wide + s])
            held[part, s].start()
    loads = {}
    for at, (name, src, dst) in enumerate((("qraw", i_qraw, qraw), ("dq", i_dq, s_dq), ("kraw", i_kraw, kraw), ("dk", i_dk, s_dk), ("dv", i_dv, s_dv), ("heads", i_heads, head_w), ("dn", i_dn, dn), ("normed", i_normed, normed), ("o", i_o, s_o), ("dy", i_dy, dy_par), ("x", i_x, x_par), ("own", i_own, out_own), ("got", i_got, out_got))):
        loads[name] = pltpu.make_async_copy(src, dst, lsem.at[at])
        loads[name].start()

    first, second, third, fourth = {}, {}, {}, {}

    def over_core(i):
        part, at = cuts[i]
        first[i] = remote(mine.at[:, :, 1 - core, :, at], got_core.at[:, :, :, at], send.at[i, 0], recv.at[i, 0], sibling)
        first[i].start()

    def over_x(i):
        part, at = cuts[i]
        first[i].wait_recv()

        @pl.loop(0, deep)
        def _(zz):
            for xx in range(wide):
                got_core[zz, xx, :, at] = (mine[zz, xx, core, :, at].astype(F32) + got_core[zz, xx, :, at].astype(F32)).astype(BF)

        second[i] = []
        for s, peer in enumerate(along_x):
            copy = remote(got_core.at[:, (x + s + 1) % wide, :, at], got_x.at[s, :, :, at], send.at[i, 1 + s], recv.at[i, 1 + s], peer)
            copy.start()
            second[i].append(copy)

    def over_z(i):
        part, at = cuts[i]
        if part == 2:
            for copy in second[i]:
                copy.wait_recv()

        @pl.loop(0, deep)
        def _(zz):
            if part == 2:
                total = got_core[zz, x, :, at].astype(F32)
                for s in range(wide - 1):
                    total += got_x[s, zz, :, at].astype(F32)
            else:
                total = terms[part][0, zz, :, at].astype(F32)
                for s in range(1, wide):
                    total += terms[part][s, zz, :, at].astype(F32)
            to_z[part][zz, :, at] = total.astype(BF)

        third[i] = []
        for s, peer in enumerate(along_z):
            copy = remote(to_z[part].at[(z + s + 1) % deep, :, at], got_z[part].at[s, :, at], send.at[i, wide + s], recv.at[i, wide + s], peer)
            copy.start()
            third[i].append(copy)

    def over_y(i):
        part, at = cuts[i]
        for copy in third[i]:
            copy.wait_recv()
        total = to_z[part][z, :, at].astype(F32)
        for s in range(deep - 1):
            total += got_z[part][s, :, at].astype(F32)
        low, high = total[:shard], total[shard:]
        to_y[part][:, at] = jnp.where(y == 0, high, low).astype(BF)
        fourth[i] = remote(to_y[part].at[:, at], got_y[part].at[:, at], send.at[i, wide + deep - 1], recv.at[i, wide + deep - 1], partner)
        fourth[i].start()
        deliver(part, y, at, jnp.where(y == 0, low, high))

    def deliver(part, half, at, values):
        if part < 2:
            ref = (up_ref, down_ref)[part]
            ref[:, pl.ds(pl.multiple_of(half * 4 * cols + at.start, LANES), at.stop - at.start)] = values
            return
        for piece in range(at.start // cols, at.stop // cols):
            some = values[:, piece * cols - at.start : (piece + 1) * cols - at.start]
            lanes = pl.ds(pl.multiple_of(half * cols, LANES), cols)
            if piece < 3:
                qkv_ref[piece, :, lanes] = some
            else:
                wo_ref[:, lanes] = some

    def last(i):
        part, at = cuts[i]
        fourth[i].wait_recv()
        deliver(part, 1 - y, at, got_y[part][:, at].astype(F32))

    def compact_rows(ref, base):
        parts = [ref[pl.ds(pl.multiple_of((base + at) * SLOT, 16), PATCHES), :].astype(F32) for at in range(slots)]
        return jnp.concatenate(parts, axis=0)

    bases = (y * slots, (1 - y) * slots)

    def head_rows(turn, at):
        if len(head_w.shape) > 2:
            value = head_w[pl.ds(turn * (deep // 2), deep // 2), :, :, :, at]
            return value.reshape(width // 2, value.shape[-1])
        return head_w[pl.ds(pl.multiple_of(turn * (width // 2), 16), width // 2), at]

    for part in range(2):
        for s in range(wide):
            held[part, s].wait()
    for i in range(4):
        over_z(i)
    ones_low = head_ones()
    gains = []
    for names, grad_in, raw_ref, gain, at in ((("dq", "qraw"), s_dq, qraw, 3, 0), (("dk", "kraw"), s_dk, kraw, 4, 1)):
        for name in names:
            loads[name].wait()

        def one_side(side, total):
            part = pl.ds(pl.multiple_of(side * own_rows, 16), own_rows)
            hat, scale = head_stats(raw_ref[part, :].astype(F32), ones_low)
            grad = compact_rows(grad_in, jnp.where(side == 0, *bases))
            scaled = grad * repeated(gains_ref[gain : gain + 1, :HD], cols // HD)
            d_raw = (scaled - head_means(scaled, ones_low) - hat * head_means(scaled * hat, ones_low)) * scale
            d_proj[part, at * cols : (at + 1) * cols] = d_raw.astype(BF)
            return total + jnp.sum(grad * hat, axis=0, keepdims=True)

        total = lax.fori_loop(0, 2, one_side, jnp.zeros((1, cols), F32))
        folded = total[:, :HD]
        for head in range(1, cols // HD):
            folded += total[:, head * HD : (head + 1) * HD]
        gains.append(folded)
    loads["dv"].wait()

    @pl.loop(0, 2)
    def _(side):
        d_proj[pl.ds(pl.multiple_of(side * own_rows, 16), own_rows), 2 * cols : 3 * cols] = compact_rows(s_dv, jnp.where(side == 0, *bases)).astype(BF)

    loads["dn"].wait()
    loads["heads"].wait()

    def add_dn(part):
        size = width // 2

        @pl.loop(0, 2)
        def _(turn):
            some = pl.ds(pl.multiple_of(turn * size, LANES), size)
            dn[part, some] = (dn[part, some].astype(F32) + dot(d_proj[part, :], head_rows(turn, slice(0, 3 * cols)), NT)).astype(BF)

    add_dn(other)
    rows_copy.append(remote(dn.at[pl.ds(own_rows, own_rows)], o_dn_got, tsend.at[deep + wide + 1], trecv.at[deep + wide + 1], partner))
    rows_copy[1].start()

    def keep(at, values):
        for b in range(batch):
            mine[b // (2 * wide), (b // 2) % wide, b % 2, :, at] = values[2 * b * shard : 2 * (b + 1) * shard].astype(BF)

    loads["normed"].wait()

    @pl.loop(0, 3)
    def _(piece):
        at = pl.ds(pl.multiple_of(piece * cols, LANES), cols)
        keep(at, dot(normed[...], d_proj[:, at], TN))

    over_core(4)
    loads["o"].wait()
    loads["dy"].wait()

    @pl.loop(0, 2)
    def _(side):
        mixed[pl.ds(pl.multiple_of(side * own_rows, 16), own_rows), :] = compact_rows(s_o, jnp.where(side == 0, *bases)).astype(BF)

    over_y(0)
    over_x(4)
    keep(slice(3 * cols, 4 * cols), dot(cotan[...], mixed[own, :], TN) + dot(dy_par[...], mixed[other, :], TN))
    over_core(5)
    add_dn(own)
    puts = [pltpu.make_async_copy(dn.at[pl.ds(0, own_rows)], o_dn, osem)]
    puts[0].start()
    over_x(5)
    over_y(1)
    loads["x"].wait()
    grad_g = jnp.zeros((1, width), F32)
    for side, ref in enumerate((tokens, x_par)):

        def one_strip(turn, total):
            vhat, _ = norm_stats(ref[pl.ds(pl.multiple_of(turn * STRIP, 16), STRIP), :].astype(F32))
            some = dn[pl.ds(pl.multiple_of(side * own_rows + turn * STRIP, 16), STRIP), :].astype(F32)
            return total + jnp.sum(some * vhat, axis=0, keepdims=True)

        grad_g = lax.fori_loop(0, own_rows // STRIP, one_strip, grad_g)

    def add_strip(turn, total):
        return total + jnp.sum(cotan[pl.ds(pl.multiple_of(turn * STRIP, 16), STRIP), :].astype(F32), axis=0, keepdims=True)

    grad_db = lax.fori_loop(0, own_rows // STRIP, add_strip, jnp.zeros((1, width), F32))
    per = gb_ref.shape[1] // batch
    both = jnp.concatenate(gains, axis=1)
    bias = gb_ref[...]
    t_all[...] = jnp.zeros(t_all.shape, F32)
    for b, (zz, xx, cc, s) in enumerate(places):
        inside = jnp.where(y == b // batch, 1.0, 0.0)
        t_all[zz, xx, cc, s, 0:1, :shard] = grad_g[:, b * shard : (b + 1) * shard]
        t_all[zz, xx, cc, s, 1:2, :shard] = grad_db[:, b * shard : (b + 1) * shard]
        t_all[zz, xx, cc, s, 2:3, :per] = bias[:, (b % batch) * per : (b % batch + 1) * per] * inside
        t_all[zz, xx, cc, s, 3:4, : 2 * HD] = both
    tiny = [remote(t_all.at[:, :, 1 - core], t_core, tsend.at[0], trecv.at[0], sibling)]
    tiny[0].start()
    for name in ("own", "got"):
        loads[name].wait()
    rows_copy[0].wait_recv()
    mixed_got = compact_rows(o_got, 0).astype(BF)
    mixed_own = mixed[own, :]
    all_heads = jnp.concatenate([jnp.where(y == 0, mixed_own, mixed_got), jnp.where(y == 0, mixed_got, mixed_own)], axis=1)

    @pl.loop(0, 2)
    def _(turn):
        some = pl.ds(pl.multiple_of(turn * (width // 2), LANES), width // 2)
        attended = dot(all_heads, head_rows(turn, slice(3 * cols, 5 * cols)), NT)
        block_ref[:, some] = (tokens[:, some].astype(F32) + attended + out_own[:, some].astype(F32) + out_got[:, some].astype(F32) + bias_ref[:, some]).astype(BF)

    tiny[0].wait_recv()
    t_x[...] = t_all[:, :, core] + t_core[...]
    group = []
    for s, peer in enumerate(along_x):
        group.append(remote(t_x.at[:, (x + s + 1) % wide], t_xgot.at[x], tsend.at[1 + s], trecv.at[1 + s], peer))
        group[s].start()
    tiny += group
    t_xgot[x] = t_x[:, x]
    over_y(2)
    over_z(4)
    for copy in group:
        copy.wait_recv()
    total = t_xgot[0]
    for xx in range(1, wide):
        total += t_xgot[xx]
    t_z[...] = total
    group = []
    for s, peer in enumerate(along_z):
        group.append(remote(t_z.at[(z + s + 1) % deep], t_zgot.at[z], tsend.at[wide + s], trecv.at[wide + s], peer))
        group[s].start()
    tiny += group
    t_zgot[z] = t_z[z]
    over_y(3)
    over_z(5)
    for copy in group:
        copy.wait_recv()
    total = t_zgot[0]
    for zz in range(1, deep):
        total += t_zgot[zz]
    t_y[...] = total
    tiny.append(remote(t_y.at[1 - y], t_ygot, tsend.at[wide + deep - 1], trecv.at[wide + deep - 1], partner))
    tiny[-1].start()
    for i in range(4):
        last(i)
    over_y(4)
    tiny[-1].wait_recv()
    small_ref[...] = t_y[y] + t_ygot[...]
    over_y(5)
    last(4)
    last(5)
    puts[0].wait()
    rows_copy[1].wait_recv()
    for copy in list(first.values()) + [c for group in list(second.values()) + list(third.values()) for c in group] + list(fourth.values()) + tiny + rows_copy:
        copy.wait_send()


def last_half(tokens, cotan, bias, gb, gains, kept, sums, batch):
    deep, wide = grid_of(batch)
    own_rows, width = tokens.shape
    rows = 2 * own_rows
    hidden = gb.shape[1]
    cols = hidden // 4
    block = hidden // 2
    shard = width // (2 * batch)
    slots = own_rows // PATCHES
    cuts = [(part, slice(at, at + block)) for part in range(3) for at in (0, block)]
    vm = pl.BlockSpec(memory_space=pltpu.VMEM)
    hbm = pl.BlockSpec(memory_space=pl.ANY)
    buf = lambda *shape: pltpu.VMEM(shape, BF)
    tile = lambda *lead: pltpu.VMEM(lead + TINY, F32)
    scratch = [buf(*k.shape) for k in kept]
    scratch += [buf(wide, deep, 2 * shard, hidden)] * 2
    scratch += [buf(deep, wide, 2, 2 * shard, hidden), buf(deep, wide, 2 * shard, hidden), buf(wide - 1, deep, 2 * shard, hidden)]
    scratch += [buf(deep, 2 * shard, hidden)] * 3 + [buf(deep - 1, 2 * shard, hidden)] * 3 + [buf(shard, hidden)] * 6
    scratch += [buf(rows, 3 * cols), buf(rows, cols), buf(slots * SLOT, cols)]
    scratch += [tile(deep, wide, 2, 2), tile(deep, wide, 2), tile(deep, wide, 2), tile(wide, deep, 2), tile(deep, 2), tile(deep, 2), tile(2), tile()]
    scratch += [pltpu.SemaphoreType.DMA((len(cuts), deep + wide))] * 2 + [pltpu.SemaphoreType.DMA((deep + wide + 2,))] * 2 + [pltpu.SemaphoreType.DMA((len(kept),)), pltpu.SemaphoreType.DMA((2 * wide,)), pltpu.SemaphoreType.DMA]
    full = lambda *shape: jax.ShapeDtypeStruct(shape, F32)
    low = jax.ShapeDtypeStruct((own_rows, width), BF)
    return pl.pallas_call(
        functools.partial(last_kernel, deep=deep, wide=wide, cuts=cuts),
        in_specs=[vm] * 5 + [hbm] * (len(kept) + 2 * wide),
        out_specs=[hbm] * 2 + [vm] * 6,
        out_shape=[low] * 3 + [full(3, shard, 2 * cols), full(shard, 2 * cols), full(shard, 2 * hidden), full(shard, 2 * hidden), full(*TINY)],
        scratch_shapes=scratch,
        compiler_params=pltpu.CompilerParams(collective_id=1, has_side_effects=True, vmem_limit_bytes=VMEM_CAP),
        name="head_gradients_and_scatter",
    )(tokens, cotan, bias, gb, gains, *kept, *sums)


def result_kernel(tokens, cotan, gain, dn_own, dn_got, block_in, qkv_in, wo_in, up_in, down_in, small, block, grad, qkv, wo, up, down, up_b, down_b, norm_g, query_g, key_g):
    vhat, scale = norm_stats(tokens[...].astype(F32))
    scaled = (dn_own[...].astype(F32) + dn_got[...].astype(F32)) * gain[...]
    d_tokens = (scaled - jnp.mean(scaled, axis=-1, keepdims=True) - vhat * jnp.mean(scaled * vhat, axis=-1, keepdims=True)) * scale
    grad[...] = (cotan[...].astype(F32) + d_tokens).astype(BF)
    block[...] = block_in[...]

    @pl.when(pl.program_id(0) == 0)
    def _():
        qkv[...] = qkv_in[...]
        wo[...] = wo_in[...]
        up[...] = up_in[...]
        down[...] = down_in[...]
        norm_g[...] = small[0:1, : norm_g.shape[1]]
        down_b[...] = small[1:2, : down_b.shape[1]]
        up_b[...] = small[2:3, : up_b.shape[1]]
        query_g[...] = small[3:4, :HD]
        key_g[...] = small[3:4, HD : 2 * HD]


def results(tokens, cotan, gain, dn_own, dn_got, block_in, sums, small, per):
    rows, width = tokens.shape
    chunk = rows // 2
    shard = sums[1].shape[0]
    blk = pl.BlockSpec((chunk, width), lambda j: (j, 0))
    whole = lambda shape: pl.BlockSpec(shape, lambda j: (0,) * len(shape))
    vectors = [(1, per), (1, shard), (1, shard), (1, HD), (1, HD)]
    return pl.pallas_call(
        result_kernel,
        grid=(rows // chunk,),
        in_specs=[blk, blk, whole(gain.shape), blk, blk, blk] + [whole(s.shape) for s in sums] + [whole(small.shape)],
        out_specs=[blk, blk] + [whole(s.shape) for s in sums] + [whole(v) for v in vectors],
        out_shape=[jax.ShapeDtypeStruct((rows, width), BF)] * 2 + [jax.ShapeDtypeStruct(s.shape, F32) for s in sums] + [jax.ShapeDtypeStruct(v, F32) for v in vectors],
        compiler_params=pltpu.CompilerParams(vmem_limit_bytes=VMEM_CAP),
        name="results",
    )(tokens, cotan, gain, dn_own, dn_got, block_in, *sums, small)


def local(tokens, cotangent, image_tokens, w_qkv, w_out, w_up, bias_up, w_down, bias_down, norm_gain, query_gain, key_gain):
    batch = lax.axis_size("batch")
    deep, wide = grid_of(batch)
    row = lambda v: v.reshape(1, -1)
    weights = (w_qkv, w_out.T, w_up, w_down.T)
    vectors = (row(norm_gain), row(bias_down), row(bias_up), row(query_gain), row(key_gain))
    made = first_half(tokens, cotangent, weights, vectors, batch)
    x_par, dy_par, normed, q, k, v, d_o, qraw, kraw, head_w, out_own, out_other, dn = made[:13]
    up_sums, down_sums = made[13 : 13 + wide], made[13 + wide : 13 + 2 * wide]
    gb, gain, bias, gains = made[13 + 2 * wide :]
    at = lambda z, x, c: (z * wide + x) * 2 + c

    def over_x(terms):
        return [terms[0]] + [lax.ppermute(terms[s], "batch", [(at(z, x, c), at(z, (x + s) % wide, c)) for z in range(deep) for x in range(wide) for c in range(2)]) for s in range(1, wide)]

    up_sums = over_x(up_sums)
    out_got = lax.ppermute(out_other, "branch", [(0, 1), (1, 0)])
    down_sums = over_x(down_sums)
    o, dq, dk, dv = attention(image_tokens[0], q, k, v, d_o)
    kept = [x_par, dy_par, normed, o, dq, dk, dv, qraw, kraw, head_w, out_own, out_got, dn]
    dn_own, dn_got, block_in, g_qkv, g_out, g_up, g_down, small = last_half(tokens, cotangent, bias, gb, gains, kept, up_sums + down_sums, batch)
    block_out, grad_tokens, g_qkv, g_out, g_up, g_down, g_up_b, g_down_b, g_norm, g_query, g_key = results(tokens, cotangent, gain, dn_own, dn_got, block_in, [g_qkv, g_out, g_up, g_down], small, bias_up.shape[0])
    flat = lambda v: v.reshape(-1)
    return (block_out, grad_tokens, g_qkv, g_out.T, g_up, flat(g_up_b), g_down.T, flat(g_down_b), flat(g_norm), flat(g_query), flat(g_key))


def solution(mesh):
    both = ("batch", "branch")
    in_specs = (P(both, None), P(both, None), P("batch", None), P(None, both, None), P(None, both), P(both, None), P(both), P(None, both), P(both), P(both), P(), P())
    out_specs = (P(both, None), P(both, None), P(None, both, None), P(None, both), P(both, None), P(both), P(None, both), P(both), P(both), P(), P())
    return jax.shard_map(local, mesh=mesh, in_specs=in_specs, out_specs=out_specs, check_vma=False)
```
